32 devices in a mesh: dp: 2 (over core), row: 4 (over y, x), col: 4 (over z).
Axes of the slice: x: 2, y: 2, z: 4, core: 2. Of those that a mesh axis runs over, the one named last changes fastest.
Arguments:
- tokens: bfloat16 [8192, 1024], P(('dp', 'row'), 'col'), may hold values from -6 to 6
- segment_ids: int32 [16, 512], P(('dp', 'col')), may hold values from 0 to 7, never falling along the last dimension, each value on 1 to 256 neighbouring positions
- gain_attn: float32 [1024], P('col'), may hold values from 0.5 to 1.5
- gain_ffn: float32 [1024], P('col'), may hold values from 0.5 to 1.5
- w_qkv: bfloat16 [1024, 3, 1024], P('col', None, 'row'), may hold values from -0.1875 to 0.1875
- w_out: bfloat16 [1024, 1024], P('row', 'col'), may hold values from -1 to 1
- w_gate_up: bfloat16 [1024, 2, 2816], P('col', None, 'row'), may hold values from -0.1875 to 0.1875
- w_down: bfloat16 [2816, 1024], P('row', 'col'), may hold values from -0.109375 to 0.109375
- grad_out: bfloat16 [8192, 1024], P(('dp', 'row'), 'col'), may hold values from -6 to 6
Outputs:
- output: bfloat16 [8192, 1024], P(('dp', 'row'), 'col')
- grad_tokens: float32 [8192, 1024], P(('dp', 'row'), 'col')
- grad_gain_attn: float32 [1024], P('col')
- grad_gain_ffn: float32 [1024], P('col')
- grad_w_qkv: float32 [1024, 3, 1024], P('col', None, 'row')
- grad_w_out: float32 [1024, 1024], P('row', 'col')
- grad_w_gate_up: float32 [1024, 2, 2816], P('col', None, 'row')
- grad_w_down: float32 [2816, 1024], P('row', 'col')
The draws below stay inside these ranges and needn't reach their ends.
Inputs may be any that keep to these rules, and one draw needn't show every extreme that they name: `segment_ids`: in each sequence the ids never fall along its 512 positions; each of the 8 ids covers 1 to 256 consecutive positions.
All inputs are finite; a program needn't handle non-finite values.
Results may differ from the reference program's by a relative error of at most 0.013.
The reference program's roundings to bfloat16 on the way count: a program that leaves them out, or rounds other values in their place, can miss the bound.
Values may be sent and summed in bfloat16 or wider, within the bound.
No kernel may reach another device: no remote copies, remote signals or barrier semaphores. Data moves between devices by JAX's collectives and lax.ppermute only.
A program may use at most 256 MiB of HBM per device.

```python
import math
import jax
import jax.numpy as jnp
import numpy as np
from jax import lax

D = 1024
HEADS = 16
HEAD_DIM = 64
FF = 2816
SEQ = 512
SEQS = 16
TOKENS = 8192
SEGS = 8
MOST_DOC = 256


def level_of(stream_key, extent, shards, smallest, top_value):
    loudness = 1.0
    for axis_at, shards_of in shards:
        heights = jax.random.uniform(jax.random.fold_in(jax.random.fold_in(stream_key, 6), axis_at), (shards_of,), jnp.float32, smallest / len(shards), top_value / len(shards))
        loudness = loudness * jnp.repeat(jnp.exp(heights), extent[axis_at] // shards_of).reshape((-1,) + (1,) * (len(extent) - 1 - axis_at))
    return loudness


def length_profile(count, total, bound, skew):
    portions = [(1 << 20) // math.isqrt(grade ** skew) + 1 for grade in range(2, count + 1)]
    surplus, counts = total - bound - (count - 1), [1] * (count - 1)
    while surplus > 0:
        free = [i for i in range(count - 1) if counts[i] < bound]
        whole, remaining = sum([portions[i] for i in free]), surplus
        for i in free:
            extra = min(bound - counts[i], max(1, remaining * portions[i] // whole), surplus)
            counts[i] = counts[i] + extra
            surplus = surplus - extra
    return np.array([bound] + counts)


def ragged(stream_key, number_of, total, limit, slope):
    if number_of == 2:
        one = jax.random.randint(stream_key, (), max(1, total - limit), min(limit, total - 1) + 1)
        return jnp.stack([one, total - one])
    sizes = jnp.asarray(length_profile(number_of, total, limit, slope), jnp.int32)
    twos = (number_of - 1) // 2
    donor, sink = sizes[1:1 + 2 * twos:2], sizes[2:2 + 2 * twos:2]
    margin = jnp.minimum(donor - 1, limit - sink)
    shifted = jax.random.randint(jax.random.fold_in(stream_key, 1), (twos,), 0, 1 << 20) % (margin + 1)
    sizes = sizes.at[1:1 + 2 * twos:2].set(donor - shifted).at[2:2 + 2 * twos:2].set(sink + shifted)
    return sizes[jax.random.permutation(jax.random.fold_in(stream_key, 2), number_of)]


def normal_values(own_key, dims, spread, limit, split=(), kind=jnp.bfloat16):
    gain = level_of(own_key, dims, split, -0.22, 0.18) if split else 1.0
    values = jax.random.normal(own_key, dims, jnp.float32) * spread * gain
    return jnp.minimum(jnp.maximum(values, -limit), limit).astype(kind)


def setup_inputs(seed: int = 0) -> dict:
    key_list = jax.random.split(jax.random.key(seed), 10)
    return {
        "tokens": normal_values(key_list[0], (TOKENS, D), 1.0, 6.0, ((0, 8), (1, 4))),
        "segment_ids": jax.vmap(lambda own: jnp.searchsorted(jnp.cumsum(ragged(own, SEGS, SEQ, MOST_DOC, 2)), jnp.arange(SEQ), side="right"))(jax.random.split(key_list[1], SEQS)).reshape((SEQS, SEQ)).astype(jnp.int32),
        "gain_attn": jnp.clip(1.0 + 0.1 * jax.random.normal(key_list[2], (D,), jnp.float32), 0.5, 1.5),
        "gain_ffn": jnp.clip(1.0 + 0.1 * jax.random.normal(key_list[3], (D,), jnp.float32), 0.5, 1.5),
        "w_qkv": normal_values(key_list[4], (D, 3, D), D ** -0.5, 0.1875, ((0, 4), (2, 4))),
        "w_out": normal_values(key_list[5], (D, D), (D // 32) ** -0.5, 1.0, ((0, 4), (1, 4))),
        "w_gate_up": normal_values(key_list[6], (D, 2, FF), D ** -0.5, 0.1875, ((0, 4), (2, 4))),
        "w_down": normal_values(key_list[7], (FF, D), FF ** -0.5, 0.109375, ((0, 4), (1, 4))),
        "grad_out": normal_values(key_list[8], (TOKENS, D), 1.0, 6.0, ((0, 8), (1, 4))),
    }


@jax.custom_vjp
def low(v):
    return lax.optimization_barrier(v.astype(jnp.bfloat16)).astype(jnp.float32)

@jax.custom_vjp
def low_back(v):
    return v

def low_keep(v):
    return (low(v), None)

def low_pass(kept, grad):
    return (grad,)

def back_keep(v):
    return (v, None)

def back_low(kept, grad):
    return (low(grad),)
low.defvjp(low_keep, low_pass)
low_back.defvjp(back_keep, back_low)
EPS = 1e-06
MASKED = -1e+30
HIGH = lax.Precision.HIGHEST

def rms_norm(values, gain_vec):
    rescale = lax.rsqrt(lax.optimization_barrier(jnp.mean(values * values, axis=-1, keepdims=True)) + EPS)
    return values * rescale * gain_vec

def attend_block(item, keys_all, values_all, key_segment):
    queries, query_segment, query_place = item
    scores = jnp.einsum('qhd,khd->hqk', queries, keys_all, precision=HIGH) * HEAD_DIM ** (-0.5)
    scores = low_back(scores)
    key_place = jnp.arange(keys_all.shape[0], dtype=jnp.int32)
    allowed = (query_segment[:, None] == key_segment[None, :]) & (key_place[None, :] <= query_place[:, None])
    scores = jnp.where(allowed[None], scores, MASKED)
    prob_rows = jax.nn.softmax(scores, axis=-1)
    return jnp.einsum('hqk,khd->qhd', low(prob_rows), values_all, precision=HIGH)

def attend_sequence(packed, segment):
    length = packed.shape[0]
    block_rows = min(512, length)
    blocks = length // block_rows
    queries = packed[:, 0].reshape(blocks, block_rows, HEADS, HEAD_DIM)
    keys_all = packed[:, 1]
    values_all = packed[:, 2]
    place = jnp.arange(length, dtype=jnp.int32).reshape(blocks, block_rows)

    def inner(item):
        return attend_block(item, keys_all, values_all, segment)
    mixed = lax.map(jax.checkpoint(inner), (queries, segment.reshape(blocks, block_rows), place))
    return mixed.reshape(length, D)

def layer_block(values, gain_attn, gain_ffn, w_qkv, w_out, w_gate_up, w_down, segment):
    length = values.shape[0]
    normed = low(rms_norm(values, gain_attn))
    packed = jnp.dot(normed, w_qkv.reshape(D, 3 * D), precision=HIGH)
    packed = low_back(low(packed)).reshape(length, 3, HEADS, HEAD_DIM)
    mixed = low_back(low(attend_sequence(packed, segment)))
    hidden = values + low_back(jnp.dot(mixed, w_out, precision=HIGH))
    normed_two = low(rms_norm(hidden, gain_ffn))
    gate_up = jnp.dot(normed_two, w_gate_up.reshape(D, 2 * FF), precision=HIGH)
    gate_up = low_back(low(gate_up))
    active = low_back(low(jax.nn.silu(gate_up[:, :FF]) * gate_up[:, FF:]))
    return hidden + low_back(jnp.dot(active, w_down, precision=HIGH))

def reference(tokens, segment_ids, gain_attn, gain_ffn, w_qkv, w_out, w_gate_up, w_down, grad_out):
    weights = tuple((a.astype(jnp.float32) for a in (gain_attn, gain_ffn, w_qkv, w_out, w_gate_up, w_down)))
    inputs = tokens.astype(jnp.float32).reshape(SEQS, SEQ, D)
    cotangents = grad_out.astype(jnp.float32).reshape(SEQS, SEQ, D)

    def step(totals, item):
        values, cotangent, segment = item

        def apply_layer(vals, *params):
            return layer_block(vals, *params, segment)
        result, pull = jax.vjp(apply_layer, values, *weights)
        grads = pull(cotangent)
        totals = tuple((a + g for a, g in zip(totals, grads[1:])))
        return (totals, (result, grads[0]))
    start_totals = tuple((jnp.zeros_like(w) for w in weights))
    totals, (results, input_grads) = lax.scan(step, start_totals, (inputs, cotangents, segment_ids))
    return (results.reshape(TOKENS, D).astype(jnp.bfloat16), input_grads.reshape(TOKENS, D), totals[0], totals[1], totals[2], totals[3], totals[4], totals[5])
```

```python
import jax
import jax.numpy as jnp
from jax import lax
from jax.sharding import PartitionSpec as P

D = 1024
HEAD_DIM = 64


EPS = 1e-06
MASKED = -1e30


def row_norm(values, gain_vec):
    squares = lax.psum(jnp.sum(values * values, axis=1), "col")
    rescale = lax.rsqrt(squares / D + EPS)
    unit_rows = values * rescale[:, None]
    return (unit_rows, rescale, (unit_rows * gain_vec[None, :]).astype(jnp.bfloat16))


def norm_backward(grad_normed, unit_rows, rescale, gain_vec):
    weighted = grad_normed * gain_vec[None, :]
    inner_sum = lax.psum(jnp.sum(weighted * unit_rows, axis=1), "col")
    grad_in = rescale[:, None] * (weighted - unit_rows * (inner_sum / D)[:, None])
    grad_gain = jnp.sum(grad_normed * unit_rows, axis=0)
    return (grad_in, grad_gain)


def project_up(normed, weight_block):
    gathered = lax.all_gather(normed, "row", axis=0, tiled=True)

    def term(begin_at, row_count):
        return jnp.dot(gathered, weight_block, preferred_element_type=jnp.float32)

    result = lax.psum_scatter(
        term(jnp.int32(0), gathered.shape[0] // lax.axis_size("col") * lax.axis_size("col")),
        "col",
        scatter_dimension=0,
        tiled=True,
    )
    return (gathered, result.astype(jnp.bfloat16))


def project_down(values, weight_block):
    gathered = lax.all_gather(values, "col", axis=0, tiled=True)

    def term(begin_at, row_count):
        return jnp.dot(gathered, weight_block, preferred_element_type=jnp.float32)

    result = lax.psum_scatter(
        term(jnp.int32(0), gathered.shape[0] // lax.axis_size("row") * lax.axis_size("row")),
        "row",
        scatter_dimension=0,
        tiled=True,
    )
    return (gathered, result)


def back_down(grad_rows, weight_block):
    gathered = lax.all_gather(grad_rows, "row", axis=0, tiled=True)

    def term(begin_at, row_count):
        return lax.dot_general(
            gathered, weight_block, (((1,), (1,)), ((), ())), preferred_element_type=jnp.float32
        )

    result = lax.psum_scatter(
        term(jnp.int32(0), gathered.shape[0] // lax.axis_size("col") * lax.axis_size("col")),
        "col",
        scatter_dimension=0,
        tiled=True,
    )
    return (gathered, result.astype(jnp.bfloat16))


def back_up(grad_cols, weight_block):
    gathered = lax.all_gather(grad_cols, "col", axis=0, tiled=True)

    def term(begin_at, row_count):
        return lax.dot_general(
            gathered, weight_block, (((1,), (1,)), ((), ())), preferred_element_type=jnp.float32
        )

    result = lax.psum_scatter(
        term(jnp.int32(0), gathered.shape[0] // lax.axis_size("row") * lax.axis_size("row")),
        "row",
        scatter_dimension=0,
        tiled=True,
    )
    return (gathered, result)


def weight_grad(left_rows, right_rows):
    return lax.dot_general(
        left_rows, right_rows, (((0,), (0,)), ((), ())), preferred_element_type=jnp.float32
    )


def block_scores(queries, keys_all, query_segment, key_segment, query_place):
    raw = jnp.einsum(
        "qhd,khd->hqk", queries, keys_all, preferred_element_type=jnp.float32
    ) * HEAD_DIM ** (-0.5)
    key_place = lax.broadcasted_iota(jnp.int32, (1, keys_all.shape[0]), 1)
    allowed = (query_segment[:, None] == key_segment[None, :]) & (key_place <= query_place[:, None])
    return jnp.where(allowed[None], raw, MASKED)


def split_blocks(queries, segment):
    length = queries.shape[0]
    block_rows = min(512, length)
    blocks = length // block_rows
    place = jnp.arange(length, dtype=jnp.int32).reshape(blocks, block_rows)
    return (
        queries.reshape(blocks, block_rows, queries.shape[1], queries.shape[2]),
        segment.reshape(blocks, block_rows),
        place,
    )


def attend_forward(queries, keys_all, values_all, segment):
    query_blocks, segment_blocks, place_blocks = split_blocks(queries, segment)

    def one_block(item):
        query_rows, query_segment, query_place = item
        scores = block_scores(query_rows, keys_all, query_segment, segment, query_place)
        row_max = jnp.max(scores, axis=-1, keepdims=True)
        expo = jnp.exp(scores - row_max)
        row_total = jnp.sum(expo, axis=-1, keepdims=True)
        prob_rows = (expo / row_total).astype(jnp.bfloat16)
        mixed = jnp.einsum(
            "hqk,khd->qhd", prob_rows, values_all, preferred_element_type=jnp.float32
        )
        return (mixed, row_max[..., 0] + jnp.log(row_total[..., 0]))

    mixed, log_total = lax.map(one_block, (query_blocks, segment_blocks, place_blocks))
    return (mixed.reshape(queries.shape[0], -1).astype(jnp.bfloat16), log_total)


def attend_backward(queries, keys_all, values_all, segment, log_total, grad_mix):
    query_blocks, segment_blocks, place_blocks = split_blocks(queries, segment)
    grad_blocks = grad_mix.reshape(query_blocks.shape)
    factor = HEAD_DIM ** (-0.5)

    def one_block(carry, item):
        key_acc, value_acc = carry
        query_rows, query_segment, query_place, log_rows, grad_rows = item
        scores = block_scores(query_rows, keys_all, query_segment, segment, query_place)
        prob_rows = jnp.exp(scores - log_rows[..., None])
        value_acc = value_acc + jnp.einsum(
            "hqk,qhd->khd",
            prob_rows.astype(jnp.bfloat16),
            grad_rows,
            preferred_element_type=jnp.float32,
        )
        grad_prob = jnp.einsum(
            "qhd,khd->hqk", grad_rows, values_all, preferred_element_type=jnp.float32
        )
        grad_scores = (
            prob_rows * (grad_prob - jnp.sum(prob_rows * grad_prob, axis=-1, keepdims=True))
        ).astype(jnp.bfloat16)
        grad_query = (
            jnp.einsum("hqk,khd->qhd", grad_scores, keys_all, preferred_element_type=jnp.float32)
            * factor
        )
        key_acc = (
            key_acc
            + jnp.einsum(
                "hqk,qhd->khd", grad_scores, query_rows, preferred_element_type=jnp.float32
            )
            * factor
        )
        return ((key_acc, value_acc), grad_query)

    zeros_like_keys = jnp.zeros(keys_all.shape, jnp.float32)
    (grad_keys, grad_values), grad_queries = lax.scan(
        one_block,
        (zeros_like_keys, zeros_like_keys),
        (query_blocks, segment_blocks, place_blocks, log_total, grad_blocks),
    )
    grad_queries = grad_queries.reshape(queries.shape)
    return jnp.stack([grad_queries, grad_keys, grad_values], axis=1).astype(jnp.bfloat16)


def local(tokens, segment_ids, gain_attn, gain_ffn, w_qkv, w_out, w_gate_up, w_down, grad_out):
    values = tokens.astype(jnp.float32)
    head_cols = w_qkv.shape[2]
    heads_here = head_cols // HEAD_DIM
    hidden_here = w_gate_up.shape[2]
    qkv_block = w_qkv.reshape(w_qkv.shape[0], 3 * head_cols)
    gate_up_block = w_gate_up.reshape(w_gate_up.shape[0], 2 * hidden_here)
    seq_count, seq_length = segment_ids.shape
    unit_one, rescale_one, normed_one = row_norm(values, gain_attn)
    gathered_one, packed = project_up(normed_one, qkv_block)
    packed = packed.reshape(-1, 3, heads_here, HEAD_DIM)
    mix_parts, log_parts = ([], [])
    for index in range(seq_count):
        rows_here = packed[index * seq_length : (index + 1) * seq_length]
        mixed, log_total = attend_forward(
            rows_here[:, 0], rows_here[:, 1], rows_here[:, 2], segment_ids[index]
        )
        mix_parts.append(mixed)
        log_parts.append(log_total)
    attn_mix = jnp.concatenate(mix_parts, axis=0)
    gathered_mix, attn_branch = project_down(attn_mix, w_out)
    hidden = values + attn_branch
    unit_two, rescale_two, normed_two = row_norm(hidden, gain_ffn)
    gathered_two, gate_up = project_up(normed_two, gate_up_block)
    gate_vals = gate_up[:, :hidden_here].astype(jnp.float32)
    up_vals = gate_up[:, hidden_here:].astype(jnp.float32)
    sigmoid_gate = jax.nn.sigmoid(gate_vals)
    silu_gate = gate_vals * sigmoid_gate
    active = (silu_gate * up_vals).astype(jnp.bfloat16)
    gathered_act, ffn_branch = project_down(active, w_down)
    output = (hidden + ffn_branch).astype(jnp.bfloat16)
    grad_rows_out, grad_active = back_down(grad_out, w_down)
    grad_down = weight_grad(gathered_act, grad_rows_out)
    grad_act_f = grad_active.astype(jnp.float32)
    grad_gate = grad_act_f * up_vals * sigmoid_gate * (1.0 + gate_vals * (1.0 - sigmoid_gate))
    grad_up = grad_act_f * silu_gate
    grad_gate_up_rows = jnp.concatenate([grad_gate, grad_up], axis=1).astype(jnp.bfloat16)
    grad_cols_two, grad_normed_two = back_up(grad_gate_up_rows, gate_up_block)
    grad_gate_up = weight_grad(gathered_two, grad_cols_two).reshape(w_gate_up.shape)
    grad_hidden_norm, grad_gain_two = norm_backward(
        grad_normed_two, unit_two, rescale_two, gain_ffn
    )
    grad_hidden = grad_out.astype(jnp.float32) + grad_hidden_norm
    grad_rows_hidden, grad_mix = back_down(grad_hidden.astype(jnp.bfloat16), w_out)
    grad_out_weight = weight_grad(gathered_mix, grad_rows_hidden)
    grad_mix = grad_mix.reshape(-1, heads_here, HEAD_DIM)
    grad_parts = []
    for index in range(seq_count):
        rows_here = packed[index * seq_length : (index + 1) * seq_length]
        grad_parts.append(
            attend_backward(
                rows_here[:, 0],
                rows_here[:, 1],
                rows_here[:, 2],
                segment_ids[index],
                log_parts[index],
                grad_mix[index * seq_length : (index + 1) * seq_length],
            )
        )
    grad_packed = jnp.concatenate(grad_parts, axis=0).reshape(-1, 3 * head_cols)
    grad_cols_one, grad_normed_one = back_up(grad_packed, qkv_block)
    grad_qkv = weight_grad(gathered_one, grad_cols_one).reshape(w_qkv.shape)
    grad_input_norm, grad_gain_one = norm_backward(
        grad_normed_one, unit_one, rescale_one, gain_attn
    )
    grad_tokens = grad_hidden + grad_input_norm
    summed = lax.psum((grad_qkv, grad_out_weight, grad_gate_up, grad_down), "dp")
    gains = lax.psum((grad_gain_one, grad_gain_two), ("dp", "row"))
    return (output, grad_tokens, gains[0], gains[1], summed[0], summed[1], summed[2], summed[3])


def swap(values):
    return lax.ppermute(values, "dp", [(0, 1), (1, 0)])


def by_core(core, mine, other, axis=0):
    first = jnp.where(core == 0, mine, other)
    second = jnp.where(core == 0, other, mine)
    return jnp.concatenate([first, second], axis=axis)


def pick(values, core, axis=0):
    half = values.shape[axis] // 2
    return lax.dynamic_slice_in_dim(values, core * half, half, axis)


def to_sequence(values, core, seq_length):
    seqs = values.shape[0] // seq_length
    half = seq_length // 2
    parts = values.reshape(seqs, seq_length, -1)
    mine = pick(parts, core, 1)
    other = swap(pick(parts, 1 - core, 1))
    chunks = by_core(core, mine, other)
    got = lax.all_to_all(chunks, "col", 0, 0, tiled=True)
    rows = got.transpose(1, 0, 2).reshape(half, -1)
    return by_core(core, rows, swap(rows))


def from_sequence(rows, core, seq_length):
    cols = lax.axis_size("col")
    half = rows.shape[0]
    chunks = rows.reshape(half, cols, -1).transpose(1, 0, 2)
    got = lax.all_to_all(chunks, "col", 0, 0, tiled=True)
    mine = pick(got, core)
    other = swap(pick(got, 1 - core))
    return by_core(core, mine, other, 1).reshape(cols // 2 * seq_length, -1)


def times(left, right):
    return jnp.dot(left, right, preferred_element_type=jnp.float32)


def times_t(left, right):
    return lax.dot_general(
        left, right, (((1,), (1,)), ((), ())), preferred_element_type=jnp.float32
    )


def norm_rows(values):
    rescale = lax.rsqrt(jnp.mean(values * values, axis=1) + EPS)[:, None]
    return (values * rescale, rescale)


def norm_rows_back(grad_normed, unit_rows, rescale, gain_vec):
    weighted = grad_normed * gain_vec[None, :]
    inner = jnp.sum(weighted * unit_rows, axis=1, keepdims=True) / D
    return (rescale * (weighted - unit_rows * inner), jnp.sum(grad_normed * unit_rows, axis=0))


def spread_weights(block, kinds):
    rows, cols = (lax.axis_size("row"), lax.axis_size("col"))
    gathered = lax.all_gather(block, ("row", "col"), axis=0, tiled=True)
    gathered = gathered.reshape(rows, cols, kinds, -1, block.shape[1])
    return gathered.transpose(2, 0, 3, 1, 4).reshape(-1, cols * block.shape[1])


def reduce_weights(parts):
    rows, cols = (lax.axis_size("row"), lax.axis_size("col"))
    pieces = []
    for grad, kinds in parts:
        block = grad.astype(jnp.bfloat16).reshape(kinds, rows, -1, cols, grad.shape[1] // cols)
        pieces.append(block.transpose(1, 3, 0, 2, 4).reshape(rows * cols, -1, block.shape[4]))
    stacked = jnp.concatenate(pieces, axis=1)
    stacked = lax.psum_scatter(stacked, "row", scatter_dimension=0, tiled=True)
    return lax.psum_scatter(stacked, "col", scatter_dimension=0, tiled=True)[0]


def chip_local(tokens, segment_ids, gain_attn, gain_ffn, w_qkv, w_out, w_gate_up, w_down, grad_out):
    core = lax.axis_index("dp")
    rows, cols = (lax.axis_size("row"), lax.axis_size("col"))
    row, col = (lax.axis_index("row"), lax.axis_index("col"))
    length = segment_ids.shape[1]
    seqs = tokens.shape[0] // length
    features = w_qkv.shape[0]
    head_cols = w_qkv.shape[2] // 2
    hidden = w_gate_up.shape[2] // 2
    heads = rows * head_cols // HEAD_DIM
    factor = HEAD_DIM ** (-0.5)

    qkv_t = pick(w_qkv, core, 2).transpose(1, 2, 0).reshape(3 * head_cols, features)
    gate_up_t = pick(w_gate_up, core, 2).transpose(1, 2, 0).reshape(2 * hidden, features)
    big_qkv = spread_weights(qkv_t, 3)
    big_out = spread_weights(pick(w_out, core), 1)
    big_gate_up = spread_weights(gate_up_t, 2)
    big_down = spread_weights(pick(w_down, core), 1)
    gains = lax.all_gather(jnp.stack([gain_attn, gain_ffn], axis=0), "col", axis=1, tiled=True)

    every_segment = lax.all_gather(segment_ids, ("dp", "col"), axis=0, tiled=True)
    place = col // seqs * (rows * seqs) + row * seqs + col % seqs
    segment = lax.dynamic_index_in_dim(every_segment, place, 0, keepdims=False)

    values = to_sequence(tokens, core, length).astype(jnp.float32)
    cotangent = to_sequence(grad_out, core, length)

    unit_one, rescale_one = norm_rows(values)
    normed_one = (unit_one * gains[0][None, :]).astype(jnp.bfloat16)
    packed = times_t(normed_one, big_qkv).astype(jnp.bfloat16).reshape(length, 3, heads, HEAD_DIM)
    queries, keys, vals = (packed[:, 0], packed[:, 1], packed[:, 2])
    scores = jnp.einsum("qhd,khd->hqk", queries, keys, preferred_element_type=jnp.float32) * factor
    spot = jnp.arange(length, dtype=jnp.int32)
    live = (segment[:, None] == segment[None, :]) & (spot[None, :] <= spot[:, None])
    scores = jnp.where(live[None], scores, MASKED)
    expo = jnp.exp(scores - jnp.max(scores, axis=-1, keepdims=True))
    prob = expo / jnp.sum(expo, axis=-1, keepdims=True)
    prob_low = prob.astype(jnp.bfloat16)
    mixed = jnp.einsum("hqk,khd->qhd", prob_low, vals, preferred_element_type=jnp.float32)
    mixed = mixed.reshape(length, -1).astype(jnp.bfloat16)
    branch = times(mixed, big_out)
    hidden_rows = values + (branch + swap(branch))
    unit_two, rescale_two = norm_rows(hidden_rows)
    normed_two = (unit_two * gains[1][None, :]).astype(jnp.bfloat16)
    gate_up = times_t(normed_two, big_gate_up).astype(jnp.bfloat16)
    half = gate_up.shape[1] // 2
    gate_vals = gate_up[:, :half].astype(jnp.float32)
    up_vals = gate_up[:, half:].astype(jnp.float32)
    sigmoid_gate = jax.nn.sigmoid(gate_vals)
    silu_gate = gate_vals * sigmoid_gate
    active = (silu_gate * up_vals).astype(jnp.bfloat16)
    ffn = times(active, big_down)
    ffn_mine = pick(ffn, core) + swap(pick(ffn, 1 - core))
    output = from_sequence((pick(hidden_rows, core) + ffn_mine).astype(jnp.bfloat16), core, length)

    grad_down = weight_grad(active, cotangent)
    grad_act = times_t(cotangent, big_down).astype(jnp.bfloat16).astype(jnp.float32)
    grad_gate = grad_act * up_vals * sigmoid_gate * (1.0 + gate_vals * (1.0 - sigmoid_gate))
    grad_up = grad_act * silu_gate
    grad_gu = jnp.concatenate([grad_gate, grad_up], axis=1).astype(jnp.bfloat16)
    grad_gate_up = weight_grad(grad_gu, normed_two)
    grad_two = times(grad_gu, big_gate_up)
    grad_two = grad_two + swap(grad_two)
    mine_ffn = reduce_weights([(grad_gate_up, 2), (grad_down, 1)])
    back_two, _ = norm_rows_back(grad_two, unit_two, rescale_two, gains[1])
    gain_two = jnp.sum(pick(grad_two * unit_two, core), axis=0)
    grad_hidden = cotangent.astype(jnp.float32) + back_two
    grad_branch = grad_hidden.astype(jnp.bfloat16)
    grad_w_out = weight_grad(mixed, grad_branch)
    grad_mix = times_t(grad_branch, big_out).astype(jnp.bfloat16).reshape(length, heads, HEAD_DIM)
    grad_vals = jnp.einsum("hqk,qhd->khd", prob_low, grad_mix, preferred_element_type=jnp.float32)
    grad_prob = jnp.einsum("qhd,khd->hqk", grad_mix, vals, preferred_element_type=jnp.float32)
    inner = jnp.sum(prob * grad_prob, axis=-1, keepdims=True)
    grad_scores = (prob * (grad_prob - inner)).astype(jnp.bfloat16)
    grad_queries = factor * jnp.einsum(
        "hqk,khd->qhd", grad_scores, keys, preferred_element_type=jnp.float32
    )
    grad_keys = factor * jnp.einsum(
        "hqk,qhd->khd", grad_scores, queries, preferred_element_type=jnp.float32
    )
    grad_packed = jnp.stack([grad_queries, grad_keys, grad_vals], axis=1)
    grad_packed = grad_packed.astype(jnp.bfloat16).reshape(length, -1)
    grad_qkv = weight_grad(grad_packed, normed_one)
    mine_attn = reduce_weights([(grad_qkv, 3), (grad_w_out, 1)])
    grad_one = times(grad_packed, big_qkv)
    grad_one = pick(grad_one, core) + swap(pick(grad_one, 1 - core))
    back_one, gain_one = norm_rows_back(
        grad_one, pick(unit_one, core), pick(rescale_one, core), gains[0]
    )
    grad_rows = (pick(grad_hidden, core) + back_one).astype(jnp.bfloat16)
    grad_tokens = from_sequence(grad_rows, core, length).astype(jnp.float32)

    gain_sums = lax.psum(jnp.stack([gain_one, gain_two], axis=0), ("dp", "row", "col"))
    gain_sums = lax.dynamic_slice_in_dim(gain_sums, col * features, features, 1)

    gu_rows = 2 * hidden
    out_ffn = swap(mine_ffn)
    out_attn = swap(mine_attn)

    def joined(mine, other, start, stop, kinds):
        left = mine[start:stop].reshape(kinds, -1, features)
        right = other[start:stop].reshape(kinds, -1, features)
        return by_core(core, left, right, 1).astype(jnp.float32)

    full_qkv = joined(mine_attn, out_attn, 0, 3 * head_cols, 3).transpose(2, 0, 1)
    full_out = joined(mine_attn, out_attn, 3 * head_cols, None, 1)[0]
    full_gate_up = joined(mine_ffn, out_ffn, 0, gu_rows, 2).transpose(2, 0, 1)
    full_down = joined(mine_ffn, out_ffn, gu_rows, None, 1)[0]
    return (
        output,
        grad_tokens,
        gain_sums[0],
        gain_sums[1],
        full_qkv,
        full_out,
        full_gate_up,
        full_down,
    )


def layer(tokens, segment_ids, *rest):
    length = segment_ids.shape[1]
    cols = lax.axis_size("col")
    if lax.axis_size("dp") == 2 and tokens.shape[0] * 2 == cols * length:
        return chip_local(tokens, segment_ids, *rest)
    return local(tokens, segment_ids, *rest)


def solution(mesh):
    in_specs = (
        P(("dp", "row"), "col"),
        P(("dp", "col"), None),
        P("col"),
        P("col"),
        P("col", None, "row"),
        P("row", "col"),
        P("col", None, "row"),
        P("row", "col"),
        P(("dp", "row"), "col"),
    )
    out_specs = (
        P(("dp", "row"), "col"),
        P(("dp", "row"), "col"),
        P("col"),
        P("col"),
        P("col", None, "row"),
        P("row", "col"),
        P("col", None, "row"),
        P("row", "col"),
    )
    return jax.shard_map(layer, mesh=mesh, in_specs=in_specs, out_specs=out_specs, check_vma=False)
```

```python
import jax
import jax.numpy as jnp
from jax import lax
from jax.sharding import PartitionSpec as P

D = 1024
HEAD_DIM = 64


EPS = 1e-06
MASKED = -1e30


def row_norm(values, gain_vec):
    squares = lax.psum(jnp.sum(values * values, axis=1), "col")
    rescale = lax.rsqrt(squares / D + EPS)
    unit_rows = values * rescale[:, None]
    return (unit_rows, rescale, (unit_rows * gain_vec[None, :]).astype(jnp.bfloat16))


def norm_backward(grad_normed, unit_rows, rescale, gain_vec):
    weighted = grad_normed * gain_vec[None, :]
    inner_sum = lax.psum(jnp.sum(weighted * unit_rows, axis=1), "col")
    grad_in = rescale[:, None] * (weighted - unit_rows * (inner_sum / D)[:, None])
    grad_gain = jnp.sum(grad_normed * unit_rows, axis=0)
    return (grad_in, grad_gain)


def project_up(normed, weight_block):
    gathered = lax.all_gather(normed, "row", axis=0, tiled=True)

    def term(begin_at, row_count):
        return jnp.dot(gathered, weight_block, preferred_element_type=jnp.float32)

    result = lax.psum_scatter(
        term(jnp.int32(0), gathered.shape[0] // lax.axis_size("col") * lax.axis_size("col")),
        "col",
        scatter_dimension=0,
        tiled=True,
    )
    return (gathered, result.astype(jnp.bfloat16))


def project_down(values, weight_block):
    gathered = lax.all_gather(values, "col", axis=0, tiled=True)

    def term(begin_at, row_count):
        return jnp.dot(gathered, weight_block, preferred_element_type=jnp.float32)

    result = lax.psum_scatter(
        term(jnp.int32(0), gathered.shape[0] // lax.axis_size("row") * lax.axis_size("row")),
        "row",
        scatter_dimension=0,
        tiled=True,
    )
    return (gathered, result)


def back_down(grad_rows, weight_block):
    gathered = lax.all_gather(grad_rows, "row", axis=0, tiled=True)

    def term(begin_at, row_count):
        return lax.dot_general(
            gathered, weight_block, (((1,), (1,)), ((), ())), preferred_element_type=jnp.float32
        )

    result = lax.psum_scatter(
        term(jnp.int32(0), gathered.shape[0] // lax.axis_size("col") * lax.axis_size("col")),
        "col",
        scatter_dimension=0,
        tiled=True,
    )
    return (gathered, result.astype(jnp.bfloat16))


def back_up(grad_cols, weight_block):
    gathered = lax.all_gather(grad_cols, "col", axis=0, tiled=True)

    def term(begin_at, row_count):
        return lax.dot_general(
            gathered, weight_block, (((1,), (1,)), ((), ())), preferred_element_type=jnp.float32
        )

    result = lax.psum_scatter(
        term(jnp.int32(0), gathered.shape[0] // lax.axis_size("row") * lax.axis_size("row")),
        "row",
        scatter_dimension=0,
        tiled=True,
    )
    return (gathered, result)


def weight_grad(left_rows, right_rows):
    return lax.dot_general(
        left_rows, right_rows, (((0,), (0,)), ((), ())), preferred_element_type=jnp.float32
    )


def block_scores(queries, keys_all, query_segment, key_segment, query_place):
    raw = jnp.einsum(
        "qhd,khd->hqk", queries, keys_all, preferred_element_type=jnp.float32
    ) * HEAD_DIM ** (-0.5)
    key_place = lax.broadcasted_iota(jnp.int32, (1, keys_all.shape[0]), 1)
    allowed = (query_segment[:, None] == key_segment[None, :]) & (key_place <= query_place[:, None])
    return jnp.where(allowed[None], raw, MASKED)


def split_blocks(queries, segment):
    length = queries.shape[0]
    block_rows = min(512, length)
    blocks = length // block_rows
    place = jnp.arange(length, dtype=jnp.int32).reshape(blocks, block_rows)
    return (
        queries.reshape(blocks, block_rows, queries.shape[1], queries.shape[2]),
        segment.reshape(blocks, block_rows),
        place,
    )


def attend_forward(queries, keys_all, values_all, segment):
    query_blocks, segment_blocks, place_blocks = split_blocks(queries, segment)

    def one_block(item):
        query_rows, query_segment, query_place = item
        scores = block_scores(query_rows, keys_all, query_segment, segment, query_place)
        row_max = jnp.max(scores, axis=-1, keepdims=True)
        expo = jnp.exp(scores - row_max)
        row_total = jnp.sum(expo, axis=-1, keepdims=True)
        prob_rows = (expo / row_total).astype(jnp.bfloat16)
        mixed = jnp.einsum(
            "hqk,khd->qhd", prob_rows, values_all, preferred_element_type=jnp.float32
        )
        return (mixed, row_max[..., 0] + jnp.log(row_total[..., 0]))

    mixed, log_total = lax.map(one_block, (query_blocks, segment_blocks, place_blocks))
    return (mixed.reshape(queries.shape[0], -1).astype(jnp.bfloat16), log_total)


def attend_backward(queries, keys_all, values_all, segment, log_total, grad_mix):
    query_blocks, segment_blocks, place_blocks = split_blocks(queries, segment)
    grad_blocks = grad_mix.reshape(query_blocks.shape)
    factor = HEAD_DIM ** (-0.5)

    def one_block(carry, item):
        key_acc, value_acc = carry
        query_rows, query_segment, query_place, log_rows, grad_rows = item
        scores = block_scores(query_rows, keys_all, query_segment, segment, query_place)
        prob_rows = jnp.exp(scores - log_rows[..., None])
        value_acc = value_acc + jnp.einsum(
            "hqk,qhd->khd",
            prob_rows.astype(jnp.bfloat16),
            grad_rows,
            preferred_element_type=jnp.float32,
        )
        grad_prob = jnp.einsum(
            "qhd,khd->hqk", grad_rows, values_all, preferred_element_type=jnp.float32
        )
        grad_scores = (
            prob_rows * (grad_prob - jnp.sum(prob_rows * grad_prob, axis=-1, keepdims=True))
        ).astype(jnp.bfloat16)
        grad_query = (
            jnp.einsum("hqk,khd->qhd", grad_scores, keys_all, preferred_element_type=jnp.float32)
            * factor
        )
        key_acc = (
            key_acc
            + jnp.einsum(
                "hqk,qhd->khd", grad_scores, query_rows, preferred_element_type=jnp.float32
            )
            * factor
        )
        return ((key_acc, value_acc), grad_query)

    zeros_like_keys = jnp.zeros(keys_all.shape, jnp.float32)
    (grad_keys, grad_values), grad_queries = lax.scan(
        one_block,
        (zeros_like_keys, zeros_like_keys),
        (query_blocks, segment_blocks, place_blocks, log_total, grad_blocks),
    )
    grad_queries = grad_queries.reshape(queries.shape)
    return jnp.stack([grad_queries, grad_keys, grad_values], axis=1).astype(jnp.bfloat16)


def local(tokens, segment_ids, gain_attn, gain_ffn, w_qkv, w_out, w_gate_up, w_down, grad_out):
    values = tokens.astype(jnp.float32)
    head_cols = w_qkv.shape[2]
    heads_here = head_cols // HEAD_DIM
    hidden_here = w_gate_up.shape[2]
    qkv_block = w_qkv.reshape(w_qkv.shape[0], 3 * head_cols)
    gate_up_block = w_gate_up.reshape(w_gate_up.shape[0], 2 * hidden_here)
    seq_count, seq_length = segment_ids.shape
    unit_one, rescale_one, normed_one = row_norm(values, gain_attn)
    gathered_one, packed = project_up(normed_one, qkv_block)
    packed = packed.reshape(-1, 3, heads_here, HEAD_DIM)
    mix_parts, log_parts = ([], [])
    for index in range(seq_count):
        rows_here = packed[index * seq_length : (index + 1) * seq_length]
        mixed, log_total = attend_forward(
            rows_here[:, 0], rows_here[:, 1], rows_here[:, 2], segment_ids[index]
        )
        mix_parts.append(mixed)
        log_parts.append(log_total)
    attn_mix = jnp.concatenate(mix_parts, axis=0)
    gathered_mix, attn_branch = project_down(attn_mix, w_out)
    hidden = values + attn_branch
    unit_two, rescale_two, normed_two = row_norm(hidden, gain_ffn)
    gathered_two, gate_up = project_up(normed_two, gate_up_block)
    gate_vals = gate_up[:, :hidden_here].astype(jnp.float32)
    up_vals = gate_up[:, hidden_here:].astype(jnp.float32)
    sigmoid_gate = jax.nn.sigmoid(gate_vals)
    silu_gate = gate_vals * sigmoid_gate
    active = (silu_gate * up_vals).astype(jnp.bfloat16)
    gathered_act, ffn_branch = project_down(active, w_down)
    output = (hidden + ffn_branch).astype(jnp.bfloat16)
    grad_rows_out, grad_active = back_down(grad_out, w_down)
    grad_down = weight_grad(gathered_act, grad_rows_out)
    grad_act_f = grad_active.astype(jnp.float32)
    grad_gate = grad_act_f * up_vals * sigmoid_gate * (1.0 + gate_vals * (1.0 - sigmoid_gate))
    grad_up = grad_act_f * silu_gate
    grad_gate_up_rows = jnp.concatenate([grad_gate, grad_up], axis=1).astype(jnp.bfloat16)
    grad_cols_two, grad_normed_two = back_up(grad_gate_up_rows, gate_up_block)
    grad_gate_up = weight_grad(gathered_two, grad_cols_two).reshape(w_gate_up.shape)
    grad_hidden_norm, grad_gain_two = norm_backward(
        grad_normed_two, unit_two, rescale_two, gain_ffn
    )
    grad_hidden = grad_out.astype(jnp.float32) + grad_hidden_norm
    grad_rows_hidden, grad_mix = back_down(grad_hidden.astype(jnp.bfloat16), w_out)
    grad_out_weight = weight_grad(gathered_mix, grad_rows_hidden)
    grad_mix = grad_mix.reshape(-1, heads_here, HEAD_DIM)
    grad_parts = []
    for index in range(seq_count):
        rows_here = packed[index * seq_length : (index + 1) * seq_length]
        grad_parts.append(
            attend_backward(
                rows_here[:, 0],
                rows_here[:, 1],
                rows_here[:, 2],
                segment_ids[index],
                log_parts[index],
                grad_mix[index * seq_length : (index + 1) * seq_length],
            )
        )
    grad_packed = jnp.concatenate(grad_parts, axis=0).reshape(-1, 3 * head_cols)
    grad_cols_one, grad_normed_one = back_up(grad_packed, qkv_block)
    grad_qkv = weight_grad(gathered_one, grad_cols_one).reshape(w_qkv.shape)
    grad_input_norm, grad_gain_one = norm_backward(
        grad_normed_one, unit_one, rescale_one, gain_attn
    )
    grad_tokens = grad_hidden + grad_input_norm
    summed = lax.psum((grad_qkv, grad_out_weight, grad_gate_up, grad_down), "dp")
    gains = lax.psum((grad_gain_one, grad_gain_two), ("dp", "row"))
    return (output, grad_tokens, gains[0], gains[1], summed[0], summed[1], summed[2], summed[3])


def swap(values):
    return lax.ppermute(values, "dp", [(0, 1), (1, 0)])


def hop(values, axis, flip):
    return lax.ppermute(values, axis, [(at, at ^ flip) for at in range(lax.axis_size(axis))])


def by_core(core, mine, other, axis=0):
    first = jnp.where(core == 0, mine, other)
    second = jnp.where(core == 0, other, mine)
    return jnp.concatenate([first, second], axis=axis)


def pick(values, core, axis=0):
    half = values.shape[axis] // 2
    return lax.dynamic_slice_in_dim(values, core * half, half, axis)


def to_sequence(values, core, col, seq_length):
    seqs = values.shape[0] // seq_length
    half = seq_length // 2
    parts = values.reshape(seqs, seq_length, -1)
    mine = pick(parts, core, 1)
    other = swap(pick(parts, 1 - core, 1))
    chunks = by_core(core, mine, other)
    got = []
    for flip in range(4):
        chunk = lax.dynamic_index_in_dim(chunks, col ^ flip, 0, keepdims=False)
        got.append(hop(chunk, "col", flip) if flip else chunk)
    rows = jnp.concatenate(got, axis=1)
    return by_core(core, rows, swap(rows))


def from_sequence(rows, core, col, seq_length):
    half = rows.shape[0]
    width = rows.shape[1] // 4
    got = []
    for flip in range(4):
        chunk = rows[:, flip * width : (flip + 1) * width]
        got.append(hop(chunk, "col", flip) if flip else chunk)
    got = jnp.stack(got, axis=0)
    seqs = 2
    mine = jnp.stack(
        [lax.dynamic_index_in_dim(got, (core * seqs + at) ^ col, 0, False) for at in range(seqs)]
    )
    other = jnp.stack(
        [
            lax.dynamic_index_in_dim(got, ((1 - core) * seqs + at) ^ col, 0, False)
            for at in range(seqs)
        ]
    )
    return by_core(core, mine, swap(other), 1).reshape(seqs * seq_length, -1)


def times(left, right):
    return jnp.dot(left, right, preferred_element_type=jnp.float32)


def times_t(left, right):
    return lax.dot_general(
        left, right, (((1,), (1,)), ((), ())), preferred_element_type=jnp.float32
    )


def norm_rows(values):
    rescale = lax.rsqrt(jnp.mean(values * values, axis=1) + EPS)[:, None]
    return (values * rescale, rescale)


def norm_rows_back(grad_normed, unit_rows, rescale, gain_vec):
    weighted = grad_normed * gain_vec[None, :]
    inner = jnp.sum(weighted * unit_rows, axis=1, keepdims=True) / D
    return rescale * (weighted - unit_rows * inner)


def spread_weights(block):
    kinds, _, width = block.shape
    grid = [[None] * 4 for _ in range(4)]
    for at in range(4):
        own = hop(block, "col", at) if at else block
        grid[0][at] = own
        grid[1][at] = hop(own, "row", 1)
        grid[2][at] = hop(own, "row", 2)
        if at < 2:
            grid[3][at] = hop(grid[1][at], "row", 2)
        else:
            grid[3][at] = hop(grid[2][at], "row", 1)
    lines = [jnp.concatenate(line, axis=2) for line in grid]
    return jnp.concatenate(lines, axis=1).reshape(-1, 4 * width)


def reduce_weights(grad, kinds):
    f32, low = (jnp.float32, jnp.bfloat16)
    width = grad.shape[1] // 4
    grid = grad.astype(low).reshape(kinds, 2, 2, -1, 4 * width)
    left, right = (grid[..., : 2 * width], grid[..., 2 * width :])
    got = hop(left[:, 1], "row", 2)
    got_r = hop(right[:, :, 1], "row", 1)
    send = (left[:, 0, 1].astype(f32) + got[:, 1].astype(f32)).astype(low)
    send_r = (right[:, 1, 0].astype(f32) + got_r[:, 1].astype(f32)).astype(low)
    last = hop(send, "row", 1)
    last_r = hop(send_r, "row", 2)
    sums = left[:, 0, 0].astype(f32) + got[:, 0].astype(f32) + last.astype(f32)
    sums_r = right[:, 0, 0].astype(f32) + got_r[:, 0].astype(f32) + last_r.astype(f32)
    parts = [sums[..., width:], sums_r[..., :width], sums_r[..., width:]]
    total = sums[..., :width]
    for flip in range(1, 4):
        total = total + hop(parts[flip - 1].astype(low), "col", flip).astype(f32)
    return total


def chip_local(tokens, segment_ids, gain_attn, gain_ffn, w_qkv, w_out, w_gate_up, w_down, grad_out):
    core = lax.axis_index("dp")
    col = lax.axis_index("col")
    length = segment_ids.shape[1]
    features = w_qkv.shape[0]
    head_cols = w_qkv.shape[2] // 2
    heads = 4 * head_cols // HEAD_DIM
    factor = HEAD_DIM ** (-0.5)

    values = to_sequence(tokens, core, col, length).astype(jnp.float32)
    attn_block = jnp.concatenate(
        [pick(w_qkv, core, 2).transpose(1, 2, 0), pick(w_out, core)[None]], axis=0
    )
    big_attn = spread_weights(attn_block)
    big_qkv, big_out = (big_attn[: 12 * head_cols], big_attn[12 * head_cols :])
    gains = jnp.stack([gain_attn, gain_ffn], axis=0)
    gains = jnp.concatenate([gains] + [hop(gains, "col", flip) for flip in range(1, 4)], axis=1)
    corner = [(4 * at + to, 4 * to + at) for at in range(4) for to in range(4)]
    segment_rows = lax.ppermute(segment_ids, ("row", "col"), corner)
    segment_rows = by_core(core, segment_rows, swap(segment_rows))
    segment = lax.dynamic_index_in_dim(segment_rows, col, 0, keepdims=False)
    big_gate_up = spread_weights(pick(w_gate_up, core, 2).transpose(1, 2, 0))
    big_down = spread_weights(pick(w_down, core)[None])
    cotangent = to_sequence(grad_out, core, col, length)

    unit_one, rescale_one = norm_rows(values)
    normed_one = (unit_one * gains[0][None, :]).astype(jnp.bfloat16)
    packed = times_t(normed_one, big_qkv).astype(jnp.bfloat16).reshape(length, 3, heads, HEAD_DIM)
    queries, keys, vals = (packed[:, 0], packed[:, 1], packed[:, 2])
    scores = jnp.einsum("qhd,khd->hqk", queries, keys, preferred_element_type=jnp.float32) * factor
    spot = jnp.arange(length, dtype=jnp.int32)
    live = (segment[:, None] == segment[None, :]) & (spot[None, :] <= spot[:, None])
    scores = jnp.where(live[None], scores, MASKED)
    expo = jnp.exp(scores - jnp.max(scores, axis=-1, keepdims=True))
    prob = expo / jnp.sum(expo, axis=-1, keepdims=True)
    prob_low = prob.astype(jnp.bfloat16)
    mixed = jnp.einsum("hqk,khd->qhd", prob_low, vals, preferred_element_type=jnp.float32)
    mixed = mixed.reshape(length, -1).astype(jnp.bfloat16)
    branch = times(mixed, big_out)
    hidden_rows = values + (branch + swap(branch))
    unit_two, rescale_two = norm_rows(hidden_rows)
    normed_two = (unit_two * gains[1][None, :]).astype(jnp.bfloat16)
    gate_up = times_t(normed_two, big_gate_up).astype(jnp.bfloat16)
    half = gate_up.shape[1] // 2
    gate_vals = gate_up[:, :half].astype(jnp.float32)
    up_vals = gate_up[:, half:].astype(jnp.float32)
    sigmoid_gate = jax.nn.sigmoid(gate_vals)
    silu_gate = gate_vals * sigmoid_gate
    active = (silu_gate * up_vals).astype(jnp.bfloat16)

    grad_down = weight_grad(active, cotangent)
    mine_down = reduce_weights(grad_down, 1)
    grad_act = times_t(cotangent, big_down).astype(jnp.bfloat16).astype(jnp.float32)
    grad_gate = grad_act * up_vals * sigmoid_gate * (1.0 + gate_vals * (1.0 - sigmoid_gate))
    grad_up = grad_act * silu_gate
    grad_gu = jnp.concatenate([grad_gate, grad_up], axis=1).astype(jnp.bfloat16)
    grad_two = times(grad_gu, big_gate_up)
    grad_two = grad_two + swap(grad_two)
    grad_gate_up = weight_grad(grad_gu, normed_two)
    mine_gate_up = reduce_weights(grad_gate_up, 2)
    ffn = times(active, big_down)
    ffn_mine = pick(ffn, core) + swap(pick(ffn, 1 - core))
    output = (pick(hidden_rows, core) + ffn_mine).astype(jnp.bfloat16)
    output = from_sequence(output, core, col, length)
    back_two = norm_rows_back(grad_two, unit_two, rescale_two, gains[1])
    gain_two = jnp.sum(pick(grad_two * unit_two, core), axis=0)
    grad_hidden = cotangent.astype(jnp.float32) + back_two
    grad_branch = grad_hidden.astype(jnp.bfloat16)
    grad_w_out = weight_grad(mixed, grad_branch)
    mine_out = reduce_weights(grad_w_out, 1)
    grad_mix = times_t(grad_branch, big_out).astype(jnp.bfloat16).reshape(length, heads, HEAD_DIM)
    grad_vals = jnp.einsum("hqk,qhd->khd", prob_low, grad_mix, preferred_element_type=jnp.float32)
    grad_prob = jnp.einsum("qhd,khd->hqk", grad_mix, vals, preferred_element_type=jnp.float32)
    inner = jnp.sum(prob * grad_prob, axis=-1, keepdims=True)
    grad_scores = (prob * (grad_prob - inner)).astype(jnp.bfloat16)
    grad_queries = factor * jnp.einsum(
        "hqk,khd->qhd", grad_scores, keys, preferred_element_type=jnp.float32
    )
    grad_keys = factor * jnp.einsum(
        "hqk,qhd->khd", grad_scores, queries, preferred_element_type=jnp.float32
    )
    grad_packed = jnp.stack([grad_queries, grad_keys, grad_vals], axis=1)
    grad_packed = grad_packed.astype(jnp.bfloat16).reshape(length, -1)
    grad_qkv = weight_grad(grad_packed, normed_one)
    mine_qkv = reduce_weights(grad_qkv, 3)
    grad_one = times(grad_packed, big_qkv)
    grad_one = pick(grad_one, core) + swap(pick(grad_one, 1 - core))
    unit_mine = pick(unit_one, core)
    back_one = norm_rows_back(grad_one, unit_mine, pick(rescale_one, core), gains[0])
    gain_one = jnp.sum(grad_one * unit_mine, axis=0)
    grad_rows = (pick(grad_hidden, core) + back_one).astype(jnp.bfloat16)
    grad_tokens = from_sequence(grad_rows, core, col, length).astype(jnp.float32)

    gain_sums = jnp.stack([gain_one, gain_two], axis=0)
    gain_sums = gain_sums + swap(gain_sums)
    gain_sums = gain_sums + hop(gain_sums, "row", 1)
    gain_sums = gain_sums + hop(gain_sums, "row", 2)
    gain_mine = gain_sums[:, :features]
    for flip in range(1, 4):
        piece = gain_sums[:, flip * features : (flip + 1) * features]
        gain_mine = gain_mine + hop(piece, "col", flip)

    def joined(mine):
        low = mine.astype(jnp.bfloat16)
        return by_core(core, low, swap(low), 1).astype(jnp.float32)

    return (
        output,
        grad_tokens,
        gain_mine[0],
        gain_mine[1],
        joined(mine_qkv).transpose(2, 0, 1),
        joined(mine_out)[0],
        joined(mine_gate_up).transpose(2, 0, 1),
        joined(mine_down)[0],
    )


def layer(tokens, segment_ids, *rest):
    sizes = (lax.axis_size("dp"), lax.axis_size("row"), lax.axis_size("col"))
    if sizes == (2, 4, 4) and tokens.shape[0] == 2 * segment_ids.shape[1]:
        return chip_local(tokens, segment_ids, *rest)
    return local(tokens, segment_ids, *rest)


def solution(mesh):
    in_specs = (
        P(("dp", "row"), "col"),
        P(("dp", "col"), None),
        P("col"),
        P("col"),
        P("col", None, "row"),
        P("row", "col"),
        P("col", None, "row"),
        P("row", "col"),
        P(("dp", "row"), "col"),
    )
    out_specs = (
        P(("dp", "row"), "col"),
        P(("dp", "row"), "col"),
        P("col"),
        P("col"),
        P("col", None, "row"),
        P("row", "col"),
        P("col", None, "row"),
        P("row", "col"),
    )
    return jax.shard_map(layer, mesh=mesh, in_specs=in_specs, out_specs=out_specs, check_vma=False)
```

```python
import jax
import jax.numpy as jnp
from jax import lax
from jax.experimental import pallas as pl
from jax.sharding import PartitionSpec as P

D = 1024
HEAD_DIM = 64


EPS = 1e-06
MASKED = -1e30


def row_norm(values, gain_vec):
    squares = lax.psum(jnp.sum(values * values, axis=1), "col")
    rescale = lax.rsqrt(squares / D + EPS)
    unit_rows = values * rescale[:, None]
    return (unit_rows, rescale, (unit_rows * gain_vec[None, :]).astype(jnp.bfloat16))


def norm_backward(grad_normed, unit_rows, rescale, gain_vec):
    weighted = grad_normed * gain_vec[None, :]
    inner_sum = lax.psum(jnp.sum(weighted * unit_rows, axis=1), "col")
    grad_in = rescale[:, None] * (weighted - unit_rows * (inner_sum / D)[:, None])
    grad_gain = jnp.sum(grad_normed * unit_rows, axis=0)
    return (grad_in, grad_gain)


def project_up(normed, weight_block):
    gathered = lax.all_gather(normed, "row", axis=0, tiled=True)

    def term(begin_at, row_count):
        return jnp.dot(gathered, weight_block, preferred_element_type=jnp.float32)

    result = lax.psum_scatter(
        term(jnp.int32(0), gathered.shape[0] // lax.axis_size("col") * lax.axis_size("col")),
        "col",
        scatter_dimension=0,
        tiled=True,
    )
    return (gathered, result.astype(jnp.bfloat16))


def project_down(values, weight_block):
    gathered = lax.all_gather(values, "col", axis=0, tiled=True)

    def term(begin_at, row_count):
        return jnp.dot(gathered, weight_block, preferred_element_type=jnp.float32)

    result = lax.psum_scatter(
        term(jnp.int32(0), gathered.shape[0] // lax.axis_size("row") * lax.axis_size("row")),
        "row",
        scatter_dimension=0,
        tiled=True,
    )
    return (gathered, result)


def back_down(grad_rows, weight_block):
    gathered = lax.all_gather(grad_rows, "row", axis=0, tiled=True)

    def term(begin_at, row_count):
        return lax.dot_general(
            gathered, weight_block, (((1,), (1,)), ((), ())), preferred_element_type=jnp.float32
        )

    result = lax.psum_scatter(
        term(jnp.int32(0), gathered.shape[0] // lax.axis_size("col") * lax.axis_size("col")),
        "col",
        scatter_dimension=0,
        tiled=True,
    )
    return (gathered, result.astype(jnp.bfloat16))


def back_up(grad_cols, weight_block):
    gathered = lax.all_gather(grad_cols, "col", axis=0, tiled=True)

    def term(begin_at, row_count):
        return lax.dot_general(
            gathered, weight_block, (((1,), (1,)), ((), ())), preferred_element_type=jnp.float32
        )

    result = lax.psum_scatter(
        term(jnp.int32(0), gathered.shape[0] // lax.axis_size("row") * lax.axis_size("row")),
        "row",
        scatter_dimension=0,
        tiled=True,
    )
    return (gathered, result)


def weight_grad(left_rows, right_rows):
    return lax.dot_general(
        left_rows, right_rows, (((0,), (0,)), ((), ())), preferred_element_type=jnp.float32
    )


def block_scores(queries, keys_all, query_segment, key_segment, query_place):
    raw = jnp.einsum(
        "qhd,khd->hqk", queries, keys_all, preferred_element_type=jnp.float32
    ) * HEAD_DIM ** (-0.5)
    key_place = lax.broadcasted_iota(jnp.int32, (1, keys_all.shape[0]), 1)
    allowed = (query_segment[:, None] == key_segment[None, :]) & (key_place <= query_place[:, None])
    return jnp.where(allowed[None], raw, MASKED)


def split_blocks(queries, segment):
    length = queries.shape[0]
    block_rows = min(512, length)
    blocks = length // block_rows
    place = jnp.arange(length, dtype=jnp.int32).reshape(blocks, block_rows)
    return (
        queries.reshape(blocks, block_rows, queries.shape[1], queries.shape[2]),
        segment.reshape(blocks, block_rows),
        place,
    )


def attend_forward(queries, keys_all, values_all, segment):
    query_blocks, segment_blocks, place_blocks = split_blocks(queries, segment)

    def one_block(item):
        query_rows, query_segment, query_place = item
        scores = block_scores(query_rows, keys_all, query_segment, segment, query_place)
        row_max = jnp.max(scores, axis=-1, keepdims=True)
        expo = jnp.exp(scores - row_max)
        row_total = jnp.sum(expo, axis=-1, keepdims=True)
        prob_rows = (expo / row_total).astype(jnp.bfloat16)
        mixed = jnp.einsum(
            "hqk,khd->qhd", prob_rows, values_all, preferred_element_type=jnp.float32
        )
        return (mixed, row_max[..., 0] + jnp.log(row_total[..., 0]))

    mixed, log_total = lax.map(one_block, (query_blocks, segment_blocks, place_blocks))
    return (mixed.reshape(queries.shape[0], -1).astype(jnp.bfloat16), log_total)


def attend_backward(queries, keys_all, values_all, segment, log_total, grad_mix):
    query_blocks, segment_blocks, place_blocks = split_blocks(queries, segment)
    grad_blocks = grad_mix.reshape(query_blocks.shape)
    factor = HEAD_DIM ** (-0.5)

    def one_block(carry, item):
        key_acc, value_acc = carry
        query_rows, query_segment, query_place, log_rows, grad_rows = item
        scores = block_scores(query_rows, keys_all, query_segment, segment, query_place)
        prob_rows = jnp.exp(scores - log_rows[..., None])
        value_acc = value_acc + jnp.einsum(
            "hqk,qhd->khd",
            prob_rows.astype(jnp.bfloat16),
            grad_rows,
            preferred_element_type=jnp.float32,
        )
        grad_prob = jnp.einsum(
            "qhd,khd->hqk", grad_rows, values_all, preferred_element_type=jnp.float32
        )
        grad_scores = (
            prob_rows * (grad_prob - jnp.sum(prob_rows * grad_prob, axis=-1, keepdims=True))
        ).astype(jnp.bfloat16)
        grad_query = (
            jnp.einsum("hqk,khd->qhd", grad_scores, keys_all, preferred_element_type=jnp.float32)
            * factor
        )
        key_acc = (
            key_acc
            + jnp.einsum(
                "hqk,qhd->khd", grad_scores, query_rows, preferred_element_type=jnp.float32
            )
            * factor
        )
        return ((key_acc, value_acc), grad_query)

    zeros_like_keys = jnp.zeros(keys_all.shape, jnp.float32)
    (grad_keys, grad_values), grad_queries = lax.scan(
        one_block,
        (zeros_like_keys, zeros_like_keys),
        (query_blocks, segment_blocks, place_blocks, log_total, grad_blocks),
    )
    grad_queries = grad_queries.reshape(queries.shape)
    return jnp.stack([grad_queries, grad_keys, grad_values], axis=1).astype(jnp.bfloat16)


def local(tokens, segment_ids, gain_attn, gain_ffn, w_qkv, w_out, w_gate_up, w_down, grad_out):
    values = tokens.astype(jnp.float32)
    head_cols = w_qkv.shape[2]
    heads_here = head_cols // HEAD_DIM
    hidden_here = w_gate_up.shape[2]
    qkv_block = w_qkv.reshape(w_qkv.shape[0], 3 * head_cols)
    gate_up_block = w_gate_up.reshape(w_gate_up.shape[0], 2 * hidden_here)
    seq_count, seq_length = segment_ids.shape
    unit_one, rescale_one, normed_one = row_norm(values, gain_attn)
    gathered_one, packed = project_up(normed_one, qkv_block)
    packed = packed.reshape(-1, 3, heads_here, HEAD_DIM)
    mix_parts, log_parts = ([], [])
    for index in range(seq_count):
        rows_here = packed[index * seq_length : (index + 1) * seq_length]
        mixed, log_total = attend_forward(
            rows_here[:, 0], rows_here[:, 1], rows_here[:, 2], segment_ids[index]
        )
        mix_parts.append(mixed)
        log_parts.append(log_total)
    attn_mix = jnp.concatenate(mix_parts, axis=0)
    gathered_mix, attn_branch = project_down(attn_mix, w_out)
    hidden = values + attn_branch
    unit_two, rescale_two, normed_two = row_norm(hidden, gain_ffn)
    gathered_two, gate_up = project_up(normed_two, gate_up_block)
    gate_vals = gate_up[:, :hidden_here].astype(jnp.float32)
    up_vals = gate_up[:, hidden_here:].astype(jnp.float32)
    sigmoid_gate = jax.nn.sigmoid(gate_vals)
    silu_gate = gate_vals * sigmoid_gate
    active = (silu_gate * up_vals).astype(jnp.bfloat16)
    gathered_act, ffn_branch = project_down(active, w_down)
    output = (hidden + ffn_branch).astype(jnp.bfloat16)
    grad_rows_out, grad_active = back_down(grad_out, w_down)
    grad_down = weight_grad(gathered_act, grad_rows_out)
    grad_act_f = grad_active.astype(jnp.float32)
    grad_gate = grad_act_f * up_vals * sigmoid_gate * (1.0 + gate_vals * (1.0 - sigmoid_gate))
    grad_up = grad_act_f * silu_gate
    grad_gate_up_rows = jnp.concatenate([grad_gate, grad_up], axis=1).astype(jnp.bfloat16)
    grad_cols_two, grad_normed_two = back_up(grad_gate_up_rows, gate_up_block)
    grad_gate_up = weight_grad(gathered_two, grad_cols_two).reshape(w_gate_up.shape)
    grad_hidden_norm, grad_gain_two = norm_backward(
        grad_normed_two, unit_two, rescale_two, gain_ffn
    )
    grad_hidden = grad_out.astype(jnp.float32) + grad_hidden_norm
    grad_rows_hidden, grad_mix = back_down(grad_hidden.astype(jnp.bfloat16), w_out)
    grad_out_weight = weight_grad(gathered_mix, grad_rows_hidden)
    grad_mix = grad_mix.reshape(-1, heads_here, HEAD_DIM)
    grad_parts = []
    for index in range(seq_count):
        rows_here = packed[index * seq_length : (index + 1) * seq_length]
        grad_parts.append(
            attend_backward(
                rows_here[:, 0],
                rows_here[:, 1],
                rows_here[:, 2],
                segment_ids[index],
                log_parts[index],
                grad_mix[index * seq_length : (index + 1) * seq_length],
            )
        )
    grad_packed = jnp.concatenate(grad_parts, axis=0).reshape(-1, 3 * head_cols)
    grad_cols_one, grad_normed_one = back_up(grad_packed, qkv_block)
    grad_qkv = weight_grad(gathered_one, grad_cols_one).reshape(w_qkv.shape)
    grad_input_norm, grad_gain_one = norm_backward(
        grad_normed_one, unit_one, rescale_one, gain_attn
    )
    grad_tokens = grad_hidden + grad_input_norm
    summed = lax.psum((grad_qkv, grad_out_weight, grad_gate_up, grad_down), "dp")
    gains = lax.psum((grad_gain_one, grad_gain_two), ("dp", "row"))
    return (output, grad_tokens, gains[0], gains[1], summed[0], summed[1], summed[2], summed[3])


def swap(values):
    return lax.ppermute(values, "dp", [(0, 1), (1, 0)])


def hop(values, axis, flip):
    return lax.ppermute(values, axis, [(at, at ^ flip) for at in range(lax.axis_size(axis))])


def by_core(core, mine, other, axis=0):
    first = jnp.where(core == 0, mine, other)
    second = jnp.where(core == 0, other, mine)
    return jnp.concatenate([first, second], axis=axis)


def pick(values, core, axis=0):
    half = values.shape[axis] // 2
    return lax.dynamic_slice_in_dim(values, core * half, half, axis)


def to_sequence(values, core, col, seq_length):
    seqs = values.shape[0] // seq_length
    half = seq_length // 2
    parts = values.reshape(seqs, seq_length, -1)
    mine = pick(parts, core, 1)
    other = swap(pick(parts, 1 - core, 1))
    chunks = by_core(core, mine, other)
    got = []
    for flip in range(4):
        chunk = lax.dynamic_index_in_dim(chunks, col ^ flip, 0, keepdims=False)
        got.append(hop(chunk, "col", flip) if flip else chunk)
    rows = jnp.concatenate(got, axis=1)
    return by_core(core, rows, swap(rows))


def from_sequence(rows, core, col, seq_length):
    half = rows.shape[0]
    width = rows.shape[1] // 4
    got = []
    for flip in range(4):
        chunk = rows[:, flip * width : (flip + 1) * width]
        got.append(hop(chunk, "col", flip) if flip else chunk)
    got = jnp.stack(got, axis=0)
    seqs = 2
    mine = jnp.stack(
        [lax.dynamic_index_in_dim(got, (core * seqs + at) ^ col, 0, False) for at in range(seqs)]
    )
    other = jnp.stack(
        [
            lax.dynamic_index_in_dim(got, ((1 - core) * seqs + at) ^ col, 0, False)
            for at in range(seqs)
        ]
    )
    return by_core(core, mine, swap(other), 1).reshape(seqs * seq_length, -1)


def times(left, right):
    return jnp.dot(left, right, preferred_element_type=jnp.float32)


def times_t(left, right):
    return lax.dot_general(
        left, right, (((1,), (1,)), ((), ())), preferred_element_type=jnp.float32
    )


def norm_rows(values):
    rescale = lax.rsqrt(jnp.mean(values * values, axis=1) + EPS)[:, None]
    return (values * rescale, rescale)


def norm_rows_back(grad_normed, unit_rows, rescale, gain_vec):
    weighted = grad_normed * gain_vec[None, :]
    inner = jnp.sum(weighted * unit_rows, axis=1, keepdims=True) / D
    return rescale * (weighted - unit_rows * inner)


def join_blocks(*refs):
    blocks, whole = (refs[:16], refs[16])
    _, rows, width = blocks[0].shape
    for at, block in enumerate(blocks):
        line, place = divmod(at, 4)
        whole[:, line * rows : (line + 1) * rows, place * width : (place + 1) * width] = block[...]


def spread_weights(block):
    grid = [[None] * 4 for _ in range(4)]
    for at in range(4):
        own = hop(block, "col", at) if at else block
        grid[0][at] = own
        grid[1][at] = hop(own, "row", 1)
        grid[2][at] = hop(own, "row", 2)
    for at in range(4):
        if at < 2:
            grid[3][at] = hop(grid[1][at], "row", 2)
        else:
            grid[3][at] = hop(grid[2][at], "row", 1)
    return grid


def join_weights(grid):
    kinds, rows, width = grid[0][0].shape
    whole = pl.pallas_call(
        join_blocks, out_shape=jax.ShapeDtypeStruct((kinds, 4 * rows, 4 * width), jnp.bfloat16)
    )(*[block for line in grid for block in line])
    return whole.reshape(-1, 4 * width)


def reduce_weights(grad, kinds):
    f32, low = (jnp.float32, jnp.bfloat16)
    width = grad.shape[1] // 4
    grid = grad.astype(low).reshape(kinds, 2, 2, -1, 4 * width)
    left, right = (grid[..., : 2 * width], grid[..., 2 * width :])
    got = hop(left[:, 1], "row", 2)
    got_r = hop(right[:, :, 1], "row", 1)
    send = (left[:, 0, 1].astype(f32) + got[:, 1].astype(f32)).astype(low)
    send_r = (right[:, 1, 0].astype(f32) + got_r[:, 1].astype(f32)).astype(low)
    last = hop(send, "row", 1)
    last_r = hop(send_r, "row", 2)
    sums = left[:, 0, 0].astype(f32) + got[:, 0].astype(f32) + last.astype(f32)
    sums_r = right[:, 0, 0].astype(f32) + got_r[:, 0].astype(f32) + last_r.astype(f32)
    parts = [sums[..., width:], sums_r[..., :width], sums_r[..., width:]]
    total = sums[..., :width]
    for flip in range(1, 4):
        total = total + hop(parts[flip - 1].astype(low), "col", flip).astype(f32)
    return total


def chip_local(tokens, segment_ids, gain_attn, gain_ffn, w_qkv, w_out, w_gate_up, w_down, grad_out):
    core = lax.axis_index("dp")
    col = lax.axis_index("col")
    length = segment_ids.shape[1]
    features = w_qkv.shape[0]
    head_cols = w_qkv.shape[2] // 2
    heads = 4 * head_cols // HEAD_DIM
    factor = HEAD_DIM ** (-0.5)

    values = to_sequence(tokens, core, col, length).astype(jnp.float32)
    attn_block = jnp.concatenate(
        [pick(w_qkv, core, 2).transpose(1, 2, 0), pick(w_out, core)[None]], axis=0
    )
    attn_grid = spread_weights(attn_block)
    big_attn = join_weights(attn_grid)
    big_qkv, big_out = (big_attn[: 12 * head_cols], big_attn[12 * head_cols :])
    gains = jnp.stack([gain_attn, gain_ffn], axis=0)
    gains = jnp.concatenate([gains] + [hop(gains, "col", flip) for flip in range(1, 4)], axis=1)
    corner = [(4 * at + to, 4 * to + at) for at in range(4) for to in range(4)]
    segment_rows = lax.ppermute(segment_ids, ("row", "col"), corner)
    segment_rows = by_core(core, segment_rows, swap(segment_rows))
    segment = lax.dynamic_index_in_dim(segment_rows, col, 0, keepdims=False)
    gate_up_block = pick(w_gate_up, core, 2).transpose(1, 2, 0)
    gate_up_block, _ = lax.optimization_barrier((gate_up_block, attn_grid[1] + attn_grid[2]))
    gate_up_grid = spread_weights(gate_up_block)
    big_gate_up = join_weights(gate_up_grid)
    late = (pick(w_down, core)[None], grad_out)
    (down_block, grad_late), _ = lax.optimization_barrier((late, gate_up_grid[1] + gate_up_grid[2]))
    big_down = join_weights(spread_weights(down_block))
    cotangent = to_sequence(grad_late, core, col, length)

    unit_one, rescale_one = norm_rows(values)
    normed_one = (unit_one * gains[0][None, :]).astype(jnp.bfloat16)
    packed = times_t(normed_one, big_qkv).astype(jnp.bfloat16).reshape(length, 3, heads, HEAD_DIM)
    queries, keys, vals = (packed[:, 0], packed[:, 1], packed[:, 2])
    scores = jnp.einsum("qhd,khd->hqk", queries, keys, preferred_element_type=jnp.float32) * factor
    spot = jnp.arange(length, dtype=jnp.int32)
    live = (segment[:, None] == segment[None, :]) & (spot[None, :] <= spot[:, None])
    scores = jnp.where(live[None], scores, MASKED)
    expo = jnp.exp(scores - jnp.max(scores, axis=-1, keepdims=True))
    prob = expo / jnp.sum(expo, axis=-1, keepdims=True)
    prob_low = prob.astype(jnp.bfloat16)
    mixed = jnp.einsum("hqk,khd->qhd", prob_low, vals, preferred_element_type=jnp.float32)
    mixed = mixed.reshape(length, -1).astype(jnp.bfloat16)
    branch = times(mixed, big_out)
    hidden_rows = values + (branch + swap(branch))
    unit_two, rescale_two = norm_rows(hidden_rows)
    normed_two = (unit_two * gains[1][None, :]).astype(jnp.bfloat16)
    gate_up = times_t(normed_two, big_gate_up).astype(jnp.bfloat16)
    half = gate_up.shape[1] // 2
    gate_vals = gate_up[:, :half].astype(jnp.float32)
    up_vals = gate_up[:, half:].astype(jnp.float32)
    sigmoid_gate = jax.nn.sigmoid(gate_vals)
    silu_gate = gate_vals * sigmoid_gate
    active = (silu_gate * up_vals).astype(jnp.bfloat16)

    grad_down = weight_grad(active, cotangent)
    mine_down = reduce_weights(grad_down, 1)
    grad_act = times_t(cotangent, big_down).astype(jnp.bfloat16).astype(jnp.float32)
    grad_gate = grad_act * up_vals * sigmoid_gate * (1.0 + gate_vals * (1.0 - sigmoid_gate))
    grad_up = grad_act * silu_gate
    grad_gu = jnp.concatenate([grad_gate, grad_up], axis=1).astype(jnp.bfloat16)
    grad_two = times(grad_gu, big_gate_up)
    grad_two = grad_two + swap(grad_two)
    grad_gate_up = weight_grad(grad_gu, normed_two)
    mine_gate_up = reduce_weights(grad_gate_up, 2)
    ffn = times(active, big_down)
    ffn_mine = pick(ffn, core) + swap(pick(ffn, 1 - core))
    output = (pick(hidden_rows, core) + ffn_mine).astype(jnp.bfloat16)
    output = from_sequence(output, core, col, length)
    back_two = norm_rows_back(grad_two, unit_two, rescale_two, gains[1])
    gain_two = jnp.sum(pick(grad_two * unit_two, core), axis=0)
    grad_hidden = cotangent.astype(jnp.float32) + back_two
    grad_branch = grad_hidden.astype(jnp.bfloat16)
    grad_w_out = weight_grad(mixed, grad_branch)
    mine_out = reduce_weights(grad_w_out, 1)
    grad_mix = times_t(grad_branch, big_out).astype(jnp.bfloat16).reshape(length, heads, HEAD_DIM)
    grad_vals = jnp.einsum("hqk,qhd->khd", prob_low, grad_mix, preferred_element_type=jnp.float32)
    grad_prob = jnp.einsum("qhd,khd->hqk", grad_mix, vals, preferred_element_type=jnp.float32)
    inner = jnp.sum(prob * grad_prob, axis=-1, keepdims=True)
    grad_scores = (prob * (grad_prob - inner)).astype(jnp.bfloat16)
    grad_queries = factor * jnp.einsum(
        "hqk,khd->qhd", grad_scores, keys, preferred_element_type=jnp.float32
    )
    grad_keys = factor * jnp.einsum(
        "hqk,qhd->khd", grad_scores, queries, preferred_element_type=jnp.float32
    )
    grad_packed = jnp.stack([grad_queries, grad_keys, grad_vals], axis=1)
    grad_packed = grad_packed.astype(jnp.bfloat16).reshape(length, -1)
    grad_qkv = weight_grad(grad_packed, normed_one)
    mine_qkv = reduce_weights(grad_qkv, 3)
    grad_one = times(grad_packed, big_qkv)
    grad_one = pick(grad_one, core) + swap(pick(grad_one, 1 - core))
    unit_mine = pick(unit_one, core)
    back_one = norm_rows_back(grad_one, unit_mine, pick(rescale_one, core), gains[0])
    gain_one = jnp.sum(grad_one * unit_mine, axis=0)
    grad_rows = (pick(grad_hidden, core) + back_one).astype(jnp.bfloat16)
    grad_tokens = from_sequence(grad_rows, core, col, length).astype(jnp.float32)

    gain_sums = jnp.stack([gain_one, gain_two], axis=0)
    gain_sums = gain_sums + swap(gain_sums)
    gain_sums = gain_sums + hop(gain_sums, "row", 1)
    gain_sums = gain_sums + hop(gain_sums, "row", 2)
    gain_mine = gain_sums[:, :features]
    for flip in range(1, 4):
        piece = gain_sums[:, flip * features : (flip + 1) * features]
        gain_mine = gain_mine + hop(piece, "col", flip)

    def joined(mine):
        low = mine.astype(jnp.bfloat16)
        return by_core(core, low, swap(low), 1).astype(jnp.float32)

    return (
        output,
        grad_tokens,
        gain_mine[0],
        gain_mine[1],
        joined(mine_qkv).transpose(2, 0, 1),
        joined(mine_out)[0],
        joined(mine_gate_up).transpose(2, 0, 1),
        joined(mine_down)[0],
    )


def layer(tokens, segment_ids, *rest):
    sizes = (lax.axis_size("dp"), lax.axis_size("row"), lax.axis_size("col"))
    if sizes == (2, 4, 4) and tokens.shape[0] == 2 * segment_ids.shape[1]:
        return chip_local(tokens, segment_ids, *rest)
    return local(tokens, segment_ids, *rest)


def solution(mesh):
    in_specs = (
        P(("dp", "row"), "col"),
        P(("dp", "col"), None),
        P("col"),
        P("col"),
        P("col", None, "row"),
        P("row", "col"),
        P("col", None, "row"),
        P("row", "col"),
        P(("dp", "row"), "col"),
    )
    out_specs = (
        P(("dp", "row"), "col"),
        P(("dp", "row"), "col"),
        P("col"),
        P("col"),
        P("col", None, "row"),
        P("row", "col"),
        P("col", None, "row"),
        P("row", "col"),
    )
    return jax.shard_map(layer, mesh=mesh, in_specs=in_specs, out_specs=out_specs, check_vma=False)
```

```python
import jax
import jax.numpy as jnp
from jax import lax
from jax.experimental import pallas as pl
from jax.experimental.pallas import tpu as pltpu
from jax.sharding import PartitionSpec as P

D = 1024
HEAD_DIM = 64


EPS = 1e-06
MASKED = -1e30


def row_norm(values, gain_vec):
    squares = lax.psum(jnp.sum(values * values, axis=1), "col")
    rescale = lax.rsqrt(squares / D + EPS)
    unit_rows = values * rescale[:, None]
    return (unit_rows, rescale, (unit_rows * gain_vec[None, :]).astype(jnp.bfloat16))


def norm_backward(grad_normed, unit_rows, rescale, gain_vec):
    weighted = grad_normed * gain_vec[None, :]
    inner_sum = lax.psum(jnp.sum(weighted * unit_rows, axis=1), "col")
    grad_in = rescale[:, None] * (weighted - unit_rows * (inner_sum / D)[:, None])
    grad_gain = jnp.sum(grad_normed * unit_rows, axis=0)
    return (grad_in, grad_gain)


def project_up(normed, weight_block):
    gathered = lax.all_gather(normed, "row", axis=0, tiled=True)

    def term(begin_at, row_count):
        return jnp.dot(gathered, weight_block, preferred_element_type=jnp.float32)

    result = lax.psum_scatter(
        term(jnp.int32(0), gathered.shape[0] // lax.axis_size("col") * lax.axis_size("col")),
        "col",
        scatter_dimension=0,
        tiled=True,
    )
    return (gathered, result.astype(jnp.bfloat16))


def project_down(values, weight_block):
    gathered = lax.all_gather(values, "col", axis=0, tiled=True)

    def term(begin_at, row_count):
        return jnp.dot(gathered, weight_block, preferred_element_type=jnp.float32)

    result = lax.psum_scatter(
        term(jnp.int32(0), gathered.shape[0] // lax.axis_size("row") * lax.axis_size("row")),
        "row",
        scatter_dimension=0,
        tiled=True,
    )
    return (gathered, result)


def back_down(grad_rows, weight_block):
    gathered = lax.all_gather(grad_rows, "row", axis=0, tiled=True)

    def term(begin_at, row_count):
        return lax.dot_general(
            gathered, weight_block, (((1,), (1,)), ((), ())), preferred_element_type=jnp.float32
        )

    result = lax.psum_scatter(
        term(jnp.int32(0), gathered.shape[0] // lax.axis_size("col") * lax.axis_size("col")),
        "col",
        scatter_dimension=0,
        tiled=True,
    )
    return (gathered, result.astype(jnp.bfloat16))


def back_up(grad_cols, weight_block):
    gathered = lax.all_gather(grad_cols, "col", axis=0, tiled=True)

    def term(begin_at, row_count):
        return lax.dot_general(
            gathered, weight_block, (((1,), (1,)), ((), ())), preferred_element_type=jnp.float32
        )

    result = lax.psum_scatter(
        term(jnp.int32(0), gathered.shape[0] // lax.axis_size("row") * lax.axis_size("row")),
        "row",
        scatter_dimension=0,
        tiled=True,
    )
    return (gathered, result)


def weight_grad(left_rows, right_rows):
    return lax.dot_general(
        left_rows, right_rows, (((0,), (0,)), ((), ())), preferred_element_type=jnp.float32
    )


def block_scores(queries, keys_all, query_segment, key_segment, query_place):
    raw = jnp.einsum(
        "qhd,khd->hqk", queries, keys_all, preferred_element_type=jnp.float32
    ) * HEAD_DIM ** (-0.5)
    key_place = lax.broadcasted_iota(jnp.int32, (1, keys_all.shape[0]), 1)
    allowed = (query_segment[:, None] == key_segment[None, :]) & (key_place <= query_place[:, None])
    return jnp.where(allowed[None], raw, MASKED)


def split_blocks(queries, segment):
    length = queries.shape[0]
    block_rows = min(512, length)
    blocks = length // block_rows
    place = jnp.arange(length, dtype=jnp.int32).reshape(blocks, block_rows)
    return (
        queries.reshape(blocks, block_rows, queries.shape[1], queries.shape[2]),
        segment.reshape(blocks, block_rows),
        place,
    )


def attend_forward(queries, keys_all, values_all, segment):
    query_blocks, segment_blocks, place_blocks = split_blocks(queries, segment)

    def one_block(item):
        query_rows, query_segment, query_place = item
        scores = block_scores(query_rows, keys_all, query_segment, segment, query_place)
        row_max = jnp.max(scores, axis=-1, keepdims=True)
        expo = jnp.exp(scores - row_max)
        row_total = jnp.sum(expo, axis=-1, keepdims=True)
        prob_rows = (expo / row_total).astype(jnp.bfloat16)
        mixed = jnp.einsum(
            "hqk,khd->qhd", prob_rows, values_all, preferred_element_type=jnp.float32
        )
        return (mixed, row_max[..., 0] + jnp.log(row_total[..., 0]))

    mixed, log_total = lax.map(one_block, (query_blocks, segment_blocks, place_blocks))
    return (mixed.reshape(queries.shape[0], -1).astype(jnp.bfloat16), log_total)


def attend_backward(queries, keys_all, values_all, segment, log_total, grad_mix):
    query_blocks, segment_blocks, place_blocks = split_blocks(queries, segment)
    grad_blocks = grad_mix.reshape(query_blocks.shape)
    factor = HEAD_DIM ** (-0.5)

    def one_block(carry, item):
        key_acc, value_acc = carry
        query_rows, query_segment, query_place, log_rows, grad_rows = item
        scores = block_scores(query_rows, keys_all, query_segment, segment, query_place)
        prob_rows = jnp.exp(scores - log_rows[..., None])
        value_acc = value_acc + jnp.einsum(
            "hqk,qhd->khd",
            prob_rows.astype(jnp.bfloat16),
            grad_rows,
            preferred_element_type=jnp.float32,
        )
        grad_prob = jnp.einsum(
            "qhd,khd->hqk", grad_rows, values_all, preferred_element_type=jnp.float32
        )
        grad_scores = (
            prob_rows * (grad_prob - jnp.sum(prob_rows * grad_prob, axis=-1, keepdims=True))
        ).astype(jnp.bfloat16)
        grad_query = (
            jnp.einsum("hqk,khd->qhd", grad_scores, keys_all, preferred_element_type=jnp.float32)
            * factor
        )
        key_acc = (
            key_acc
            + jnp.einsum(
                "hqk,qhd->khd", grad_scores, query_rows, preferred_element_type=jnp.float32
            )
            * factor
        )
        return ((key_acc, value_acc), grad_query)

    zeros_like_keys = jnp.zeros(keys_all.shape, jnp.float32)
    (grad_keys, grad_values), grad_queries = lax.scan(
        one_block,
        (zeros_like_keys, zeros_like_keys),
        (query_blocks, segment_blocks, place_blocks, log_total, grad_blocks),
    )
    grad_queries = grad_queries.reshape(queries.shape)
    return jnp.stack([grad_queries, grad_keys, grad_values], axis=1).astype(jnp.bfloat16)


def local(tokens, segment_ids, gain_attn, gain_ffn, w_qkv, w_out, w_gate_up, w_down, grad_out):
    values = tokens.astype(jnp.float32)
    head_cols = w_qkv.shape[2]
    heads_here = head_cols // HEAD_DIM
    hidden_here = w_gate_up.shape[2]
    qkv_block = w_qkv.reshape(w_qkv.shape[0], 3 * head_cols)
    gate_up_block = w_gate_up.reshape(w_gate_up.shape[0], 2 * hidden_here)
    seq_count, seq_length = segment_ids.shape
    unit_one, rescale_one, normed_one = row_norm(values, gain_attn)
    gathered_one, packed = project_up(normed_one, qkv_block)
    packed = packed.reshape(-1, 3, heads_here, HEAD_DIM)
    mix_parts, log_parts = ([], [])
    for index in range(seq_count):
        rows_here = packed[index * seq_length : (index + 1) * seq_length]
        mixed, log_total = attend_forward(
            rows_here[:, 0], rows_here[:, 1], rows_here[:, 2], segment_ids[index]
        )
        mix_parts.append(mixed)
        log_parts.append(log_total)
    attn_mix = jnp.concatenate(mix_parts, axis=0)
    gathered_mix, attn_branch = project_down(attn_mix, w_out)
    hidden = values + attn_branch
    unit_two, rescale_two, normed_two = row_norm(hidden, gain_ffn)
    gathered_two, gate_up = project_up(normed_two, gate_up_block)
    gate_vals = gate_up[:, :hidden_here].astype(jnp.float32)
    up_vals = gate_up[:, hidden_here:].astype(jnp.float32)
    sigmoid_gate = jax.nn.sigmoid(gate_vals)
    silu_gate = gate_vals * sigmoid_gate
    active = (silu_gate * up_vals).astype(jnp.bfloat16)
    gathered_act, ffn_branch = project_down(active, w_down)
    output = (hidden + ffn_branch).astype(jnp.bfloat16)
    grad_rows_out, grad_active = back_down(grad_out, w_down)
    grad_down = weight_grad(gathered_act, grad_rows_out)
    grad_act_f = grad_active.astype(jnp.float32)
    grad_gate = grad_act_f * up_vals * sigmoid_gate * (1.0 + gate_vals * (1.0 - sigmoid_gate))
    grad_up = grad_act_f * silu_gate
    grad_gate_up_rows = jnp.concatenate([grad_gate, grad_up], axis=1).astype(jnp.bfloat16)
    grad_cols_two, grad_normed_two = back_up(grad_gate_up_rows, gate_up_block)
    grad_gate_up = weight_grad(gathered_two, grad_cols_two).reshape(w_gate_up.shape)
    grad_hidden_norm, grad_gain_two = norm_backward(
        grad_normed_two, unit_two, rescale_two, gain_ffn
    )
    grad_hidden = grad_out.astype(jnp.float32) + grad_hidden_norm
    grad_rows_hidden, grad_mix = back_down(grad_hidden.astype(jnp.bfloat16), w_out)
    grad_out_weight = weight_grad(gathered_mix, grad_rows_hidden)
    grad_mix = grad_mix.reshape(-1, heads_here, HEAD_DIM)
    grad_parts = []
    for index in range(seq_count):
        rows_here = packed[index * seq_length : (index + 1) * seq_length]
        grad_parts.append(
            attend_backward(
                rows_here[:, 0],
                rows_here[:, 1],
                rows_here[:, 2],
                segment_ids[index],
                log_parts[index],
                grad_mix[index * seq_length : (index + 1) * seq_length],
            )
        )
    grad_packed = jnp.concatenate(grad_parts, axis=0).reshape(-1, 3 * head_cols)
    grad_cols_one, grad_normed_one = back_up(grad_packed, qkv_block)
    grad_qkv = weight_grad(gathered_one, grad_cols_one).reshape(w_qkv.shape)
    grad_input_norm, grad_gain_one = norm_backward(
        grad_normed_one, unit_one, rescale_one, gain_attn
    )
    grad_tokens = grad_hidden + grad_input_norm
    summed = lax.psum((grad_qkv, grad_out_weight, grad_gate_up, grad_down), "dp")
    gains = lax.psum((grad_gain_one, grad_gain_two), ("dp", "row"))
    return (output, grad_tokens, gains[0], gains[1], summed[0], summed[1], summed[2], summed[3])


def swap(values):
    return lax.ppermute(values, "dp", [(0, 1), (1, 0)])


def hop(values, axis, flip):
    return lax.ppermute(values, axis, [(at, at ^ flip) for at in range(lax.axis_size(axis))])


def by_core(core, mine, other, axis=0):
    first = jnp.where(core == 0, mine, other)
    second = jnp.where(core == 0, other, mine)
    return jnp.concatenate([first, second], axis=axis)


def pick(values, core, axis=0):
    half = values.shape[axis] // 2
    return lax.dynamic_slice_in_dim(values, core * half, half, axis)


def to_sequence(values, core, col, seq_length):
    seqs = values.shape[0] // seq_length
    half = seq_length // 2
    parts = values.reshape(seqs, seq_length, -1)
    mine = pick(parts, core, 1)
    other = swap(pick(parts, 1 - core, 1))
    chunks = by_core(core, mine, other)
    got = []
    for flip in range(4):
        chunk = lax.dynamic_index_in_dim(chunks, col ^ flip, 0, keepdims=False)
        got.append(hop(chunk, "col", flip) if flip else chunk)
    rows = jnp.concatenate(got, axis=1)
    return by_core(core, rows, swap(rows))


def from_sequence(rows, core, col, seq_length):
    half = rows.shape[0]
    width = rows.shape[1] // 4
    got = []
    for flip in range(4):
        chunk = rows[:, flip * width : (flip + 1) * width]
        got.append(hop(chunk, "col", flip) if flip else chunk)
    got = jnp.stack(got, axis=0)
    seqs = 2
    mine = jnp.stack(
        [lax.dynamic_index_in_dim(got, (core * seqs + at) ^ col, 0, False) for at in range(seqs)]
    )
    other = jnp.stack(
        [
            lax.dynamic_index_in_dim(got, ((1 - core) * seqs + at) ^ col, 0, False)
            for at in range(seqs)
        ]
    )
    return by_core(core, mine, swap(other), 1).reshape(seqs * seq_length, -1)


def times(left, right):
    return jnp.dot(left, right, preferred_element_type=jnp.float32)


def times_t(left, right):
    return lax.dot_general(
        left, right, (((1,), (1,)), ((), ())), preferred_element_type=jnp.float32
    )


def norm_rows(values):
    rescale = lax.rsqrt(jnp.mean(values * values, axis=1) + EPS)[:, None]
    return (values * rescale, rescale)


def norm_rows_back(grad_normed, unit_rows, rescale, gain_vec):
    weighted = grad_normed * gain_vec[None, :]
    inner = jnp.sum(weighted * unit_rows, axis=1, keepdims=True) / D
    return rescale * (weighted - unit_rows * inner)


def join_blocks(*refs):
    blocks, whole = (refs[:16], refs[16])
    _, rows, width = blocks[0].shape
    for at, block in enumerate(blocks):
        line, place = divmod(at, 4)
        whole[:, line * rows : (line + 1) * rows, place * width : (place + 1) * width] = block[...]


def spread_weights(block):
    grid = [[None] * 4 for _ in range(4)]
    for at in range(4):
        own = hop(block, "col", at) if at else block
        grid[0][at] = own
        grid[1][at] = hop(own, "row", 1)
        grid[2][at] = hop(own, "row", 2)
    for at in range(4):
        if at < 2:
            grid[3][at] = hop(grid[1][at], "row", 2)
        else:
            grid[3][at] = hop(grid[2][at], "row", 1)
    return grid


def join_weights(grid):
    kinds, rows, width = grid[0][0].shape
    whole = pl.pallas_call(
        join_blocks, out_shape=jax.ShapeDtypeStruct((kinds, 4 * rows, 4 * width), jnp.bfloat16)
    )(*[block for line in grid for block in line])
    return whole.reshape(-1, 4 * width)


def after(values, first):
    return lax.optimization_barrier((values, first))[0]


def wide(values):
    return values.astype(jnp.float32)


def low(values):
    return values.astype(jnp.bfloat16)


def start_rows(grad, kinds):
    grid = low(grad).reshape(kinds, 2, 2, -1, grad.shape[1])
    half = grad.shape[1] // 2
    left, right = (grid[..., :half], grid[..., half:])
    got = hop(left[:, 1], "row", 2)
    got_r = hop(right[:, :, 1], "row", 1)
    return (left, right, got, got_r)


def middle_rows(state):
    left, right, got, got_r = state
    sent = low(wide(left[:, 0, 1]) + wide(got[:, 1]))
    sent_r = low(wide(right[:, 1, 0]) + wide(got_r[:, 1]))
    return ((sent, sent_r), state + (hop(sent, "row", 1), hop(sent_r, "row", 2)))


def end_rows(state):
    left, right, got, got_r, last, last_r = state
    sums = wide(left[:, 0, 0]) + wide(got[:, 0]) + wide(last)
    sums_r = wide(right[:, 0, 0]) + wide(got_r[:, 0]) + wide(last_r)
    return (sums, sums_r)


def end_cols(state):
    sums, sums_r = state
    width = sums.shape[-1] // 2
    parts = [sums[..., width:], sums_r[..., :width], sums_r[..., width:]]
    total = sums[..., :width]
    for flip in range(1, 4):
        total = total + wide(hop(low(parts[flip - 1]), "col", flip))
    return total


def start_cols(grad):
    width = grad.shape[1] // 4
    grid = [low(grad[:, at * width : (at + 1) * width]) for at in range(4)]
    return [grid[0]] + [hop(grid[flip], "col", flip) for flip in range(1, 4)]


def middle_cols(state):
    return wide(state[0]) + wide(state[1]) + wide(state[2]) + wide(state[3])


def join_halves(core_ref, mine, other, whole):
    rows = mine.shape[1]
    for at in range(2):
        part = slice(at * rows, (at + 1) * rows)

        @pl.when(core_ref[0] == at)
        def _():
            whole[:, part, :] = mine[...]

        @pl.when(core_ref[0] != at)
        def _():
            whole[:, part, :] = other[...].astype(jnp.float32)


def joined(mine, core):
    kinds, rows, width = mine.shape
    mine_low = low(mine)
    vmem = pl.BlockSpec(memory_space=pltpu.VMEM)
    return pl.pallas_call(
        join_halves,
        out_shape=jax.ShapeDtypeStruct((kinds, 2 * rows, width), jnp.float32),
        in_specs=[pl.BlockSpec(memory_space=pltpu.SMEM), vmem, vmem],
        out_specs=vmem,
    )(core[None], mine, swap(mine_low))


def chip_local(tokens, segment_ids, gain_attn, gain_ffn, w_qkv, w_out, w_gate_up, w_down, grad_out):
    core = lax.axis_index("dp")
    col = lax.axis_index("col")
    length = segment_ids.shape[1]
    features = w_qkv.shape[0]
    head_cols = w_qkv.shape[2] // 2
    heads = 4 * head_cols // HEAD_DIM
    factor = HEAD_DIM ** (-0.5)

    values = to_sequence(tokens, core, col, length).astype(jnp.float32)
    attn_block = jnp.concatenate(
        [pick(w_qkv, core, 2).transpose(1, 2, 0), pick(w_out, core)[None]], axis=0
    )
    attn_grid = spread_weights(attn_block)
    big_attn = join_weights(attn_grid)
    big_qkv, big_out = (big_attn[: 12 * head_cols], big_attn[12 * head_cols :])
    gains = jnp.stack([gain_attn, gain_ffn], axis=0)
    gains = jnp.concatenate([gains] + [hop(gains, "col", flip) for flip in range(1, 4)], axis=1)
    corner = [(4 * at + to, 4 * to + at) for at in range(4) for to in range(4)]
    segment_rows = lax.ppermute(segment_ids, ("row", "col"), corner)
    segment_rows = by_core(core, segment_rows, swap(segment_rows))
    segment = lax.dynamic_index_in_dim(segment_rows, col, 0, keepdims=False)
    ffn_block = jnp.concatenate(
        [pick(w_gate_up, core, 2).transpose(1, 2, 0), pick(w_down, core)[None]], axis=0
    )
    ffn_block = after(ffn_block, attn_grid[1] + attn_grid[2])
    ffn_grid = spread_weights(ffn_block)
    big_ffn = join_weights(ffn_grid)
    spread = big_ffn.shape[0] // 3
    big_gate_up, big_down = (big_ffn[: 2 * spread], big_ffn[2 * spread :])
    cotangent = to_sequence(after(grad_out, ffn_grid[0]), core, col, length)

    unit_one, rescale_one = norm_rows(values)
    normed_one = (unit_one * gains[0][None, :]).astype(jnp.bfloat16)
    packed = times_t(normed_one, big_qkv).astype(jnp.bfloat16).reshape(length, 3, heads, HEAD_DIM)
    queries, keys, vals = (packed[:, 0], packed[:, 1], packed[:, 2])
    scores = jnp.einsum("qhd,khd->hqk", queries, keys, preferred_element_type=jnp.float32) * factor
    spot = jnp.arange(length, dtype=jnp.int32)
    live = (segment[:, None] == segment[None, :]) & (spot[None, :] <= spot[:, None])
    scores = jnp.where(live[None], scores, MASKED)
    expo = jnp.exp(scores - jnp.max(scores, axis=-1, keepdims=True))
    prob = expo / jnp.sum(expo, axis=-1, keepdims=True)
    prob_low = prob.astype(jnp.bfloat16)
    mixed = jnp.einsum("hqk,khd->qhd", prob_low, vals, preferred_element_type=jnp.float32)
    mixed = mixed.reshape(length, -1).astype(jnp.bfloat16)
    branch = times(mixed, big_out)
    hidden_rows = values + (branch + swap(branch))
    unit_two, rescale_two = norm_rows(hidden_rows)
    normed_two = (unit_two * gains[1][None, :]).astype(jnp.bfloat16)
    gate_up = times_t(normed_two, big_gate_up).astype(jnp.bfloat16)
    half = gate_up.shape[1] // 2
    gate_vals = gate_up[:, :half].astype(jnp.float32)
    up_vals = gate_up[:, half:].astype(jnp.float32)
    sigmoid_gate = jax.nn.sigmoid(gate_vals)
    silu_gate = gate_vals * sigmoid_gate
    active = (silu_gate * up_vals).astype(jnp.bfloat16)

    down_state = start_cols(weight_grad(active, cotangent))
    grad_act = wide(low(times_t(cotangent, big_down)))
    grad_gate = grad_act * up_vals * sigmoid_gate * (1.0 + gate_vals * (1.0 - sigmoid_gate))
    grad_up = grad_act * silu_gate
    grad_gu = jnp.concatenate([grad_gate, grad_up], axis=1).astype(jnp.bfloat16)
    grad_two = times(grad_gu, big_gate_up)
    grad_two = grad_two + swap(grad_two)
    gate_up_state = start_rows(weight_grad(grad_gu, normed_two), 2)
    back_two = norm_rows_back(grad_two, unit_two, rescale_two, gains[1])
    gain_two = jnp.sum(pick(grad_two * unit_two, core), axis=0)
    grad_hidden = cotangent.astype(jnp.float32) + back_two
    grad_branch = grad_hidden.astype(jnp.bfloat16)
    grad_w_out = low(weight_grad(mixed, grad_branch))
    grad_mix = times_t(grad_branch, big_out).astype(jnp.bfloat16).reshape(length, heads, HEAD_DIM)
    grad_vals = jnp.einsum("hqk,qhd->khd", prob_low, grad_mix, preferred_element_type=jnp.float32)
    grad_prob = jnp.einsum("qhd,khd->hqk", grad_mix, vals, preferred_element_type=jnp.float32)
    inner = jnp.sum(prob * grad_prob, axis=-1, keepdims=True)
    grad_scores = (prob * (grad_prob - inner)).astype(jnp.bfloat16)
    grad_queries = factor * jnp.einsum(
        "hqk,khd->qhd", grad_scores, keys, preferred_element_type=jnp.float32
    )
    grad_keys = factor * jnp.einsum(
        "hqk,qhd->khd", grad_scores, queries, preferred_element_type=jnp.float32
    )
    grad_packed = jnp.stack([grad_queries, grad_keys, grad_vals], axis=1)
    grad_packed = grad_packed.astype(jnp.bfloat16).reshape(length, -1)
    grad_attn = jnp.concatenate([low(weight_grad(grad_packed, normed_one)), grad_w_out], axis=0)

    attn_state = start_rows(grad_attn, 4)
    gate_up_state = after(gate_up_state, grad_attn)
    active = after(active, grad_attn)
    sent, gate_up_state = middle_rows(gate_up_state)
    down_state = after(down_state, sent)
    grad_one = times(grad_packed, big_qkv)
    grad_one = pick(grad_one, core) + swap(pick(grad_one, 1 - core))
    ffn = times(active, big_down)
    ffn_mine = pick(ffn, core) + swap(pick(ffn, 1 - core))
    output = (pick(hidden_rows, core) + ffn_mine).astype(jnp.bfloat16)
    output = from_sequence(output, core, col, length)
    down_rows = middle_cols(down_state)
    _, down_state = middle_rows(start_rows(down_rows, 1))
    gate_up_mine = end_rows(gate_up_state)
    unit_mine = pick(unit_one, core)
    back_one = norm_rows_back(grad_one, unit_mine, pick(rescale_one, core), gains[0])
    gain_one = jnp.sum(grad_one * unit_mine, axis=0)
    grad_rows = (pick(grad_hidden, core) + back_one).astype(jnp.bfloat16)
    _, attn_state = middle_rows(attn_state)
    attn_mine = end_rows(attn_state)
    gain_sums = jnp.stack([gain_one, gain_two], axis=0)
    gain_sums, grad_rows = after((gain_sums, grad_rows), attn_mine)
    mine_gate_up = end_cols(gate_up_mine)
    mine_attn = end_cols(attn_mine)
    down_left, down_right = end_rows(down_state)
    mine_down = jnp.concatenate([down_left, down_right], axis=-1)
    grad_tokens = from_sequence(grad_rows, core, col, length).astype(jnp.float32)

    gain_sums = gain_sums + swap(gain_sums)
    gain_sums = gain_sums + hop(gain_sums, "row", 1)
    gain_sums = gain_sums + hop(gain_sums, "row", 2)
    gain_mine = gain_sums[:, :features]
    for flip in range(1, 4):
        piece = gain_sums[:, flip * features : (flip + 1) * features]
        gain_mine = gain_mine + hop(piece, "col", flip)

    whole_attn = joined(mine_attn, core)
    return (
        output,
        grad_tokens,
        gain_mine[0],
        gain_mine[1],
        whole_attn[:3].transpose(2, 0, 1),
        whole_attn[3],
        joined(mine_gate_up, core).transpose(2, 0, 1),
        joined(mine_down, core)[0],
    )


def layer(tokens, segment_ids, *rest):
    sizes = (lax.axis_size("dp"), lax.axis_size("row"), lax.axis_size("col"))
    if sizes == (2, 4, 4) and tokens.shape[0] == 2 * segment_ids.shape[1]:
        return chip_local(tokens, segment_ids, *rest)
    return local(tokens, segment_ids, *rest)


def solution(mesh):
    in_specs = (
        P(("dp", "row"), "col"),
        P(("dp", "col"), None),
        P("col"),
        P("col"),
        P("col", None, "row"),
        P("row", "col"),
        P("col", None, "row"),
        P("row", "col"),
        P(("dp", "row"), "col"),
    )
    out_specs = (
        P(("dp", "row"), "col"),
        P(("dp", "row"), "col"),
        P("col"),
        P("col"),
        P("col", None, "row"),
        P("row", "col"),
        P("col", None, "row"),
        P("row", "col"),
    )
    return jax.shard_map(layer, mesh=mesh, in_specs=in_specs, out_specs=out_specs, check_vma=False)
```

```python
import jax
import jax.numpy as jnp
from jax import lax
from jax.experimental import pallas as pl
from jax.experimental.pallas import tpu as pltpu
from jax.sharding import PartitionSpec as P

D = 1024
HEAD_DIM = 64


EPS = 1e-06
MASKED = -1e30


def row_norm(values, gain_vec):
    squares = lax.psum(jnp.sum(values * values, axis=1), "col")
    rescale = lax.rsqrt(squares / D + EPS)
    unit_rows = values * rescale[:, None]
    return (unit_rows, rescale, (unit_rows * gain_vec[None, :]).astype(jnp.bfloat16))


def norm_backward(grad_normed, unit_rows, rescale, gain_vec):
    weighted = grad_normed * gain_vec[None, :]
    inner_sum = lax.psum(jnp.sum(weighted * unit_rows, axis=1), "col")
    grad_in = rescale[:, None] * (weighted - unit_rows * (inner_sum / D)[:, None])
    grad_gain = jnp.sum(grad_normed * unit_rows, axis=0)
    return (grad_in, grad_gain)


def project_up(normed, weight_block):
    gathered = lax.all_gather(normed, "row", axis=0, tiled=True)

    def term(begin_at, row_count):
        return jnp.dot(gathered, weight_block, preferred_element_type=jnp.float32)

    result = lax.psum_scatter(
        term(jnp.int32(0), gathered.shape[0] // lax.axis_size("col") * lax.axis_size("col")),
        "col",
        scatter_dimension=0,
        tiled=True,
    )
    return (gathered, result.astype(jnp.bfloat16))


def project_down(values, weight_block):
    gathered = lax.all_gather(values, "col", axis=0, tiled=True)

    def term(begin_at, row_count):
        return jnp.dot(gathered, weight_block, preferred_element_type=jnp.float32)

    result = lax.psum_scatter(
        term(jnp.int32(0), gathered.shape[0] // lax.axis_size("row") * lax.axis_size("row")),
        "row",
        scatter_dimension=0,
        tiled=True,
    )
    return (gathered, result)


def back_down(grad_rows, weight_block):
    gathered = lax.all_gather(grad_rows, "row", axis=0, tiled=True)

    def term(begin_at, row_count):
        return lax.dot_general(
            gathered, weight_block, (((1,), (1,)), ((), ())), preferred_element_type=jnp.float32
        )

    result = lax.psum_scatter(
        term(jnp.int32(0), gathered.shape[0] // lax.axis_size("col") * lax.axis_size("col")),
        "col",
        scatter_dimension=0,
        tiled=True,
    )
    return (gathered, result.astype(jnp.bfloat16))


def back_up(grad_cols, weight_block):
    gathered = lax.all_gather(grad_cols, "col", axis=0, tiled=True)

    def term(begin_at, row_count):
        return lax.dot_general(
            gathered, weight_block, (((1,), (1,)), ((), ())), preferred_element_type=jnp.float32
        )

    result = lax.psum_scatter(
        term(jnp.int32(0), gathered.shape[0] // lax.axis_size("row") * lax.axis_size("row")),
        "row",
        scatter_dimension=0,
        tiled=True,
    )
    return (gathered, result)


def weight_grad(left_rows, right_rows):
    return lax.dot_general(
        left_rows, right_rows, (((0,), (0,)), ((), ())), preferred_element_type=jnp.float32
    )


def block_scores(queries, keys_all, query_segment, key_segment, query_place):
    raw = jnp.einsum(
        "qhd,khd->hqk", queries, keys_all, preferred_element_type=jnp.float32
    ) * HEAD_DIM ** (-0.5)
    key_place = lax.broadcasted_iota(jnp.int32, (1, keys_all.shape[0]), 1)
    allowed = (query_segment[:, None] == key_segment[None, :]) & (key_place <= query_place[:, None])
    return jnp.where(allowed[None], raw, MASKED)


def split_blocks(queries, segment):
    length = queries.shape[0]
    block_rows = min(512, length)
    blocks = length // block_rows
    place = jnp.arange(length, dtype=jnp.int32).reshape(blocks, block_rows)
    return (
        queries.reshape(blocks, block_rows, queries.shape[1], queries.shape[2]),
        segment.reshape(blocks, block_rows),
        place,
    )


def attend_forward(queries, keys_all, values_all, segment):
    query_blocks, segment_blocks, place_blocks = split_blocks(queries, segment)

    def one_block(item):
        query_rows, query_segment, query_place = item
        scores = block_scores(query_rows, keys_all, query_segment, segment, query_place)
        row_max = jnp.max(scores, axis=-1, keepdims=True)
        expo = jnp.exp(scores - row_max)
        row_total = jnp.sum(expo, axis=-1, keepdims=True)
        prob_rows = (expo / row_total).astype(jnp.bfloat16)
        mixed = jnp.einsum(
            "hqk,khd->qhd", prob_rows, values_all, preferred_element_type=jnp.float32
        )
        return (mixed, row_max[..., 0] + jnp.log(row_total[..., 0]))

    mixed, log_total = lax.map(one_block, (query_blocks, segment_blocks, place_blocks))
    return (mixed.reshape(queries.shape[0], -1).astype(jnp.bfloat16), log_total)


def attend_backward(queries, keys_all, values_all, segment, log_total, grad_mix):
    query_blocks, segment_blocks, place_blocks = split_blocks(queries, segment)
    grad_blocks = grad_mix.reshape(query_blocks.shape)
    factor = HEAD_DIM ** (-0.5)

    def one_block(carry, item):
        key_acc, value_acc = carry
        query_rows, query_segment, query_place, log_rows, grad_rows = item
        scores = block_scores(query_rows, keys_all, query_segment, segment, query_place)
        prob_rows = jnp.exp(scores - log_rows[..., None])
        value_acc = value_acc + jnp.einsum(
            "hqk,qhd->khd",
            prob_rows.astype(jnp.bfloat16),
            grad_rows,
            preferred_element_type=jnp.float32,
        )
        grad_prob = jnp.einsum(
            "qhd,khd->hqk", grad_rows, values_all, preferred_element_type=jnp.float32
        )
        grad_scores = (
            prob_rows * (grad_prob - jnp.sum(prob_rows * grad_prob, axis=-1, keepdims=True))
        ).astype(jnp.bfloat16)
        grad_query = (
            jnp.einsum("hqk,khd->qhd", grad_scores, keys_all, preferred_element_type=jnp.float32)
            * factor
        )
        key_acc = (
            key_acc
            + jnp.einsum(
                "hqk,qhd->khd", grad_scores, query_rows, preferred_element_type=jnp.float32
            )
            * factor
        )
        return ((key_acc, value_acc), grad_query)

    zeros_like_keys = jnp.zeros(keys_all.shape, jnp.float32)
    (grad_keys, grad_values), grad_queries = lax.scan(
        one_block,
        (zeros_like_keys, zeros_like_keys),
        (query_blocks, segment_blocks, place_blocks, log_total, grad_blocks),
    )
    grad_queries = grad_queries.reshape(queries.shape)
    return jnp.stack([grad_queries, grad_keys, grad_values], axis=1).astype(jnp.bfloat16)


def local(tokens, segment_ids, gain_attn, gain_ffn, w_qkv, w_out, w_gate_up, w_down, grad_out):
    values = tokens.astype(jnp.float32)
    head_cols = w_qkv.shape[2]
    heads_here = head_cols // HEAD_DIM
    hidden_here = w_gate_up.shape[2]
    qkv_block = w_qkv.reshape(w_qkv.shape[0], 3 * head_cols)
    gate_up_block = w_gate_up.reshape(w_gate_up.shape[0], 2 * hidden_here)
    seq_count, seq_length = segment_ids.shape
    unit_one, rescale_one, normed_one = row_norm(values, gain_attn)
    gathered_one, packed = project_up(normed_one, qkv_block)
    packed = packed.reshape(-1, 3, heads_here, HEAD_DIM)
    mix_parts, log_parts = ([], [])
    for index in range(seq_count):
        rows_here = packed[index * seq_length : (index + 1) * seq_length]
        mixed, log_total = attend_forward(
            rows_here[:, 0], rows_here[:, 1], rows_here[:, 2], segment_ids[index]
        )
        mix_parts.append(mixed)
        log_parts.append(log_total)
    attn_mix = jnp.concatenate(mix_parts, axis=0)
    gathered_mix, attn_branch = project_down(attn_mix, w_out)
    hidden = values + attn_branch
    unit_two, rescale_two, normed_two = row_norm(hidden, gain_ffn)
    gathered_two, gate_up = project_up(normed_two, gate_up_block)
    gate_vals = gate_up[:, :hidden_here].astype(jnp.float32)
    up_vals = gate_up[:, hidden_here:].astype(jnp.float32)
    sigmoid_gate = jax.nn.sigmoid(gate_vals)
    silu_gate = gate_vals * sigmoid_gate
    active = (silu_gate * up_vals).astype(jnp.bfloat16)
    gathered_act, ffn_branch = project_down(active, w_down)
    output = (hidden + ffn_branch).astype(jnp.bfloat16)
    grad_rows_out, grad_active = back_down(grad_out, w_down)
    grad_down = weight_grad(gathered_act, grad_rows_out)
    grad_act_f = grad_active.astype(jnp.float32)
    grad_gate = grad_act_f * up_vals * sigmoid_gate * (1.0 + gate_vals * (1.0 - sigmoid_gate))
    grad_up = grad_act_f * silu_gate
    grad_gate_up_rows = jnp.concatenate([grad_gate, grad_up], axis=1).astype(jnp.bfloat16)
    grad_cols_two, grad_normed_two = back_up(grad_gate_up_rows, gate_up_block)
    grad_gate_up = weight_grad(gathered_two, grad_cols_two).reshape(w_gate_up.shape)
    grad_hidden_norm, grad_gain_two = norm_backward(
        grad_normed_two, unit_two, rescale_two, gain_ffn
    )
    grad_hidden = grad_out.astype(jnp.float32) + grad_hidden_norm
    grad_rows_hidden, grad_mix = back_down(grad_hidden.astype(jnp.bfloat16), w_out)
    grad_out_weight = weight_grad(gathered_mix, grad_rows_hidden)
    grad_mix = grad_mix.reshape(-1, heads_here, HEAD_DIM)
    grad_parts = []
    for index in range(seq_count):
        rows_here = packed[index * seq_length : (index + 1) * seq_length]
        grad_parts.append(
            attend_backward(
                rows_here[:, 0],
                rows_here[:, 1],
                rows_here[:, 2],
                segment_ids[index],
                log_parts[index],
                grad_mix[index * seq_length : (index + 1) * seq_length],
            )
        )
    grad_packed = jnp.concatenate(grad_parts, axis=0).reshape(-1, 3 * head_cols)
    grad_cols_one, grad_normed_one = back_up(grad_packed, qkv_block)
    grad_qkv = weight_grad(gathered_one, grad_cols_one).reshape(w_qkv.shape)
    grad_input_norm, grad_gain_one = norm_backward(
        grad_normed_one, unit_one, rescale_one, gain_attn
    )
    grad_tokens = grad_hidden + grad_input_norm
    summed = lax.psum((grad_qkv, grad_out_weight, grad_gate_up, grad_down), "dp")
    gains = lax.psum((grad_gain_one, grad_gain_two), ("dp", "row"))
    return (output, grad_tokens, gains[0], gains[1], summed[0], summed[1], summed[2], summed[3])


def swap(values):
    return lax.ppermute(values, "dp", [(0, 1), (1, 0)])


def hop(values, axis, flip):
    return lax.ppermute(values, axis, [(at, at ^ flip) for at in range(lax.axis_size(axis))])


def after(values, first):
    return lax.optimization_barrier((values, first))[0]


def by_core(core, mine, other, axis=0):
    first = jnp.where(core == 0, mine, other)
    second = jnp.where(core == 0, other, mine)
    return jnp.concatenate([first, second], axis=axis)


def pick(values, core, axis=0):
    half = values.shape[axis] // 2
    return lax.dynamic_slice_in_dim(values, core * half, half, axis)


def to_sequence(values, core, col, seq_length):
    seqs = values.shape[0] // seq_length
    half = seq_length // 2
    parts = values.reshape(seqs, seq_length, -1)
    mine = pick(parts, core, 1)
    other = swap(pick(parts, 1 - core, 1))
    chunks = by_core(core, mine, other)
    got = []
    for flip in range(4):
        chunk = lax.dynamic_index_in_dim(chunks, col ^ flip, 0, keepdims=False)
        got.append(hop(chunk, "col", flip) if flip else chunk)
    rows = jnp.concatenate(got, axis=1)
    return by_core(core, rows, swap(rows))


def from_sequence(rows, core, col, seq_length):
    half = rows.shape[0]
    width = rows.shape[1] // 4
    got = []
    for flip in range(4):
        chunk = rows[:, flip * width : (flip + 1) * width]
        got.append(hop(chunk, "col", flip) if flip else chunk)
    got = jnp.stack(got, axis=0)
    seqs = 2
    mine = jnp.stack(
        [lax.dynamic_index_in_dim(got, (core * seqs + at) ^ col, 0, False) for at in range(seqs)]
    )
    other = jnp.stack(
        [
            lax.dynamic_index_in_dim(got, ((1 - core) * seqs + at) ^ col, 0, False)
            for at in range(seqs)
        ]
    )
    return by_core(core, mine, swap(other), 1).reshape(seqs * seq_length, -1)


def times(left, right):
    return jnp.dot(left, right, preferred_element_type=jnp.float32)


def times_t(left, right):
    return lax.dot_general(
        left, right, (((1,), (1,)), ((), ())), preferred_element_type=jnp.float32
    )


def norm_rows(values):
    rescale = lax.rsqrt(jnp.mean(values * values, axis=1) + EPS)[:, None]
    return (values * rescale, rescale)


def norm_rows_back(grad_normed, unit_rows, rescale, gain_vec):
    weighted = grad_normed * gain_vec[None, :]
    inner = jnp.sum(weighted * unit_rows, axis=1, keepdims=True) / D
    return rescale * (weighted - unit_rows * inner)


def join_blocks(*refs):
    blocks, whole = (refs[:16], refs[16])
    _, rows, width = blocks[0].shape
    for at, block in enumerate(blocks):
        line, place = divmod(at, 4)
        whole[:, line * rows : (line + 1) * rows, place * width : (place + 1) * width] = block[...]


def spread_weights(block, first_cols=None, first_rows=None):
    grid = [[None] * 4 for _ in range(4)]
    block_cols = block if first_cols is None else after(block, first_cols)
    block_rows = block if first_rows is None else after(block, first_rows)
    near = hop(block_cols, "col", 1)
    far = hop(block_cols, "col", 3)
    grid[0] = [block_rows, near, hop(near, "col", 3), far]
    for at in (0, 1, 3, 2):
        grid[1][at] = hop(grid[0][at], "row", 1)
        grid[2][at] = hop(grid[0][at], "row", 2)
    for at in range(4):
        if at < 2:
            grid[3][at] = hop(grid[1][at], "row", 2)
        else:
            grid[3][at] = hop(grid[2][at], "row", 1)
    return grid


def join_weights(grid):
    kinds, rows, width = grid[0][0].shape
    whole = pl.pallas_call(
        join_blocks, out_shape=jax.ShapeDtypeStruct((kinds, 4 * rows, 4 * width), jnp.bfloat16)
    )(*[block for line in grid for block in line])
    return whole.reshape(-1, 4 * width)


def wide(values):
    return values.astype(jnp.float32)


def low(values):
    return values.astype(jnp.bfloat16)


def start_rows(grad, kinds):
    grid = low(grad).reshape(kinds, 2, 2, -1, grad.shape[1])
    half = grad.shape[1] // 2
    left, right = (grid[..., :half], grid[..., half:])
    got = hop(left[:, 1], "row", 2)
    got_r = hop(right[:, :, 1], "row", 1)
    return (left, right, got, got_r)


def middle_rows(state):
    left, right, got, got_r = state
    sent = low(wide(left[:, 0, 1]) + wide(got[:, 1]))
    sent_r = low(wide(right[:, 1, 0]) + wide(got_r[:, 1]))
    return ((sent, sent_r), state + (hop(sent, "row", 1), hop(sent_r, "row", 2)))


def end_rows(state):
    left, right, got, got_r, last, last_r = state
    sums = wide(left[:, 0, 0]) + wide(got[:, 0]) + wide(last)
    sums_r = wide(right[:, 0, 0]) + wide(got_r[:, 0]) + wide(last_r)
    return (sums, sums_r)


def start_end_cols(state):
    sums, sums_r = state
    width = sums.shape[-1] // 2
    parts = [low(sums[..., width:]), low(sums_r[..., :width]), low(sums_r[..., width:])]
    return (parts, sums[..., :width], [hop(parts[flip - 1], "col", flip) for flip in (1, 2, 3)])


def end_cols(total, got):
    return total + wide(got[0]) + wide(got[1]) + wide(got[2])


def start_cols(grad):
    width = grad.shape[1] // 4
    grid = [low(grad[:, at * width : (at + 1) * width]) for at in range(4)]
    return [grid[0]] + [hop(grid[flip], "col", flip) for flip in range(1, 4)]


def middle_cols(state):
    return wide(state[0]) + wide(state[1]) + wide(state[2]) + wide(state[3])


def join_halves(core_ref, mine, other, whole):
    rows = mine.shape[1]
    for at in range(2):
        part = slice(at * rows, (at + 1) * rows)

        @pl.when(core_ref[0] == at)
        def _():
            whole[:, part, :] = mine[...]

        @pl.when(core_ref[0] != at)
        def _():
            whole[:, part, :] = other[...].astype(jnp.float32)


def joined(mine, core):
    kinds, rows, width = mine.shape
    mine_low = low(mine)
    vmem = pl.BlockSpec(memory_space=pltpu.VMEM)
    return pl.pallas_call(
        join_halves,
        out_shape=jax.ShapeDtypeStruct((kinds, 2 * rows, width), jnp.float32),
        in_specs=[pl.BlockSpec(memory_space=pltpu.SMEM), vmem, vmem],
        out_specs=vmem,
    )(core[None], mine, swap(mine_low))


def chip_local(tokens, segment_ids, gain_attn, gain_ffn, w_qkv, w_out, w_gate_up, w_down, grad_out):
    core = lax.axis_index("dp")
    col = lax.axis_index("col")
    length = segment_ids.shape[1]
    features = w_qkv.shape[0]
    head_cols = w_qkv.shape[2] // 2
    heads = 4 * head_cols // HEAD_DIM
    factor = HEAD_DIM ** (-0.5)

    values = to_sequence(tokens, core, col, length).astype(jnp.float32)
    attn_block = jnp.concatenate(
        [pick(w_qkv, core, 2).transpose(1, 2, 0), pick(w_out, core)[None]], axis=0
    )
    attn_grid = spread_weights(attn_block)
    big_attn = join_weights(attn_grid)
    big_qkv, big_out = (big_attn[: 12 * head_cols], big_attn[12 * head_cols :])
    gains = jnp.stack([gain_attn, gain_ffn], axis=0)
    gains = jnp.concatenate([gains] + [hop(gains, "col", flip) for flip in range(1, 4)], axis=1)
    corner = [(4 * at + to, 4 * to + at) for at in range(4) for to in range(4)]
    segment_rows = lax.ppermute(segment_ids, ("row", "col"), corner)
    segment_rows = by_core(core, segment_rows, swap(segment_rows))
    segment = lax.dynamic_index_in_dim(segment_rows, col, 0, keepdims=False)
    ffn_block = jnp.concatenate(
        [pick(w_gate_up, core, 2).transpose(1, 2, 0), pick(w_down, core)[None]], axis=0
    )
    ffn_grid = spread_weights(ffn_block, attn_grid[0], attn_grid[1] + attn_grid[2])
    big_ffn = join_weights(ffn_grid)
    spread = big_ffn.shape[0] // 3
    big_gate_up, big_down = (big_ffn[: 2 * spread], big_ffn[2 * spread :])
    cotangent = to_sequence(after(grad_out, ffn_grid[1] + ffn_grid[2]), core, col, length)

    unit_one, rescale_one = norm_rows(values)
    normed_one = (unit_one * gains[0][None, :]).astype(jnp.bfloat16)
    packed = times_t(normed_one, big_qkv).astype(jnp.bfloat16).reshape(length, 3, heads, HEAD_DIM)
    queries, keys, vals = (packed[:, 0], packed[:, 1], packed[:, 2])
    scores = jnp.einsum("qhd,khd->hqk", queries, keys, preferred_element_type=jnp.float32) * factor
    spot = jnp.arange(length, dtype=jnp.int32)
    live = (segment[:, None] == segment[None, :]) & (spot[None, :] <= spot[:, None])
    scores = jnp.where(live[None], scores, MASKED)
    expo = jnp.exp(scores - jnp.max(scores, axis=-1, keepdims=True))
    prob = expo / jnp.sum(expo, axis=-1, keepdims=True)
    prob_low = prob.astype(jnp.bfloat16)
    mixed = jnp.einsum("hqk,khd->qhd", prob_low, vals, preferred_element_type=jnp.float32)
    mixed = mixed.reshape(length, -1).astype(jnp.bfloat16)
    branch = times(mixed, big_out)
    hidden_rows = values + (branch + swap(branch))
    unit_two, rescale_two = norm_rows(hidden_rows)
    normed_two = (unit_two * gains[1][None, :]).astype(jnp.bfloat16)
    gate_up = times_t(normed_two, big_gate_up).astype(jnp.bfloat16)
    half = gate_up.shape[1] // 2
    gate_vals = gate_up[:, :half].astype(jnp.float32)
    up_vals = gate_up[:, half:].astype(jnp.float32)
    sigmoid_gate = jax.nn.sigmoid(gate_vals)
    silu_gate = gate_vals * sigmoid_gate
    active = (silu_gate * up_vals).astype(jnp.bfloat16)

    down_state = start_cols(weight_grad(active, cotangent))
    grad_act = wide(low(times_t(cotangent, big_down)))
    grad_gate = grad_act * up_vals * sigmoid_gate * (1.0 + gate_vals * (1.0 - sigmoid_gate))
    grad_up = grad_act * silu_gate
    grad_gu = jnp.concatenate([grad_gate, grad_up], axis=1).astype(jnp.bfloat16)
    grad_two = times(grad_gu, big_gate_up)
    grad_two = grad_two + swap(grad_two)
    gate_up_state = start_rows(weight_grad(grad_gu, normed_two), 2)
    back_two = norm_rows_back(grad_two, unit_two, rescale_two, gains[1])
    gain_two = jnp.sum(pick(grad_two * unit_two, core), axis=0)
    grad_hidden = cotangent.astype(jnp.float32) + back_two
    grad_branch = grad_hidden.astype(jnp.bfloat16)
    grad_w_out = low(weight_grad(mixed, grad_branch))
    grad_mix = times_t(grad_branch, big_out).astype(jnp.bfloat16).reshape(length, heads, HEAD_DIM)
    grad_vals = jnp.einsum("hqk,qhd->khd", prob_low, grad_mix, preferred_element_type=jnp.float32)
    grad_prob = jnp.einsum("qhd,khd->hqk", grad_mix, vals, preferred_element_type=jnp.float32)
    inner = jnp.sum(prob * grad_prob, axis=-1, keepdims=True)
    grad_scores = (prob * (grad_prob - inner)).astype(jnp.bfloat16)
    grad_queries = factor * jnp.einsum(
        "hqk,khd->qhd", grad_scores, keys, preferred_element_type=jnp.float32
    )
    grad_keys = factor * jnp.einsum(
        "hqk,qhd->khd", grad_scores, queries, preferred_element_type=jnp.float32
    )
    grad_packed = jnp.stack([grad_queries, grad_keys, grad_vals], axis=1)
    grad_packed = grad_packed.astype(jnp.bfloat16).reshape(length, -1)
    grad_attn = jnp.concatenate([low(weight_grad(grad_packed, normed_one)), grad_w_out], axis=0)

    gate_up_sent, gate_up_state = middle_rows(after(gate_up_state, grad_attn))
    grad_attn = after(grad_attn, gate_up_sent)
    attn_state = start_rows(grad_attn, 4)
    active = after(active, grad_attn)
    grad_packed = after(grad_packed, grad_attn)
    grad_one = times(grad_packed, big_qkv)
    grad_one = pick(grad_one, core) + swap(pick(grad_one, 1 - core))
    ffn = times(active, big_down)
    ffn_mine = pick(ffn, core) + swap(pick(ffn, 1 - core))
    output = (pick(hidden_rows, core) + ffn_mine).astype(jnp.bfloat16)
    unit_mine = pick(unit_one, core)
    back_one = norm_rows_back(grad_one, unit_mine, pick(rescale_one, core), gains[0])
    gain_one = jnp.sum(grad_one * unit_mine, axis=0)
    grad_rows = (pick(grad_hidden, core) + back_one).astype(jnp.bfloat16)

    gate_up_state = after(gate_up_state, (output, grad_rows))
    parts, gate_up_own, gate_up_got = start_end_cols(end_rows(gate_up_state))
    output = from_sequence(after(output, parts), core, col, length)
    down_rows = middle_cols(after(down_state, parts))
    down_state = start_rows(down_rows, 1)
    attn_sent, attn_state = middle_rows(after(attn_state, down_rows))
    down_sent, down_state = middle_rows(after(down_state, attn_sent))
    attn_parts, attn_own, attn_got = start_end_cols(end_rows(after(attn_state, down_sent)))
    gain_sums = jnp.stack([gain_one, gain_two], axis=0)
    gain_sums, grad_rows = after((gain_sums, grad_rows), attn_parts)
    grad_tokens = from_sequence(grad_rows, core, col, length).astype(jnp.float32)
    gate_up_got, down_state = after((gate_up_got, down_state), attn_parts)
    mine_gate_up = end_cols(gate_up_own, gate_up_got)
    mine_down = jnp.concatenate(end_rows(down_state), axis=-1)
    mine_attn = end_cols(attn_own, attn_got)

    gain_sums = gain_sums + swap(gain_sums)
    gain_sums = gain_sums + hop(gain_sums, "row", 1)
    gain_sums = gain_sums + hop(gain_sums, "row", 2)
    gain_mine = gain_sums[:, :features]
    for flip in range(1, 4):
        piece = gain_sums[:, flip * features : (flip + 1) * features]
        gain_mine = gain_mine + hop(piece, "col", flip)

    whole_attn = joined(mine_attn, core)
    return (
        output,
        grad_tokens,
        gain_mine[0],
        gain_mine[1],
        whole_attn[:3].transpose(2, 0, 1),
        whole_attn[3],
        joined(mine_gate_up, core).transpose(2, 0, 1),
        joined(mine_down, core)[0],
    )


def layer(tokens, segment_ids, *rest):
    sizes = (lax.axis_size("dp"), lax.axis_size("row"), lax.axis_size("col"))
    if sizes == (2, 4, 4) and tokens.shape[0] == 2 * segment_ids.shape[1]:
        return chip_local(tokens, segment_ids, *rest)
    return local(tokens, segment_ids, *rest)


def solution(mesh):
    in_specs = (
        P(("dp", "row"), "col"),
        P(("dp", "col"), None),
        P("col"),
        P("col"),
        P("col", None, "row"),
        P("row", "col"),
        P("col", None, "row"),
        P("row", "col"),
        P(("dp", "row"), "col"),
    )
    out_specs = (
        P(("dp", "row"), "col"),
        P(("dp", "row"), "col"),
        P("col"),
        P("col"),
        P("col", None, "row"),
        P("row", "col"),
        P("col", None, "row"),
        P("row", "col"),
    )
    return jax.shard_map(layer, mesh=mesh, in_specs=in_specs, out_specs=out_specs, check_vma=False)
```

```python
import jax
import jax.numpy as jnp
from jax import lax
from jax.experimental import pallas as pl
from jax.experimental.pallas import tpu as pltpu
from jax.sharding import PartitionSpec as P

D = 1024
HEAD_DIM = 64


EPS = 1e-06
MASKED = -1e30


def row_norm(values, gain_vec):
    squares = lax.psum(jnp.sum(values * values, axis=1), "col")
    rescale = lax.rsqrt(squares / D + EPS)
    unit_rows = values * rescale[:, None]
    return (unit_rows, rescale, (unit_rows * gain_vec[None, :]).astype(jnp.bfloat16))


def norm_backward(grad_normed, unit_rows, rescale, gain_vec):
    weighted = grad_normed * gain_vec[None, :]
    inner_sum = lax.psum(jnp.sum(weighted * unit_rows, axis=1), "col")
    grad_in = rescale[:, None] * (weighted - unit_rows * (inner_sum / D)[:, None])
    grad_gain = jnp.sum(grad_normed * unit_rows, axis=0)
    return (grad_in, grad_gain)


def project_up(normed, weight_block):
    gathered = lax.all_gather(normed, "row", axis=0, tiled=True)

    def term(begin_at, row_count):
        return jnp.dot(gathered, weight_block, preferred_element_type=jnp.float32)

    result = lax.psum_scatter(
        term(jnp.int32(0), gathered.shape[0] // lax.axis_size("col") * lax.axis_size("col")),
        "col",
        scatter_dimension=0,
        tiled=True,
    )
    return (gathered, result.astype(jnp.bfloat16))


def project_down(values, weight_block):
    gathered = lax.all_gather(values, "col", axis=0, tiled=True)

    def term(begin_at, row_count):
        return jnp.dot(gathered, weight_block, preferred_element_type=jnp.float32)

    result = lax.psum_scatter(
        term(jnp.int32(0), gathered.shape[0] // lax.axis_size("row") * lax.axis_size("row")),
        "row",
        scatter_dimension=0,
        tiled=True,
    )
    return (gathered, result)


def back_down(grad_rows, weight_block):
    gathered = lax.all_gather(grad_rows, "row", axis=0, tiled=True)

    def term(begin_at, row_count):
        return lax.dot_general(
            gathered, weight_block, (((1,), (1,)), ((), ())), preferred_element_type=jnp.float32
        )

    result = lax.psum_scatter(
        term(jnp.int32(0), gathered.shape[0] // lax.axis_size("col") * lax.axis_size("col")),
        "col",
        scatter_dimension=0,
        tiled=True,
    )
    return (gathered, result.astype(jnp.bfloat16))


def back_up(grad_cols, weight_block):
    gathered = lax.all_gather(grad_cols, "col", axis=0, tiled=True)

    def term(begin_at, row_count):
        return lax.dot_general(
            gathered, weight_block, (((1,), (1,)), ((), ())), preferred_element_type=jnp.float32
        )

    result = lax.psum_scatter(
        term(jnp.int32(0), gathered.shape[0] // lax.axis_size("row") * lax.axis_size("row")),
        "row",
        scatter_dimension=0,
        tiled=True,
    )
    return (gathered, result)


def weight_grad(left_rows, right_rows):
    return lax.dot_general(
        left_rows, right_rows, (((0,), (0,)), ((), ())), preferred_element_type=jnp.float32
    )


def block_scores(queries, keys_all, query_segment, key_segment, query_place):
    raw = jnp.einsum(
        "qhd,khd->hqk", queries, keys_all, preferred_element_type=jnp.float32
    ) * HEAD_DIM ** (-0.5)
    key_place = lax.broadcasted_iota(jnp.int32, (1, keys_all.shape[0]), 1)
    allowed = (query_segment[:, None] == key_segment[None, :]) & (key_place <= query_place[:, None])
    return jnp.where(allowed[None], raw, MASKED)


def split_blocks(queries, segment):
    length = queries.shape[0]
    block_rows = min(512, length)
    blocks = length // block_rows
    place = jnp.arange(length, dtype=jnp.int32).reshape(blocks, block_rows)
    return (
        queries.reshape(blocks, block_rows, queries.shape[1], queries.shape[2]),
        segment.reshape(blocks, block_rows),
        place,
    )


def attend_forward(queries, keys_all, values_all, segment):
    query_blocks, segment_blocks, place_blocks = split_blocks(queries, segment)

    def one_block(item):
        query_rows, query_segment, query_place = item
        scores = block_scores(query_rows, keys_all, query_segment, segment, query_place)
        row_max = jnp.max(scores, axis=-1, keepdims=True)
        expo = jnp.exp(scores - row_max)
        row_total = jnp.sum(expo, axis=-1, keepdims=True)
        prob_rows = (expo / row_total).astype(jnp.bfloat16)
        mixed = jnp.einsum(
            "hqk,khd->qhd", prob_rows, values_all, preferred_element_type=jnp.float32
        )
        return (mixed, row_max[..., 0] + jnp.log(row_total[..., 0]))

    mixed, log_total = lax.map(one_block, (query_blocks, segment_blocks, place_blocks))
    return (mixed.reshape(queries.shape[0], -1).astype(jnp.bfloat16), log_total)


def attend_backward(queries, keys_all, values_all, segment, log_total, grad_mix):
    query_blocks, segment_blocks, place_blocks = split_blocks(queries, segment)
    grad_blocks = grad_mix.reshape(query_blocks.shape)
    factor = HEAD_DIM ** (-0.5)

    def one_block(carry, item):
        key_acc, value_acc = carry
        query_rows, query_segment, query_place, log_rows, grad_rows = item
        scores = block_scores(query_rows, keys_all, query_segment, segment, query_place)
        prob_rows = jnp.exp(scores - log_rows[..., None])
        value_acc = value_acc + jnp.einsum(
            "hqk,qhd->khd",
            prob_rows.astype(jnp.bfloat16),
            grad_rows,
            preferred_element_type=jnp.float32,
        )
        grad_prob = jnp.einsum(
            "qhd,khd->hqk", grad_rows, values_all, preferred_element_type=jnp.float32
        )
        grad_scores = (
            prob_rows * (grad_prob - jnp.sum(prob_rows * grad_prob, axis=-1, keepdims=True))
        ).astype(jnp.bfloat16)
        grad_query = (
            jnp.einsum("hqk,khd->qhd", grad_scores, keys_all, preferred_element_type=jnp.float32)
            * factor
        )
        key_acc = (
            key_acc
            + jnp.einsum(
                "hqk,qhd->khd", grad_scores, query_rows, preferred_element_type=jnp.float32
            )
            * factor
        )
        return ((key_acc, value_acc), grad_query)

    zeros_like_keys = jnp.zeros(keys_all.shape, jnp.float32)
    (grad_keys, grad_values), grad_queries = lax.scan(
        one_block,
        (zeros_like_keys, zeros_like_keys),
        (query_blocks, segment_blocks, place_blocks, log_total, grad_blocks),
    )
    grad_queries = grad_queries.reshape(queries.shape)
    return jnp.stack([grad_queries, grad_keys, grad_values], axis=1).astype(jnp.bfloat16)


def local(tokens, segment_ids, gain_attn, gain_ffn, w_qkv, w_out, w_gate_up, w_down, grad_out):
    values = tokens.astype(jnp.float32)
    head_cols = w_qkv.shape[2]
    heads_here = head_cols // HEAD_DIM
    hidden_here = w_gate_up.shape[2]
    qkv_block = w_qkv.reshape(w_qkv.shape[0], 3 * head_cols)
    gate_up_block = w_gate_up.reshape(w_gate_up.shape[0], 2 * hidden_here)
    seq_count, seq_length = segment_ids.shape
    unit_one, rescale_one, normed_one = row_norm(values, gain_attn)
    gathered_one, packed = project_up(normed_one, qkv_block)
    packed = packed.reshape(-1, 3, heads_here, HEAD_DIM)
    mix_parts, log_parts = ([], [])
    for index in range(seq_count):
        rows_here = packed[index * seq_length : (index + 1) * seq_length]
        mixed, log_total = attend_forward(
            rows_here[:, 0], rows_here[:, 1], rows_here[:, 2], segment_ids[index]
        )
        mix_parts.append(mixed)
        log_parts.append(log_total)
    attn_mix = jnp.concatenate(mix_parts, axis=0)
    gathered_mix, attn_branch = project_down(attn_mix, w_out)
    hidden = values + attn_branch
    unit_two, rescale_two, normed_two = row_norm(hidden, gain_ffn)
    gathered_two, gate_up = project_up(normed_two, gate_up_block)
    gate_vals = gate_up[:, :hidden_here].astype(jnp.float32)
    up_vals = gate_up[:, hidden_here:].astype(jnp.float32)
    sigmoid_gate = jax.nn.sigmoid(gate_vals)
    silu_gate = gate_vals * sigmoid_gate
    active = (silu_gate * up_vals).astype(jnp.bfloat16)
    gathered_act, ffn_branch = project_down(active, w_down)
    output = (hidden + ffn_branch).astype(jnp.bfloat16)
    grad_rows_out, grad_active = back_down(grad_out, w_down)
    grad_down = weight_grad(gathered_act, grad_rows_out)
    grad_act_f = grad_active.astype(jnp.float32)
    grad_gate = grad_act_f * up_vals * sigmoid_gate * (1.0 + gate_vals * (1.0 - sigmoid_gate))
    grad_up = grad_act_f * silu_gate
    grad_gate_up_rows = jnp.concatenate([grad_gate, grad_up], axis=1).astype(jnp.bfloat16)
    grad_cols_two, grad_normed_two = back_up(grad_gate_up_rows, gate_up_block)
    grad_gate_up = weight_grad(gathered_two, grad_cols_two).reshape(w_gate_up.shape)
    grad_hidden_norm, grad_gain_two = norm_backward(
        grad_normed_two, unit_two, rescale_two, gain_ffn
    )
    grad_hidden = grad_out.astype(jnp.float32) + grad_hidden_norm
    grad_rows_hidden, grad_mix = back_down(grad_hidden.astype(jnp.bfloat16), w_out)
    grad_out_weight = weight_grad(gathered_mix, grad_rows_hidden)
    grad_mix = grad_mix.reshape(-1, heads_here, HEAD_DIM)
    grad_parts = []
    for index in range(seq_count):
        rows_here = packed[index * seq_length : (index + 1) * seq_length]
        grad_parts.append(
            attend_backward(
                rows_here[:, 0],
                rows_here[:, 1],
                rows_here[:, 2],
                segment_ids[index],
                log_parts[index],
                grad_mix[index * seq_length : (index + 1) * seq_length],
            )
        )
    grad_packed = jnp.concatenate(grad_parts, axis=0).reshape(-1, 3 * head_cols)
    grad_cols_one, grad_normed_one = back_up(grad_packed, qkv_block)
    grad_qkv = weight_grad(gathered_one, grad_cols_one).reshape(w_qkv.shape)
    grad_input_norm, grad_gain_one = norm_backward(
        grad_normed_one, unit_one, rescale_one, gain_attn
    )
    grad_tokens = grad_hidden + grad_input_norm
    summed = lax.psum((grad_qkv, grad_out_weight, grad_gate_up, grad_down), "dp")
    gains = lax.psum((grad_gain_one, grad_gain_two), ("dp", "row"))
    return (output, grad_tokens, gains[0], gains[1], summed[0], summed[1], summed[2], summed[3])


def swap(values):
    return lax.ppermute(values, "dp", [(0, 1), (1, 0)])


def hop(values, axis, flip):
    return lax.ppermute(values, axis, [(at, at ^ flip) for at in range(lax.axis_size(axis))])


def after(values, first):
    return lax.optimization_barrier((values, first))[0]


def by_core(core, mine, other, axis=0):
    first = jnp.where(core == 0, mine, other)
    second = jnp.where(core == 0, other, mine)
    return jnp.concatenate([first, second], axis=axis)


def pick(values, core, axis=0):
    half = values.shape[axis] // 2
    return lax.dynamic_slice_in_dim(values, core * half, half, axis)


def to_sequence(values, core, col, seq_length):
    seqs = values.shape[0] // seq_length
    half = seq_length // 2
    parts = values.reshape(seqs, seq_length, -1)
    mine = pick(parts, core, 1)
    other = swap(pick(parts, 1 - core, 1))
    chunks = by_core(core, mine, other)
    got = []
    for flip in range(4):
        chunk = lax.dynamic_index_in_dim(chunks, col ^ flip, 0, keepdims=False)
        got.append(hop(chunk, "col", flip) if flip else chunk)
    rows = jnp.concatenate(got, axis=1)
    return by_core(core, rows, swap(rows))


def from_sequence(rows, core, col, seq_length):
    half = rows.shape[0]
    width = rows.shape[1] // 4
    got = []
    for flip in range(4):
        chunk = rows[:, flip * width : (flip + 1) * width]
        got.append(hop(chunk, "col", flip) if flip else chunk)
    got = jnp.stack(got, axis=0)
    seqs = 2
    mine = jnp.stack(
        [lax.dynamic_index_in_dim(got, (core * seqs + at) ^ col, 0, False) for at in range(seqs)]
    )
    other = jnp.stack(
        [
            lax.dynamic_index_in_dim(got, ((1 - core) * seqs + at) ^ col, 0, False)
            for at in range(seqs)
        ]
    )
    return by_core(core, mine, swap(other), 1).reshape(seqs * seq_length, -1)


def times(left, right):
    return jnp.dot(left, right, preferred_element_type=jnp.float32)


def times_t(left, right):
    return lax.dot_general(
        left, right, (((1,), (1,)), ((), ())), preferred_element_type=jnp.float32
    )


def norm_rows(values):
    rescale = lax.rsqrt(jnp.mean(values * values, axis=1) + EPS)[:, None]
    return (values * rescale, rescale)


def norm_rows_back(grad_normed, unit_rows, rescale, gain_vec):
    weighted = grad_normed * gain_vec[None, :]
    inner = jnp.sum(weighted * unit_rows, axis=1, keepdims=True) / D
    return rescale * (weighted - unit_rows * inner)


def join_blocks(*refs):
    blocks, whole = (refs[:16], refs[16])
    _, rows, width = blocks[0].shape
    for at, block in enumerate(blocks):
        line, place = divmod(at, 4)
        whole[:, line * rows : (line + 1) * rows, place * width : (place + 1) * width] = block[...]


def spread_weights(block, first_cols=None, first_rows=None):
    grid = [[None] * 4 for _ in range(4)]
    block_cols = block if first_cols is None else after(block, first_cols)
    block_rows = block if first_rows is None else after(block, first_rows)
    near = hop(block_cols, "col", 1)
    far = hop(block_cols, "col", 3)
    grid[0] = [block_rows, near, hop(near, "col", 3), far]
    for at in (0, 1, 3, 2):
        grid[1][at] = hop(grid[0][at], "row", 1)
        grid[2][at] = hop(grid[0][at], "row", 2)
    for at in range(4):
        if at < 2:
            grid[3][at] = hop(grid[1][at], "row", 2)
        else:
            grid[3][at] = hop(grid[2][at], "row", 1)
    return grid


def join_weights(grid):
    kinds, rows, width = grid[0][0].shape
    whole = pl.pallas_call(
        join_blocks, out_shape=jax.ShapeDtypeStruct((kinds, 4 * rows, 4 * width), jnp.bfloat16)
    )(*[block for line in grid for block in line])
    return whole.reshape(-1, 4 * width)


def order_blocks(place_ref, blocks, whole):
    _, _, rows, width = blocks.shape
    for at in range(16):
        line, place = divmod(at, 4)
        block = blocks[(place_ref[0] ^ line) * 4 + (place_ref[1] ^ place)]
        whole[:, line * rows : (line + 1) * rows, place * width : (place + 1) * width] = block


def gather_weights(block, row, col):
    kinds, rows, width = block.shape
    blocks = lax.all_gather(block, ("row", "col"), axis=0)
    vmem = pl.BlockSpec(memory_space=pltpu.VMEM)
    whole = pl.pallas_call(
        order_blocks,
        out_shape=jax.ShapeDtypeStruct((kinds, 4 * rows, 4 * width), jnp.bfloat16),
        in_specs=[pl.BlockSpec(memory_space=pltpu.SMEM), vmem],
        out_specs=vmem,
    )(jnp.stack([row, col]), blocks)
    return whole.reshape(-1, 4 * width)


def wide(values):
    return values.astype(jnp.float32)


def low(values):
    return values.astype(jnp.bfloat16)


def start_rows(grad, kinds):
    grid = low(grad).reshape(kinds, 2, 2, -1, grad.shape[1])
    half = grad.shape[1] // 2
    left, right = (grid[..., :half], grid[..., half:])
    got = hop(left[:, 1], "row", 2)
    got_r = hop(right[:, :, 1], "row", 1)
    return (left, right, got, got_r)


def middle_rows(state):
    left, right, got, got_r = state
    sent = low(wide(left[:, 0, 1]) + wide(got[:, 1]))
    sent_r = low(wide(right[:, 1, 0]) + wide(got_r[:, 1]))
    return ((sent, sent_r), state + (hop(sent, "row", 1), hop(sent_r, "row", 2)))


def end_rows(state):
    left, right, got, got_r, last, last_r = state
    sums = wide(left[:, 0, 0]) + wide(got[:, 0]) + wide(last)
    sums_r = wide(right[:, 0, 0]) + wide(got_r[:, 0]) + wide(last_r)
    return (sums, sums_r)


def start_end_cols(state):
    sums, sums_r = state
    width = sums.shape[-1] // 2
    parts = [low(sums[..., width:]), low(sums_r[..., :width]), low(sums_r[..., width:])]
    return (parts, sums[..., :width], [hop(parts[flip - 1], "col", flip) for flip in (1, 2, 3)])


def end_cols(total, got):
    return total + wide(got[0]) + wide(got[1]) + wide(got[2])


def start_cols(grad):
    width = grad.shape[1] // 4
    grid = [low(grad[:, at * width : (at + 1) * width]) for at in range(4)]
    return [grid[0]] + [hop(grid[flip], "col", flip) for flip in range(1, 4)]


def middle_cols(state):
    return wide(state[0]) + wide(state[1]) + wide(state[2]) + wide(state[3])


def join_halves(core_ref, mine, other, whole):
    rows = mine.shape[1]
    for at in range(2):
        part = slice(at * rows, (at + 1) * rows)

        @pl.when(core_ref[0] == at)
        def _():
            whole[:, part, :] = mine[...]

        @pl.when(core_ref[0] != at)
        def _():
            whole[:, part, :] = other[...].astype(jnp.float32)


def joined(mine, core):
    kinds, rows, width = mine.shape
    mine_low = low(mine)
    vmem = pl.BlockSpec(memory_space=pltpu.VMEM)
    return pl.pallas_call(
        join_halves,
        out_shape=jax.ShapeDtypeStruct((kinds, 2 * rows, width), jnp.float32),
        in_specs=[pl.BlockSpec(memory_space=pltpu.SMEM), vmem, vmem],
        out_specs=vmem,
    )(core[None], mine, swap(mine_low))


def chip_local(tokens, segment_ids, gain_attn, gain_ffn, w_qkv, w_out, w_gate_up, w_down, grad_out):
    core = lax.axis_index("dp")
    col = lax.axis_index("col")
    length = segment_ids.shape[1]
    features = w_qkv.shape[0]
    head_cols = w_qkv.shape[2] // 2
    heads = 4 * head_cols // HEAD_DIM
    factor = HEAD_DIM ** (-0.5)

    values = to_sequence(tokens, core, col, length).astype(jnp.float32)
    attn_block = jnp.concatenate(
        [pick(w_qkv, core, 2).transpose(1, 2, 0), pick(w_out, core)[None]], axis=0
    )
    attn_grid = spread_weights(attn_block)
    big_attn = join_weights(attn_grid)
    big_qkv, big_out = (big_attn[: 12 * head_cols], big_attn[12 * head_cols :])
    gains = jnp.stack([gain_attn, gain_ffn], axis=0)
    gains = jnp.concatenate([gains] + [hop(gains, "col", flip) for flip in range(1, 4)], axis=1)
    corner = [(4 * at + to, 4 * to + at) for at in range(4) for to in range(4)]
    segment_rows = lax.ppermute(segment_ids, ("row", "col"), corner)
    segment_rows = by_core(core, segment_rows, swap(segment_rows))
    segment = lax.dynamic_index_in_dim(segment_rows, col, 0, keepdims=False)
    ffn_block = jnp.concatenate(
        [pick(w_gate_up, core, 2).transpose(1, 2, 0), pick(w_down, core)[None]], axis=0
    )
    big_ffn = gather_weights(ffn_block, lax.axis_index("row"), col)
    spread = big_ffn.shape[0] // 3
    big_gate_up, big_down = (big_ffn[: 2 * spread], big_ffn[2 * spread :])
    cotangent = to_sequence(after(grad_out, attn_grid[3]), core, col, length)

    unit_one, rescale_one = norm_rows(values)
    normed_one = (unit_one * gains[0][None, :]).astype(jnp.bfloat16)
    packed = times_t(normed_one, big_qkv).astype(jnp.bfloat16).reshape(length, 3, heads, HEAD_DIM)
    queries, keys, vals = (packed[:, 0], packed[:, 1], packed[:, 2])
    scores = jnp.einsum("qhd,khd->hqk", queries, keys, preferred_element_type=jnp.float32) * factor
    spot = jnp.arange(length, dtype=jnp.int32)
    live = (segment[:, None] == segment[None, :]) & (spot[None, :] <= spot[:, None])
    scores = jnp.where(live[None], scores, MASKED)
    expo = jnp.exp(scores - jnp.max(scores, axis=-1, keepdims=True))
    prob = expo / jnp.sum(expo, axis=-1, keepdims=True)
    prob_low = prob.astype(jnp.bfloat16)
    mixed = jnp.einsum("hqk,khd->qhd", prob_low, vals, preferred_element_type=jnp.float32)
    mixed = mixed.reshape(length, -1).astype(jnp.bfloat16)
    branch = times(mixed, big_out)
    hidden_rows = values + (branch + swap(branch))
    unit_two, rescale_two = norm_rows(hidden_rows)
    normed_two = (unit_two * gains[1][None, :]).astype(jnp.bfloat16)
    gate_up = times_t(normed_two, big_gate_up).astype(jnp.bfloat16)
    half = gate_up.shape[1] // 2
    gate_vals = gate_up[:, :half].astype(jnp.float32)
    up_vals = gate_up[:, half:].astype(jnp.float32)
    sigmoid_gate = jax.nn.sigmoid(gate_vals)
    silu_gate = gate_vals * sigmoid_gate
    active = (silu_gate * up_vals).astype(jnp.bfloat16)

    down_state = start_cols(weight_grad(active, cotangent))
    grad_act = wide(low(times_t(cotangent, big_down)))
    grad_gate = grad_act * up_vals * sigmoid_gate * (1.0 + gate_vals * (1.0 - sigmoid_gate))
    grad_up = grad_act * silu_gate
    grad_gu = jnp.concatenate([grad_gate, grad_up], axis=1).astype(jnp.bfloat16)
    grad_two = times(grad_gu, big_gate_up)
    grad_two = grad_two + swap(grad_two)
    gate_up_state = start_rows(weight_grad(grad_gu, normed_two), 2)
    back_two = norm_rows_back(grad_two, unit_two, rescale_two, gains[1])
    gain_two = jnp.sum(pick(grad_two * unit_two, core), axis=0)
    grad_hidden = cotangent.astype(jnp.float32) + back_two
    grad_branch = grad_hidden.astype(jnp.bfloat16)
    grad_w_out = low(weight_grad(mixed, grad_branch))
    grad_mix = times_t(grad_branch, big_out).astype(jnp.bfloat16).reshape(length, heads, HEAD_DIM)
    grad_vals = jnp.einsum("hqk,qhd->khd", prob_low, grad_mix, preferred_element_type=jnp.float32)
    grad_prob = jnp.einsum("qhd,khd->hqk", grad_mix, vals, preferred_element_type=jnp.float32)
    inner = jnp.sum(prob * grad_prob, axis=-1, keepdims=True)
    grad_scores = (prob * (grad_prob - inner)).astype(jnp.bfloat16)
    grad_queries = factor * jnp.einsum(
        "hqk,khd->qhd", grad_scores, keys, preferred_element_type=jnp.float32
    )
    grad_keys = factor * jnp.einsum(
        "hqk,qhd->khd", grad_scores, queries, preferred_element_type=jnp.float32
    )
    grad_packed = jnp.stack([grad_queries, grad_keys, grad_vals], axis=1)
    grad_packed = grad_packed.astype(jnp.bfloat16).reshape(length, -1)
    grad_attn = jnp.concatenate([low(weight_grad(grad_packed, normed_one)), grad_w_out], axis=0)

    gate_up_sent, gate_up_state = middle_rows(after(gate_up_state, grad_attn))
    grad_attn = after(grad_attn, gate_up_sent)
    attn_state = start_rows(grad_attn, 4)
    active = after(active, grad_attn)
    grad_packed = after(grad_packed, grad_attn)
    grad_one = times(grad_packed, big_qkv)
    grad_one = pick(grad_one, core) + swap(pick(grad_one, 1 - core))
    ffn = times(active, big_down)
    ffn_mine = pick(ffn, core) + swap(pick(ffn, 1 - core))
    output = (pick(hidden_rows, core) + ffn_mine).astype(jnp.bfloat16)
    unit_mine = pick(unit_one, core)
    back_one = norm_rows_back(grad_one, unit_mine, pick(rescale_one, core), gains[0])
    gain_one = jnp.sum(grad_one * unit_mine, axis=0)
    grad_rows = (pick(grad_hidden, core) + back_one).astype(jnp.bfloat16)

    gate_up_state = after(gate_up_state, (output, grad_rows))
    parts, gate_up_own, gate_up_got = start_end_cols(end_rows(gate_up_state))
    output = from_sequence(after(output, parts), core, col, length)
    down_rows = middle_cols(after(down_state, parts))
    down_state = start_rows(down_rows, 1)
    attn_sent, attn_state = middle_rows(after(attn_state, down_rows))
    down_sent, down_state = middle_rows(after(down_state, attn_sent))
    attn_parts, attn_own, attn_got = start_end_cols(end_rows(after(attn_state, down_sent)))
    gain_sums = jnp.stack([gain_one, gain_two], axis=0)
    gain_sums, grad_rows = after((gain_sums, grad_rows), attn_parts)
    grad_tokens = from_sequence(grad_rows, core, col, length).astype(jnp.float32)
    gate_up_got, down_state = after((gate_up_got, down_state), attn_parts)
    mine_gate_up = end_cols(gate_up_own, gate_up_got)
    mine_down = jnp.concatenate(end_rows(down_state), axis=-1)
    mine_attn = end_cols(attn_own, attn_got)

    gain_sums = gain_sums + swap(gain_sums)
    gain_sums = gain_sums + hop(gain_sums, "row", 1)
    gain_sums = gain_sums + hop(gain_sums, "row", 2)
    gain_mine = gain_sums[:, :features]
    for flip in range(1, 4):
        piece = gain_sums[:, flip * features : (flip + 1) * features]
        gain_mine = gain_mine + hop(piece, "col", flip)

    whole_attn = joined(mine_attn, core)
    return (
        output,
        grad_tokens,
        gain_mine[0],
        gain_mine[1],
        whole_attn[:3].transpose(2, 0, 1),
        whole_attn[3],
        joined(mine_gate_up, core).transpose(2, 0, 1),
        joined(mine_down, core)[0],
    )


def layer(tokens, segment_ids, *rest):
    sizes = (lax.axis_size("dp"), lax.axis_size("row"), lax.axis_size("col"))
    if sizes == (2, 4, 4) and tokens.shape[0] == 2 * segment_ids.shape[1]:
        return chip_local(tokens, segment_ids, *rest)
    return local(tokens, segment_ids, *rest)


def solution(mesh):
    in_specs = (
        P(("dp", "row"), "col"),
        P(("dp", "col"), None),
        P("col"),
        P("col"),
        P("col", None, "row"),
        P("row", "col"),
        P("col", None, "row"),
        P("row", "col"),
        P(("dp", "row"), "col"),
    )
    out_specs = (
        P(("dp", "row"), "col"),
        P(("dp", "row"), "col"),
        P("col"),
        P("col"),
        P("col", None, "row"),
        P("row", "col"),
        P("col", None, "row"),
        P("row", "col"),
    )
    return jax.shard_map(layer, mesh=mesh, in_specs=in_specs, out_specs=out_specs, check_vma=False)
```

```python
import jax
import jax.numpy as jnp
from jax import lax
from jax.experimental import pallas as pl
from jax.experimental.pallas import tpu as pltpu
from jax.sharding import PartitionSpec as P

D = 1024
HEAD_DIM = 64


EPS = 1e-06
MASKED = -1e30


def row_norm(values, gain_vec):
    squares = lax.psum(jnp.sum(values * values, axis=1), "col")
    rescale = lax.rsqrt(squares / D + EPS)
    unit_rows = values * rescale[:, None]
    return (unit_rows, rescale, (unit_rows * gain_vec[None, :]).astype(jnp.bfloat16))


def norm_backward(grad_normed, unit_rows, rescale, gain_vec):
    weighted = grad_normed * gain_vec[None, :]
    inner_sum = lax.psum(jnp.sum(weighted * unit_rows, axis=1), "col")
    grad_in = rescale[:, None] * (weighted - unit_rows * (inner_sum / D)[:, None])
    grad_gain = jnp.sum(grad_normed * unit_rows, axis=0)
    return (grad_in, grad_gain)


def project_up(normed, weight_block):
    gathered = lax.all_gather(normed, "row", axis=0, tiled=True)

    def term(begin_at, row_count):
        return jnp.dot(gathered, weight_block, preferred_element_type=jnp.float32)

    result = lax.psum_scatter(
        term(jnp.int32(0), gathered.shape[0] // lax.axis_size("col") * lax.axis_size("col")),
        "col",
        scatter_dimension=0,
        tiled=True,
    )
    return (gathered, result.astype(jnp.bfloat16))


def project_down(values, weight_block):
    gathered = lax.all_gather(values, "col", axis=0, tiled=True)

    def term(begin_at, row_count):
        return jnp.dot(gathered, weight_block, preferred_element_type=jnp.float32)

    result = lax.psum_scatter(
        term(jnp.int32(0), gathered.shape[0] // lax.axis_size("row") * lax.axis_size("row")),
        "row",
        scatter_dimension=0,
        tiled=True,
    )
    return (gathered, result)


def back_down(grad_rows, weight_block):
    gathered = lax.all_gather(grad_rows, "row", axis=0, tiled=True)

    def term(begin_at, row_count):
        return lax.dot_general(
            gathered, weight_block, (((1,), (1,)), ((), ())), preferred_element_type=jnp.float32
        )

    result = lax.psum_scatter(
        term(jnp.int32(0), gathered.shape[0] // lax.axis_size("col") * lax.axis_size("col")),
        "col",
        scatter_dimension=0,
        tiled=True,
    )
    return (gathered, result.astype(jnp.bfloat16))


def back_up(grad_cols, weight_block):
    gathered = lax.all_gather(grad_cols, "col", axis=0, tiled=True)

    def term(begin_at, row_count):
        return lax.dot_general(
            gathered, weight_block, (((1,), (1,)), ((), ())), preferred_element_type=jnp.float32
        )

    result = lax.psum_scatter(
        term(jnp.int32(0), gathered.shape[0] // lax.axis_size("row") * lax.axis_size("row")),
        "row",
        scatter_dimension=0,
        tiled=True,
    )
    return (gathered, result)


def weight_grad(left_rows, right_rows):
    return lax.dot_general(
        left_rows, right_rows, (((0,), (0,)), ((), ())), preferred_element_type=jnp.float32
    )


def block_scores(queries, keys_all, query_segment, key_segment, query_place):
    raw = jnp.einsum(
        "qhd,khd->hqk", queries, keys_all, preferred_element_type=jnp.float32
    ) * HEAD_DIM ** (-0.5)
    key_place = lax.broadcasted_iota(jnp.int32, (1, keys_all.shape[0]), 1)
    allowed = (query_segment[:, None] == key_segment[None, :]) & (key_place <= query_place[:, None])
    return jnp.where(allowed[None], raw, MASKED)


def split_blocks(queries, segment):
    length = queries.shape[0]
    block_rows = min(512, length)
    blocks = length // block_rows
    place = jnp.arange(length, dtype=jnp.int32).reshape(blocks, block_rows)
    return (
        queries.reshape(blocks, block_rows, queries.shape[1], queries.shape[2]),
        segment.reshape(blocks, block_rows),
        place,
    )


def attend_forward(queries, keys_all, values_all, segment):
    query_blocks, segment_blocks, place_blocks = split_blocks(queries, segment)

    def one_block(item):
        query_rows, query_segment, query_place = item
        scores = block_scores(query_rows, keys_all, query_segment, segment, query_place)
        row_max = jnp.max(scores, axis=-1, keepdims=True)
        expo = jnp.exp(scores - row_max)
        row_total = jnp.sum(expo, axis=-1, keepdims=True)
        prob_rows = (expo / row_total).astype(jnp.bfloat16)
        mixed = jnp.einsum(
            "hqk,khd->qhd", prob_rows, values_all, preferred_element_type=jnp.float32
        )
        return (mixed, row_max[..., 0] + jnp.log(row_total[..., 0]))

    mixed, log_total = lax.map(one_block, (query_blocks, segment_blocks, place_blocks))
    return (mixed.reshape(queries.shape[0], -1).astype(jnp.bfloat16), log_total)


def attend_backward(queries, keys_all, values_all, segment, log_total, grad_mix):
    query_blocks, segment_blocks, place_blocks = split_blocks(queries, segment)
    grad_blocks = grad_mix.reshape(query_blocks.shape)
    factor = HEAD_DIM ** (-0.5)

    def one_block(carry, item):
        key_acc, value_acc = carry
        query_rows, query_segment, query_place, log_rows, grad_rows = item
        scores = block_scores(query_rows, keys_all, query_segment, segment, query_place)
        prob_rows = jnp.exp(scores - log_rows[..., None])
        value_acc = value_acc + jnp.einsum(
            "hqk,qhd->khd",
            prob_rows.astype(jnp.bfloat16),
            grad_rows,
            preferred_element_type=jnp.float32,
        )
        grad_prob = jnp.einsum(
            "qhd,khd->hqk", grad_rows, values_all, preferred_element_type=jnp.float32
        )
        grad_scores = (
            prob_rows * (grad_prob - jnp.sum(prob_rows * grad_prob, axis=-1, keepdims=True))
        ).astype(jnp.bfloat16)
        grad_query = (
            jnp.einsum("hqk,khd->qhd", grad_scores, keys_all, preferred_element_type=jnp.float32)
            * factor
        )
        key_acc = (
            key_acc
            + jnp.einsum(
                "hqk,qhd->khd", grad_scores, query_rows, preferred_element_type=jnp.float32
            )
            * factor
        )
        return ((key_acc, value_acc), grad_query)

    zeros_like_keys = jnp.zeros(keys_all.shape, jnp.float32)
    (grad_keys, grad_values), grad_queries = lax.scan(
        one_block,
        (zeros_like_keys, zeros_like_keys),
        (query_blocks, segment_blocks, place_blocks, log_total, grad_blocks),
    )
    grad_queries = grad_queries.reshape(queries.shape)
    return jnp.stack([grad_queries, grad_keys, grad_values], axis=1).astype(jnp.bfloat16)


def local(tokens, segment_ids, gain_attn, gain_ffn, w_qkv, w_out, w_gate_up, w_down, grad_out):
    values = tokens.astype(jnp.float32)
    head_cols = w_qkv.shape[2]
    heads_here = head_cols // HEAD_DIM
    hidden_here = w_gate_up.shape[2]
    qkv_block = w_qkv.reshape(w_qkv.shape[0], 3 * head_cols)
    gate_up_block = w_gate_up.reshape(w_gate_up.shape[0], 2 * hidden_here)
    seq_count, seq_length = segment_ids.shape
    unit_one, rescale_one, normed_one = row_norm(values, gain_attn)
    gathered_one, packed = project_up(normed_one, qkv_block)
    packed = packed.reshape(-1, 3, heads_here, HEAD_DIM)
    mix_parts, log_parts = ([], [])
    for index in range(seq_count):
        rows_here = packed[index * seq_length : (index + 1) * seq_length]
        mixed, log_total = attend_forward(
            rows_here[:, 0], rows_here[:, 1], rows_here[:, 2], segment_ids[index]
        )
        mix_parts.append(mixed)
        log_parts.append(log_total)
    attn_mix = jnp.concatenate(mix_parts, axis=0)
    gathered_mix, attn_branch = project_down(attn_mix, w_out)
    hidden = values + attn_branch
    unit_two, rescale_two, normed_two = row_norm(hidden, gain_ffn)
    gathered_two, gate_up = project_up(normed_two, gate_up_block)
    gate_vals = gate_up[:, :hidden_here].astype(jnp.float32)
    up_vals = gate_up[:, hidden_here:].astype(jnp.float32)
    sigmoid_gate = jax.nn.sigmoid(gate_vals)
    silu_gate = gate_vals * sigmoid_gate
    active = (silu_gate * up_vals).astype(jnp.bfloat16)
    gathered_act, ffn_branch = project_down(active, w_down)
    output = (hidden + ffn_branch).astype(jnp.bfloat16)
    grad_rows_out, grad_active = back_down(grad_out, w_down)
    grad_down = weight_grad(gathered_act, grad_rows_out)
    grad_act_f = grad_active.astype(jnp.float32)
    grad_gate = grad_act_f * up_vals * sigmoid_gate * (1.0 + gate_vals * (1.0 - sigmoid_gate))
    grad_up = grad_act_f * silu_gate
    grad_gate_up_rows = jnp.concatenate([grad_gate, grad_up], axis=1).astype(jnp.bfloat16)
    grad_cols_two, grad_normed_two = back_up(grad_gate_up_rows, gate_up_block)
    grad_gate_up = weight_grad(gathered_two, grad_cols_two).reshape(w_gate_up.shape)
    grad_hidden_norm, grad_gain_two = norm_backward(
        grad_normed_two, unit_two, rescale_two, gain_ffn
    )
    grad_hidden = grad_out.astype(jnp.float32) + grad_hidden_norm
    grad_rows_hidden, grad_mix = back_down(grad_hidden.astype(jnp.bfloat16), w_out)
    grad_out_weight = weight_grad(gathered_mix, grad_rows_hidden)
    grad_mix = grad_mix.reshape(-1, heads_here, HEAD_DIM)
    grad_parts = []
    for index in range(seq_count):
        rows_here = packed[index * seq_length : (index + 1) * seq_length]
        grad_parts.append(
            attend_backward(
                rows_here[:, 0],
                rows_here[:, 1],
                rows_here[:, 2],
                segment_ids[index],
                log_parts[index],
                grad_mix[index * seq_length : (index + 1) * seq_length],
            )
        )
    grad_packed = jnp.concatenate(grad_parts, axis=0).reshape(-1, 3 * head_cols)
    grad_cols_one, grad_normed_one = back_up(grad_packed, qkv_block)
    grad_qkv = weight_grad(gathered_one, grad_cols_one).reshape(w_qkv.shape)
    grad_input_norm, grad_gain_one = norm_backward(
        grad_normed_one, unit_one, rescale_one, gain_attn
    )
    grad_tokens = grad_hidden + grad_input_norm
    summed = lax.psum((grad_qkv, grad_out_weight, grad_gate_up, grad_down), "dp")
    gains = lax.psum((grad_gain_one, grad_gain_two), ("dp", "row"))
    return (output, grad_tokens, gains[0], gains[1], summed[0], summed[1], summed[2], summed[3])


def swap(values):
    return lax.ppermute(values, "dp", [(0, 1), (1, 0)])


def hop(values, axis, flip):
    return lax.ppermute(values, axis, [(at, at ^ flip) for at in range(lax.axis_size(axis))])


def after(values, first):
    return lax.optimization_barrier((values, first))[0]


def by_core(core, mine, other, axis=0):
    first = jnp.where(core == 0, mine, other)
    second = jnp.where(core == 0, other, mine)
    return jnp.concatenate([first, second], axis=axis)


def pick(values, core, axis=0):
    half = values.shape[axis] // 2
    return lax.dynamic_slice_in_dim(values, core * half, half, axis)


def to_sequence(values, core, col, seq_length):
    seqs = values.shape[0] // seq_length
    half = seq_length // 2
    parts = values.reshape(seqs, seq_length, -1)
    mine = pick(parts, core, 1)
    other = swap(pick(parts, 1 - core, 1))
    chunks = by_core(core, mine, other)
    got = []
    for flip in range(4):
        chunk = lax.dynamic_index_in_dim(chunks, col ^ flip, 0, keepdims=False)
        got.append(hop(chunk, "col", flip) if flip else chunk)
    rows = jnp.concatenate(got, axis=1)
    return by_core(core, rows, swap(rows))


def send_rows(rows):
    width = rows.shape[1] // 4
    parts = [rows[:, at * width : (at + 1) * width] for at in range(4)]
    return [parts[0]] + [hop(parts[flip], "col", flip) for flip in range(1, 4)]


def from_sequence(got, core, col, seq_length):
    got = jnp.stack(got, axis=0)
    seqs = 2

    def of_core(which):
        picked = [
            lax.dynamic_index_in_dim(got, (which * seqs + at) ^ col, 0, False) for at in range(seqs)
        ]
        return jnp.stack(picked)

    mine, other = (of_core(core), of_core(1 - core))
    return by_core(core, mine, swap(other), 1).reshape(seqs * seq_length, -1)


def times(left, right):
    return jnp.dot(left, right, preferred_element_type=jnp.float32)


def times_t(left, right):
    return lax.dot_general(
        left, right, (((1,), (1,)), ((), ())), preferred_element_type=jnp.float32
    )


def norm_rows(values):
    rescale = lax.rsqrt(jnp.mean(values * values, axis=1) + EPS)[:, None]
    return (values * rescale, rescale)


def norm_rows_back(grad_normed, unit_rows, rescale, gain_vec):
    weighted = grad_normed * gain_vec[None, :]
    inner = jnp.sum(weighted * unit_rows, axis=1, keepdims=True) / D
    return rescale * (weighted - unit_rows * inner)


def join_blocks(*refs):
    blocks, wholes = (refs[:16], refs[16:])
    _, rows, width = blocks[0].shape
    for at, block in enumerate(blocks):
        line, place = divmod(at, 4)
        kind = 0
        for whole in wholes:
            part = block[kind : kind + whole.shape[0]]
            kind += whole.shape[0]
            whole[:, line * rows : (line + 1) * rows, place * width : (place + 1) * width] = part


def spread_weights(block, first_cols=None, first_rows=None):
    grid = [[None] * 4 for _ in range(4)]
    block_cols = block if first_cols is None else after(block, first_cols)
    block_rows = block if first_rows is None else after(block, first_rows)
    near = hop(block_cols, "col", 1)
    far = hop(block_cols, "col", 3)
    grid[0] = [block_rows, near, hop(near, "col", 3), far]
    for at in (0, 1, 3, 2):
        grid[1][at] = hop(grid[0][at], "row", 1)
        grid[2][at] = hop(grid[0][at], "row", 2)
    for at in range(4):
        if at < 2:
            grid[3][at] = hop(grid[1][at], "row", 2)
        else:
            grid[3][at] = hop(grid[2][at], "row", 1)
    return grid


def join_weights(grid, splits):
    _, rows, width = grid[0][0].shape
    shapes = [jax.ShapeDtypeStruct((at, 4 * rows, 4 * width), jnp.bfloat16) for at in splits]
    wholes = pl.pallas_call(join_blocks, out_shape=shapes)(*[b for line in grid for b in line])
    return [whole.reshape(-1, 4 * width) for whole in wholes]


def order_blocks(place_ref, blocks, whole):
    _, _, rows, width = blocks.shape
    for at in range(16):
        line, place = divmod(at, 4)
        block = blocks[(place_ref[0] ^ line) * 4 + (place_ref[1] ^ place)]
        whole[:, line * rows : (line + 1) * rows, place * width : (place + 1) * width] = block


def gather_weights(block, row, col):
    kinds, rows, width = block.shape
    blocks = lax.all_gather(block, ("row", "col"), axis=0)
    vmem = pl.BlockSpec(memory_space=pltpu.VMEM)
    whole = pl.pallas_call(
        order_blocks,
        out_shape=jax.ShapeDtypeStruct((kinds, 4 * rows, 4 * width), jnp.bfloat16),
        in_specs=[pl.BlockSpec(memory_space=pltpu.SMEM), vmem],
        out_specs=vmem,
    )(jnp.stack([row, col]), blocks)
    return whole.reshape(-1, 4 * width)


def wide(values):
    return values.astype(jnp.float32)


def low(values):
    return values.astype(jnp.bfloat16)


def start_rows(grad, kinds):
    grid = low(grad).reshape(kinds, 2, 2, -1, grad.shape[1])
    half = grad.shape[1] // 2
    left, right = (grid[..., :half], grid[..., half:])
    got = hop(left[:, 1], "row", 2)
    got_r = hop(right[:, :, 1], "row", 1)
    return (left, right, got, got_r)


def middle_rows(state):
    left, right, got, got_r = state
    sent = low(wide(left[:, 0, 1]) + wide(got[:, 1]))
    sent_r = low(wide(right[:, 1, 0]) + wide(got_r[:, 1]))
    return ((sent, sent_r), state + (hop(sent, "row", 1), hop(sent_r, "row", 2)))


def end_rows(state):
    left, right, got, got_r, last, last_r = state
    sums = wide(left[:, 0, 0]) + wide(got[:, 0]) + wide(last)
    sums_r = wide(right[:, 0, 0]) + wide(got_r[:, 0]) + wide(last_r)
    return (sums, sums_r)


def start_end_cols(state):
    sums, sums_r = state
    width = sums.shape[-1] // 2
    parts = [low(sums[..., width:]), low(sums_r[..., :width]), low(sums_r[..., width:])]
    return (parts, sums[..., :width], [hop(parts[flip - 1], "col", flip) for flip in (1, 2, 3)])


def end_cols(total, got):
    return total + wide(got[0]) + wide(got[1]) + wide(got[2])


def place_blocks(place_ref, whole, blocks):
    _, rows, width = blocks.shape
    for at in range(16):
        line, place = divmod(at, 4)
        block = whole[line * rows : (line + 1) * rows, place * width : (place + 1) * width]
        blocks[(place_ref[0] ^ line) * 4 + (place_ref[1] ^ place)] = block


def scatter_weights(grad, row, col):
    vmem = pl.BlockSpec(memory_space=pltpu.VMEM)
    shape = (16, grad.shape[0] // 4, grad.shape[1] // 4)
    blocks = pl.pallas_call(
        place_blocks,
        out_shape=jax.ShapeDtypeStruct(shape, jnp.bfloat16),
        in_specs=[pl.BlockSpec(memory_space=pltpu.SMEM), vmem],
        out_specs=vmem,
    )(jnp.stack([row, col]), low(grad))
    return lax.psum_scatter(blocks, "row", scatter_dimension=0, tiled=True)


def join_halves(core_ref, mine, other, whole):
    rows = mine.shape[1]
    for at in range(2):
        part = slice(at * rows, (at + 1) * rows)

        @pl.when(core_ref[0] == at)
        def _():
            whole[:, part, :] = mine[...].astype(jnp.float32)

        @pl.when(core_ref[0] != at)
        def _():
            whole[:, part, :] = other[...].astype(jnp.float32)


def joined(mine, core):
    kinds, rows, width = mine.shape
    mine_low = low(mine)
    vmem = pl.BlockSpec(memory_space=pltpu.VMEM)
    return pl.pallas_call(
        join_halves,
        out_shape=jax.ShapeDtypeStruct((kinds, 2 * rows, width), jnp.float32),
        in_specs=[pl.BlockSpec(memory_space=pltpu.SMEM), vmem, vmem],
        out_specs=vmem,
    )(core[None], mine, swap(mine_low))


def chip_local(tokens, segment_ids, gain_attn, gain_ffn, w_qkv, w_out, w_gate_up, w_down, grad_out):
    core = lax.axis_index("dp")
    col = lax.axis_index("col")
    length = segment_ids.shape[1]
    features = w_qkv.shape[0]
    head_cols = w_qkv.shape[2] // 2
    heads = 4 * head_cols // HEAD_DIM
    factor = HEAD_DIM ** (-0.5)

    values = to_sequence(tokens, core, col, length).astype(jnp.float32)
    attn_block = jnp.concatenate(
        [pick(w_qkv, core, 2).transpose(1, 2, 0), pick(w_out, core)[None]], axis=0
    )
    attn_grid = spread_weights(attn_block)
    big_qkv, big_out = join_weights(attn_grid, (3, 1))
    gains = jnp.stack([gain_attn, gain_ffn], axis=0)
    gains = jnp.concatenate([gains] + [hop(gains, "col", flip) for flip in range(1, 4)], axis=1)
    corner = [(4 * at + to, 4 * to + at) for at in range(4) for to in range(4)]
    segment_rows = lax.ppermute(segment_ids, ("row", "col"), corner)
    segment_rows = by_core(core, segment_rows, swap(segment_rows))
    segment = lax.dynamic_index_in_dim(segment_rows, col, 0, keepdims=False)
    row = lax.axis_index("row")
    big_gate_up = gather_weights(pick(w_gate_up, core, 2).transpose(1, 2, 0), row, col)
    down_block = pick(w_down, core)[None]
    down_grid = spread_weights(down_block, attn_grid[0], attn_grid[1] + attn_grid[2])
    (big_down,) = join_weights(down_grid, (1,))
    cotangent = to_sequence(after(grad_out, attn_grid[3]), core, col, length)

    unit_one, rescale_one = norm_rows(values)
    normed_one = (unit_one * gains[0][None, :]).astype(jnp.bfloat16)
    packed = times_t(normed_one, big_qkv).astype(jnp.bfloat16).reshape(length, 3, heads, HEAD_DIM)
    queries, keys, vals = (packed[:, 0], packed[:, 1], packed[:, 2])
    scores = jnp.einsum("qhd,khd->hqk", queries, keys, preferred_element_type=jnp.float32) * factor
    spot = jnp.arange(length, dtype=jnp.int32)
    live = (segment[:, None] == segment[None, :]) & (spot[None, :] <= spot[:, None])
    scores = jnp.where(live[None], scores, MASKED)
    expo = jnp.exp(scores - jnp.max(scores, axis=-1, keepdims=True))
    prob = expo / jnp.sum(expo, axis=-1, keepdims=True)
    prob_low = prob.astype(jnp.bfloat16)
    mixed = jnp.einsum("hqk,khd->qhd", prob_low, vals, preferred_element_type=jnp.float32)
    mixed = mixed.reshape(length, -1).astype(jnp.bfloat16)
    branch = times(mixed, big_out)
    hidden_rows = values + (branch + swap(branch))
    unit_two, rescale_two = norm_rows(hidden_rows)
    normed_two = (unit_two * gains[1][None, :]).astype(jnp.bfloat16)
    gate_up = times_t(normed_two, big_gate_up).astype(jnp.bfloat16)
    half = gate_up.shape[1] // 2
    gate_vals = gate_up[:, :half].astype(jnp.float32)
    up_vals = gate_up[:, half:].astype(jnp.float32)
    sigmoid_gate = jax.nn.sigmoid(gate_vals)
    silu_gate = gate_vals * sigmoid_gate
    active = (silu_gate * up_vals).astype(jnp.bfloat16)

    down_rows = scatter_weights(weight_grad(active, cotangent), row, col)
    grad_act = wide(low(times_t(cotangent, big_down)))
    grad_gate = grad_act * up_vals * sigmoid_gate * (1.0 + gate_vals * (1.0 - sigmoid_gate))
    grad_up = grad_act * silu_gate
    grad_gu = jnp.concatenate([grad_gate, grad_up], axis=1).astype(jnp.bfloat16)
    grad_two = times(grad_gu, big_gate_up)
    grad_two = grad_two + swap(grad_two)
    gate_up_state = start_rows(weight_grad(grad_gu, normed_two), 2)
    back_two = norm_rows_back(grad_two, unit_two, rescale_two, gains[1])
    gain_two = jnp.sum(pick(grad_two * unit_two, core), axis=0)
    grad_hidden = cotangent.astype(jnp.float32) + back_two
    grad_branch = grad_hidden.astype(jnp.bfloat16)
    grad_w_out = low(weight_grad(mixed, grad_branch))
    grad_mix = times_t(grad_branch, big_out).astype(jnp.bfloat16).reshape(length, heads, HEAD_DIM)
    grad_vals = jnp.einsum("hqk,qhd->khd", prob_low, grad_mix, preferred_element_type=jnp.float32)
    grad_prob = jnp.einsum("qhd,khd->hqk", grad_mix, vals, preferred_element_type=jnp.float32)
    inner = jnp.sum(prob * grad_prob, axis=-1, keepdims=True)
    grad_scores = (prob * (grad_prob - inner)).astype(jnp.bfloat16)
    grad_queries = factor * jnp.einsum(
        "hqk,khd->qhd", grad_scores, keys, preferred_element_type=jnp.float32
    )
    grad_keys = factor * jnp.einsum(
        "hqk,qhd->khd", grad_scores, queries, preferred_element_type=jnp.float32
    )
    grad_packed = jnp.stack([grad_queries, grad_keys, grad_vals], axis=1)
    grad_packed = grad_packed.astype(jnp.bfloat16).reshape(length, -1)
    grad_attn = jnp.concatenate([low(weight_grad(grad_packed, normed_one)), grad_w_out], axis=0)

    gate_up_sent, gate_up_state = middle_rows(after(gate_up_state, grad_attn))
    grad_attn = after(grad_attn, gate_up_sent)
    attn_state = start_rows(grad_attn, 4)
    active = after(active, grad_attn)
    grad_packed = after(grad_packed, grad_attn)
    grad_one = times(grad_packed, big_qkv)
    grad_one = pick(grad_one, core) + swap(pick(grad_one, 1 - core))
    ffn = times(active, big_down)
    ffn_mine = pick(ffn, core) + swap(pick(ffn, 1 - core))
    output = (pick(hidden_rows, core) + ffn_mine).astype(jnp.bfloat16)
    unit_mine = pick(unit_one, core)
    back_one = norm_rows_back(grad_one, unit_mine, pick(rescale_one, core), gains[0])
    gain_one = jnp.sum(grad_one * unit_mine, axis=0)
    grad_rows = (pick(grad_hidden, core) + back_one).astype(jnp.bfloat16)

    gate_up_state = after(gate_up_state, (output, grad_rows))
    parts, gate_up_own, gate_up_got = start_end_cols(end_rows(gate_up_state))
    output = send_rows(after(output, parts))
    _, attn_state = middle_rows(after(attn_state, (parts, down_rows)))
    mine_down = lax.psum_scatter(down_rows, "col", scatter_dimension=0, tiled=True)
    attn_state = after(attn_state, (gate_up_got, output))
    attn_parts, attn_own, attn_got = start_end_cols(end_rows(attn_state))
    gain_sums = jnp.stack([gain_one, gain_two], axis=0)
    gain_sums, grad_rows = after((gain_sums, grad_rows), attn_parts)
    grad_tokens = from_sequence(send_rows(grad_rows), core, col, length).astype(jnp.float32)
    gate_up_got, output, mine_down = after((gate_up_got, output, mine_down), attn_parts)
    output = from_sequence(output, core, col, length)
    mine_gate_up = end_cols(gate_up_own, gate_up_got)
    mine_attn = end_cols(attn_own, attn_got)

    gain_sums = gain_sums + swap(gain_sums)
    gain_sums = gain_sums + hop(gain_sums, "row", 1)
    gain_sums = gain_sums + hop(gain_sums, "row", 2)
    gain_mine = gain_sums[:, :features]
    for flip in range(1, 4):
        piece = gain_sums[:, flip * features : (flip + 1) * features]
        gain_mine = gain_mine + hop(piece, "col", flip)

    whole_attn = joined(mine_attn, core)
    return (
        output,
        grad_tokens,
        gain_mine[0],
        gain_mine[1],
        whole_attn[:3].transpose(2, 0, 1),
        whole_attn[3],
        joined(mine_gate_up, core).transpose(2, 0, 1),
        joined(mine_down, core)[0],
    )


def layer(tokens, segment_ids, *rest):
    sizes = (lax.axis_size("dp"), lax.axis_size("row"), lax.axis_size("col"))
    if sizes == (2, 4, 4) and tokens.shape[0] == 2 * segment_ids.shape[1]:
        return chip_local(tokens, segment_ids, *rest)
    return local(tokens, segment_ids, *rest)


def solution(mesh):
    in_specs = (
        P(("dp", "row"), "col"),
        P(("dp", "col"), None),
        P("col"),
        P("col"),
        P("col", None, "row"),
        P("row", "col"),
        P("col", None, "row"),
        P("row", "col"),
        P(("dp", "row"), "col"),
    )
    out_specs = (
        P(("dp", "row"), "col"),
        P(("dp", "row"), "col"),
        P("col"),
        P("col"),
        P("col", None, "row"),
        P("row", "col"),
        P("col", None, "row"),
        P("row", "col"),
    )
    return jax.shard_map(layer, mesh=mesh, in_specs=in_specs, out_specs=out_specs, check_vma=False)
```

```python
import jax
import jax.numpy as jnp
from jax import lax
from jax.experimental import pallas as pl
from jax.experimental.pallas import tpu as pltpu
from jax.sharding import PartitionSpec as P

D = 1024
HEAD_DIM = 64


EPS = 1e-06
MASKED = -1e30


def row_norm(values, gain_vec):
    squares = lax.psum(jnp.sum(values * values, axis=1), "col")
    rescale = lax.rsqrt(squares / D + EPS)
    unit_rows = values * rescale[:, None]
    return (unit_rows, rescale, (unit_rows * gain_vec[None, :]).astype(jnp.bfloat16))


def norm_backward(grad_normed, unit_rows, rescale, gain_vec):
    weighted = grad_normed * gain_vec[None, :]
    inner_sum = lax.psum(jnp.sum(weighted * unit_rows, axis=1), "col")
    grad_in = rescale[:, None] * (weighted - unit_rows * (inner_sum / D)[:, None])
    grad_gain = jnp.sum(grad_normed * unit_rows, axis=0)
    return (grad_in, grad_gain)


def project_up(normed, weight_block):
    gathered = lax.all_gather(normed, "row", axis=0, tiled=True)

    def term(begin_at):
        return jnp.dot(gathered, weight_block, preferred_element_type=jnp.float32)

    result = lax.psum_scatter(
        term(jnp.int32(0)),
        "col",
        scatter_dimension=0,
        tiled=True,
    )
    return (gathered, result.astype(jnp.bfloat16))


def project_down(values, weight_block):
    gathered = lax.all_gather(values, "col", axis=0, tiled=True)

    def term(begin_at):
        return jnp.dot(gathered, weight_block, preferred_element_type=jnp.float32)

    result = lax.psum_scatter(
        term(jnp.int32(0)),
        "row",
        scatter_dimension=0,
        tiled=True,
    )
    return (gathered, result)


def back_down(grad_rows, weight_block):
    gathered = lax.all_gather(grad_rows, "row", axis=0, tiled=True)

    def term(begin_at):
        return lax.dot_general(
            gathered, weight_block, (((1,), (1,)), ((), ())), preferred_element_type=jnp.float32
        )

    result = lax.psum_scatter(
        term(jnp.int32(0)),
        "col",
        scatter_dimension=0,
        tiled=True,
    )
    return (gathered, result.astype(jnp.bfloat16))


def back_up(grad_cols, weight_block):
    gathered = lax.all_gather(grad_cols, "col", axis=0, tiled=True)

    def term(begin_at):
        return lax.dot_general(
            gathered, weight_block, (((1,), (1,)), ((), ())), preferred_element_type=jnp.float32
        )

    result = lax.psum_scatter(
        term(jnp.int32(0)),
        "row",
        scatter_dimension=0,
        tiled=True,
    )
    return (gathered, result)


def weight_grad(left_rows, right_rows):
    return lax.dot_general(
        left_rows, right_rows, (((0,), (0,)), ((), ())), preferred_element_type=jnp.float32
    )


def block_scores(queries, keys_all, query_segment, key_segment, query_place):
    raw = jnp.einsum(
        "qhd,khd->hqk", queries, keys_all, preferred_element_type=jnp.float32
    ) * HEAD_DIM ** (-0.5)
    key_place = lax.broadcasted_iota(jnp.int32, (1, keys_all.shape[0]), 1)
    allowed = (query_segment[:, None] == key_segment[None, :]) & (key_place <= query_place[:, None])
    return jnp.where(allowed[None], raw, MASKED)


def split_blocks(queries, segment):
    length = queries.shape[0]
    block_rows = min(512, length)
    blocks = length // block_rows
    place = jnp.arange(length, dtype=jnp.int32).reshape(blocks, block_rows)
    return (
        queries.reshape(blocks, block_rows, queries.shape[1], queries.shape[2]),
        segment.reshape(blocks, block_rows),
        place,
    )


def attend_forward(queries, keys_all, values_all, segment):
    query_blocks, segment_blocks, place_blocks = split_blocks(queries, segment)

    def one_block(item):
        query_rows, query_segment, query_place = item
        scores = block_scores(query_rows, keys_all, query_segment, segment, query_place)
        row_max = jnp.max(scores, axis=-1, keepdims=True)
        expo = jnp.exp(scores - row_max)
        row_total = jnp.sum(expo, axis=-1, keepdims=True)
        prob_rows = (expo / row_total).astype(jnp.bfloat16)
        mixed = jnp.einsum(
            "hqk,khd->qhd", prob_rows, values_all, preferred_element_type=jnp.float32
        )
        return (mixed, row_max[..., 0] + jnp.log(row_total[..., 0]))

    mixed, log_total = lax.map(one_block, (query_blocks, segment_blocks, place_blocks))
    return (mixed.reshape(queries.shape[0], -1).astype(jnp.bfloat16), log_total)


def attend_backward(queries, keys_all, values_all, segment, log_total, grad_mix):
    query_blocks, segment_blocks, place_blocks = split_blocks(queries, segment)
    grad_blocks = grad_mix.reshape(query_blocks.shape)
    factor = HEAD_DIM ** (-0.5)

    def one_block(carry, item):
        key_acc, value_acc = carry
        query_rows, query_segment, query_place, log_rows, grad_rows = item
        scores = block_scores(query_rows, keys_all, query_segment, segment, query_place)
        prob_rows = jnp.exp(scores - log_rows[..., None])
        value_acc = value_acc + jnp.einsum(
            "hqk,qhd->khd",
            prob_rows.astype(jnp.bfloat16),
            grad_rows,
            preferred_element_type=jnp.float32,
        )
        grad_prob = jnp.einsum(
            "qhd,khd->hqk", grad_rows, values_all, preferred_element_type=jnp.float32
        )
        grad_scores = (
            prob_rows * (grad_prob - jnp.sum(prob_rows * grad_prob, axis=-1, keepdims=True))
        ).astype(jnp.bfloat16)
        grad_query = (
            jnp.einsum("hqk,khd->qhd", grad_scores, keys_all, preferred_element_type=jnp.float32)
            * factor
        )
        key_acc = (
            key_acc
            + jnp.einsum(
                "hqk,qhd->khd", grad_scores, query_rows, preferred_element_type=jnp.float32
            )
            * factor
        )
        return ((key_acc, value_acc), grad_query)

    zeros_like_keys = jnp.zeros(keys_all.shape, jnp.float32)
    (grad_keys, grad_values), grad_queries = lax.scan(
        one_block,
        (zeros_like_keys, zeros_like_keys),
        (query_blocks, segment_blocks, place_blocks, log_total, grad_blocks),
    )
    grad_queries = grad_queries.reshape(queries.shape)
    return jnp.stack([grad_queries, grad_keys, grad_values], axis=1).astype(jnp.bfloat16)


def local(tokens, segment_ids, gain_attn, gain_ffn, w_qkv, w_out, w_gate_up, w_down, grad_out):
    values = tokens.astype(jnp.float32)
    head_cols = w_qkv.shape[2]
    heads_here = head_cols // HEAD_DIM
    hidden_here = w_gate_up.shape[2]
    qkv_block = w_qkv.reshape(w_qkv.shape[0], 3 * head_cols)
    gate_up_block = w_gate_up.reshape(w_gate_up.shape[0], 2 * hidden_here)
    seq_count, seq_length = segment_ids.shape
    unit_one, rescale_one, normed_one = row_norm(values, gain_attn)
    gathered_one, packed = project_up(normed_one, qkv_block)
    packed = packed.reshape(-1, 3, heads_here, HEAD_DIM)
    mix_parts, log_parts = ([], [])
    for index in range(seq_count):
        rows_here = packed[index * seq_length : (index + 1) * seq_length]
        mixed, log_total = attend_forward(
            rows_here[:, 0], rows_here[:, 1], rows_here[:, 2], segment_ids[index]
        )
        mix_parts.append(mixed)
        log_parts.append(log_total)
    attn_mix = jnp.concatenate(mix_parts, axis=0)
    gathered_mix, attn_branch = project_down(attn_mix, w_out)
    hidden = values + attn_branch
    unit_two, rescale_two, normed_two = row_norm(hidden, gain_ffn)
    gathered_two, gate_up = project_up(normed_two, gate_up_block)
    gate_vals = gate_up[:, :hidden_here].astype(jnp.float32)
    up_vals = gate_up[:, hidden_here:].astype(jnp.float32)
    sigmoid_gate = jax.nn.sigmoid(gate_vals)
    silu_gate = gate_vals * sigmoid_gate
    active = (silu_gate * up_vals).astype(jnp.bfloat16)
    gathered_act, ffn_branch = project_down(active, w_down)
    output = (hidden + ffn_branch).astype(jnp.bfloat16)
    grad_rows_out, grad_active = back_down(grad_out, w_down)
    grad_down = weight_grad(gathered_act, grad_rows_out)
    grad_act_f = grad_active.astype(jnp.float32)
    grad_gate = grad_act_f * up_vals * sigmoid_gate * (1.0 + gate_vals * (1.0 - sigmoid_gate))
    grad_up = grad_act_f * silu_gate
    grad_gate_up_rows = jnp.concatenate([grad_gate, grad_up], axis=1).astype(jnp.bfloat16)
    grad_cols_two, grad_normed_two = back_up(grad_gate_up_rows, gate_up_block)
    grad_gate_up = weight_grad(gathered_two, grad_cols_two).reshape(w_gate_up.shape)
    grad_hidden_norm, grad_gain_two = norm_backward(
        grad_normed_two, unit_two, rescale_two, gain_ffn
    )
    grad_hidden = grad_out.astype(jnp.float32) + grad_hidden_norm
    grad_rows_hidden, grad_mix = back_down(grad_hidden.astype(jnp.bfloat16), w_out)
    grad_out_weight = weight_grad(gathered_mix, grad_rows_hidden)
    grad_mix = grad_mix.reshape(-1, heads_here, HEAD_DIM)
    grad_parts = []
    for index in range(seq_count):
        rows_here = packed[index * seq_length : (index + 1) * seq_length]
        grad_parts.append(
            attend_backward(
                rows_here[:, 0],
                rows_here[:, 1],
                rows_here[:, 2],
                segment_ids[index],
                log_parts[index],
                grad_mix[index * seq_length : (index + 1) * seq_length],
            )
        )
    grad_packed = jnp.concatenate(grad_parts, axis=0).reshape(-1, 3 * head_cols)
    grad_cols_one, grad_normed_one = back_up(grad_packed, qkv_block)
    grad_qkv = weight_grad(gathered_one, grad_cols_one).reshape(w_qkv.shape)
    grad_input_norm, grad_gain_one = norm_backward(
        grad_normed_one, unit_one, rescale_one, gain_attn
    )
    grad_tokens = grad_hidden + grad_input_norm
    summed = lax.psum((grad_qkv, grad_out_weight, grad_gate_up, grad_down), "dp")
    gains = lax.psum((grad_gain_one, grad_gain_two), ("dp", "row"))
    return (output, grad_tokens, gains[0], gains[1], summed[0], summed[1], summed[2], summed[3])


def swap(values):
    return lax.ppermute(values, "dp", [(0, 1), (1, 0)])


def hop(values, axis, flip):
    return lax.ppermute(values, axis, [(at, at ^ flip) for at in range(lax.axis_size(axis))])


def after(values, first):
    return lax.optimization_barrier((values, first))[0]


def by_core(core, mine, other, axis=0):
    first = jnp.where(core == 0, mine, other)
    second = jnp.where(core == 0, other, mine)
    return jnp.concatenate([first, second], axis=axis)


def pick(values, core, axis=0):
    half = values.shape[axis] // 2
    return lax.dynamic_slice_in_dim(values, core * half, half, axis)


def send_chunks(values, core, col, seq_length):
    seqs = values.shape[0] // seq_length
    parts = values.reshape(seqs, seq_length, -1)
    mine = pick(parts, core, 1)
    other = swap(pick(parts, 1 - core, 1))
    chunks = by_core(core, mine, other)
    got = []
    for flip in range(4):
        chunk = lax.dynamic_index_in_dim(chunks, col ^ flip, 0, keepdims=False)
        got.append(hop(chunk, "col", flip) if flip else chunk)
    return got


def to_sequence(got, core):
    rows = jnp.concatenate(got, axis=1)
    return by_core(core, rows, swap(rows))


def send_rows(rows):
    width = rows.shape[1] // 4
    parts = [rows[:, at * width : (at + 1) * width] for at in range(4)]
    return [parts[0]] + [hop(parts[flip], "col", flip) for flip in range(1, 4)]


def from_sequence(got, core, col, seq_length):
    got = jnp.stack(got, axis=0)
    seqs = 2

    def of_core(which):
        picked = [
            lax.dynamic_index_in_dim(got, (which * seqs + at) ^ col, 0, False) for at in range(seqs)
        ]
        return jnp.stack(picked)

    mine, other = (of_core(core), of_core(1 - core))
    return by_core(core, mine, swap(other), 1).reshape(seqs * seq_length, -1)


def times(left, right):
    return jnp.dot(left, right, preferred_element_type=jnp.float32)


def times_t(left, right):
    return lax.dot_general(
        left, right, (((1,), (1,)), ((), ())), preferred_element_type=jnp.float32
    )


def norm_rows(values):
    rescale = lax.rsqrt(jnp.mean(values * values, axis=1) + EPS)[:, None]
    return (values * rescale, rescale)


def norm_rows_back(grad_normed, unit_rows, rescale, gain_vec):
    weighted = grad_normed * gain_vec[None, :]
    inner = jnp.sum(weighted * unit_rows, axis=1, keepdims=True) / D
    return rescale * (weighted - unit_rows * inner)


def join_blocks(*refs):
    blocks, wholes = (refs[:16], refs[16:])
    _, rows, width = blocks[0].shape
    for at, block in enumerate(blocks):
        line, place = divmod(at, 4)
        kind = 0
        for whole in wholes:
            part = block[kind : kind + whole.shape[0]]
            kind += whole.shape[0]
            whole[:, line * rows : (line + 1) * rows, place * width : (place + 1) * width] = part


def spread_weights(block, first_cols=None, first_rows=None):
    grid = [[None] * 4 for _ in range(4)]
    block_cols = block if first_cols is None else after(block, first_cols)
    block_rows = block if first_rows is None else after(block, first_rows)
    near = hop(block_cols, "col", 1)
    far = hop(block_cols, "col", 3)
    grid[0] = [block_rows, near, hop(near, "col", 3), far]
    for at in (0, 1, 3, 2):
        grid[1][at] = hop(grid[0][at], "row", 1)
        grid[2][at] = hop(grid[0][at], "row", 2)
    for at in range(4):
        if at < 2:
            grid[3][at] = hop(grid[1][at], "row", 2)
        else:
            grid[3][at] = hop(grid[2][at], "row", 1)
    return grid


def join_weights(grid, splits):
    _, rows, width = grid[0][0].shape
    shapes = [jax.ShapeDtypeStruct((at, 4 * rows, 4 * width), jnp.bfloat16) for at in splits]
    wholes = pl.pallas_call(join_blocks, out_shape=shapes)(*[b for line in grid for b in line])
    return [whole.reshape(-1, 4 * width) for whole in wholes]


def wide(values):
    return values.astype(jnp.float32)


def low(values):
    return values.astype(jnp.bfloat16)


def start_rows(grad, kinds):
    grid = low(grad).reshape(kinds, 2, 2, -1, grad.shape[1])
    half = grad.shape[1] // 2
    left, right = (grid[..., :half], grid[..., half:])
    got = hop(left[:, 1], "row", 2)
    got_r = hop(right[:, :, 1], "row", 1)
    return (left, right, got, got_r)


def middle_rows(state):
    left, right, got, got_r = state
    sent = low(wide(left[:, 0, 1]) + wide(got[:, 1]))
    sent_r = low(wide(right[:, 1, 0]) + wide(got_r[:, 1]))
    return ((sent, sent_r), state + (hop(sent, "row", 1), hop(sent_r, "row", 2)))


def end_rows(state):
    left, right, got, got_r, last, last_r = state
    sums = wide(left[:, 0, 0]) + wide(got[:, 0]) + wide(last)
    sums_r = wide(right[:, 0, 0]) + wide(got_r[:, 0]) + wide(last_r)
    return (sums, sums_r)


def relay_cols(parts):
    own, first, second, third = parts
    got = hop(jnp.stack([third, second]), "col", 3)
    return (own, first, got)


def relay_last(state):
    own, first, got = state
    sent = low(wide(first) + wide(got[1]))
    return (sent, (own, got[0], hop(sent, "col", 1)))


def relay_sum(state):
    own, got, last = state
    return wide(own) + wide(got) + wide(last)


def split_cols(state):
    sums, sums_r = state
    width = sums.shape[-1] // 2
    parts = [low(sums[..., width:]), low(sums_r[..., :width]), low(sums_r[..., width:])]
    return [sums[..., :width]] + parts


def send_cols(parts):
    return [hop(parts[flip], "col", flip) for flip in (1, 2, 3)]


def end_cols(total, got):
    return total + wide(got[0]) + wide(got[1]) + wide(got[2])


def start_cols(grad):
    width = grad.shape[1] // 4
    return relay_cols([low(grad[:, at * width : (at + 1) * width]) for at in range(4)])


def join_halves(core_ref, mine, other, whole):
    rows = mine.shape[1]
    for at in range(2):
        part = slice(at * rows, (at + 1) * rows)

        @pl.when(core_ref[0] == at)
        def _():
            whole[:, part, :] = mine[...]

        @pl.when(core_ref[0] != at)
        def _():
            whole[:, part, :] = other[...].astype(jnp.float32)


def joined(mine, core):
    kinds, rows, width = mine.shape
    mine_low = low(mine)
    vmem = pl.BlockSpec(memory_space=pltpu.VMEM)
    return pl.pallas_call(
        join_halves,
        out_shape=jax.ShapeDtypeStruct((kinds, 2 * rows, width), jnp.float32),
        in_specs=[pl.BlockSpec(memory_space=pltpu.SMEM), vmem, vmem],
        out_specs=vmem,
    )(core[None], mine, swap(mine_low))


def chip_local(tokens, segment_ids, gain_attn, gain_ffn, w_qkv, w_out, w_gate_up, w_down, grad_out):
    core = lax.axis_index("dp")
    col = lax.axis_index("col")
    length = segment_ids.shape[1]
    features = w_qkv.shape[0]
    head_cols = w_qkv.shape[2] // 2
    heads = 4 * head_cols // HEAD_DIM
    factor = HEAD_DIM ** (-0.5)

    token_chunks = send_chunks(tokens, core, col, length)
    attn_block = jnp.concatenate(
        [pick(w_qkv, core, 2).transpose(1, 2, 0), pick(w_out, core)[None]], axis=0
    )
    attn_grid = spread_weights(attn_block)
    token_chunks = after(token_chunks, attn_grid[0])
    values = to_sequence(token_chunks, core).astype(jnp.float32)
    gains = jnp.stack([gain_attn, gain_ffn], axis=0)
    gains = jnp.concatenate([gains] + [hop(gains, "col", flip) for flip in range(1, 4)], axis=1)
    corner = [(4 * at + to, 4 * to + at) for at in range(4) for to in range(4)]
    segment_rows = lax.ppermute(segment_ids, ("row", "col"), corner)
    segment_rows = by_core(core, segment_rows, swap(segment_rows))
    segment = lax.dynamic_index_in_dim(segment_rows, col, 0, keepdims=False)
    ffn_block = jnp.concatenate(
        [pick(w_gate_up, core, 2).transpose(1, 2, 0), pick(w_down, core)[None]], axis=0
    )
    ffn_grid = spread_weights(ffn_block, attn_grid[0], attn_grid[1] + attn_grid[2])
    big_qkv, big_out = after(join_weights(attn_grid, (3, 1)), ffn_grid[0])
    grad_chunks = send_chunks(after(grad_out, ffn_grid[0]), core, col, length)
    big_gate_up, big_down = join_weights(ffn_grid, (2, 1))
    cotangent = to_sequence(after(grad_chunks, ffn_grid[1] + ffn_grid[2]), core)

    unit_one, rescale_one = norm_rows(values)
    normed_one = (unit_one * gains[0][None, :]).astype(jnp.bfloat16)
    packed = times_t(normed_one, big_qkv).astype(jnp.bfloat16)
    packed = packed.reshape(length, 3, heads, HEAD_DIM)
    queries, keys, vals = (packed[:, 0], packed[:, 1], packed[:, 2])
    scores = jnp.einsum("qhd,khd->hqk", queries, keys, preferred_element_type=jnp.float32) * factor
    spot = jnp.arange(length, dtype=jnp.int32)
    live = (segment[:, None] == segment[None, :]) & (spot[None, :] <= spot[:, None])
    scores = jnp.where(live[None], scores, MASKED)
    expo = jnp.exp(scores - jnp.max(scores, axis=-1, keepdims=True))
    prob = expo / jnp.sum(expo, axis=-1, keepdims=True)
    prob_low = prob.astype(jnp.bfloat16)
    mixed = jnp.einsum("hqk,khd->qhd", prob_low, vals, preferred_element_type=jnp.float32)
    mixed = mixed.reshape(length, -1).astype(jnp.bfloat16)
    branch = times(mixed, big_out)
    hidden_rows = values + (branch + swap(branch))
    unit_two, rescale_two = norm_rows(hidden_rows)
    normed_two = (unit_two * gains[1][None, :]).astype(jnp.bfloat16)
    gate_up = times_t(normed_two, big_gate_up).astype(jnp.bfloat16)
    half = gate_up.shape[1] // 2
    gate_vals = gate_up[:, :half].astype(jnp.float32)
    up_vals = gate_up[:, half:].astype(jnp.float32)
    sigmoid_gate = jax.nn.sigmoid(gate_vals)
    silu_gate = gate_vals * sigmoid_gate
    active = (silu_gate * up_vals).astype(jnp.bfloat16)

    down_state = start_cols(weight_grad(active, cotangent))
    grad_act = wide(low(times_t(cotangent, big_down)))
    grad_gate = grad_act * up_vals * sigmoid_gate * (1.0 + gate_vals * (1.0 - sigmoid_gate))
    grad_up = grad_act * silu_gate
    grad_gu = jnp.concatenate([grad_gate, grad_up], axis=1).astype(jnp.bfloat16)
    grad_two = times(grad_gu, big_gate_up)
    grad_two = grad_two + swap(grad_two)
    gate_up_state = start_rows(weight_grad(grad_gu, normed_two), 2)
    back_two = norm_rows_back(grad_two, unit_two, rescale_two, gains[1])
    gain_two = jnp.sum(pick(grad_two * unit_two, core), axis=0)
    grad_hidden = cotangent.astype(jnp.float32) + back_two
    grad_branch = grad_hidden.astype(jnp.bfloat16)
    grad_w_out = low(weight_grad(mixed, grad_branch))
    grad_mix = times_t(grad_branch, big_out).astype(jnp.bfloat16).reshape(length, heads, HEAD_DIM)
    grad_vals = jnp.einsum("hqk,qhd->khd", prob_low, grad_mix, preferred_element_type=jnp.float32)
    grad_prob = jnp.einsum("qhd,khd->hqk", grad_mix, vals, preferred_element_type=jnp.float32)
    inner = jnp.sum(prob * grad_prob, axis=-1, keepdims=True)
    grad_scores = (prob * (grad_prob - inner)).astype(jnp.bfloat16)
    grad_queries = factor * jnp.einsum(
        "hqk,khd->qhd", grad_scores, keys, preferred_element_type=jnp.float32
    )
    grad_keys = factor * jnp.einsum(
        "hqk,qhd->khd", grad_scores, queries, preferred_element_type=jnp.float32
    )
    grad_packed = jnp.stack([grad_queries, grad_keys, grad_vals], axis=1)
    grad_packed = grad_packed.astype(jnp.bfloat16).reshape(length, -1)
    grad_attn = jnp.concatenate([low(weight_grad(grad_packed, normed_one)), grad_w_out], axis=0)

    gate_up_sent, gate_up_state = middle_rows(after(gate_up_state, grad_attn))
    grad_attn = after(grad_attn, gate_up_sent)
    attn_state = start_rows(grad_attn, 4)
    down_sent, down_state = relay_last(after(down_state, grad_attn))
    active = after(active, grad_attn)
    grad_packed = after(grad_packed, grad_attn)
    grad_one = times(grad_packed, big_qkv)
    grad_one = pick(grad_one, core) + swap(pick(grad_one, 1 - core))
    ffn = times(active, big_down)
    ffn_mine = pick(ffn, core) + swap(pick(ffn, 1 - core))
    output = (pick(hidden_rows, core) + ffn_mine).astype(jnp.bfloat16)
    unit_mine = pick(unit_one, core)
    back_one = norm_rows_back(grad_one, unit_mine, pick(rescale_one, core), gains[0])
    gain_one = jnp.sum(grad_one * unit_mine, axis=0)
    grad_rows = (pick(grad_hidden, core) + back_one).astype(jnp.bfloat16)

    gate_up_state = after(gate_up_state, (output, grad_rows))
    parts = split_cols(end_rows(gate_up_state))
    gate_up_state = relay_cols(parts)
    output = send_rows(after(output, parts))
    down_rows = low(relay_sum(after(down_state, parts)))
    down_state = start_rows(down_rows, 1)
    attn_state = after(attn_state, down_rows)
    attn_sent, attn_state = middle_rows(attn_state)
    gate_up_state = after(gate_up_state, attn_sent)
    gate_up_sent, gate_up_state = relay_last(gate_up_state)
    down_sent, down_state = middle_rows(after(down_state, gate_up_sent))
    attn_state = after(attn_state, down_sent)
    attn_parts = split_cols(end_rows(attn_state))
    attn_got = send_cols(attn_parts)
    gain_sums = jnp.stack([gain_one, gain_two], axis=0)
    gain_sums, grad_rows = after((gain_sums, grad_rows), attn_parts)
    grad_tokens = from_sequence(send_rows(grad_rows), core, col, length).astype(jnp.float32)
    gate_up_state, down_state, output = after((gate_up_state, down_state, output), attn_parts)
    output = from_sequence(output, core, col, length)
    mine_gate_up = relay_sum(gate_up_state)
    mine_down = jnp.concatenate(end_rows(down_state), axis=-1)
    mine_attn = end_cols(attn_parts[0], attn_got)

    gain_sums = gain_sums + swap(gain_sums)
    gain_sums = gain_sums + hop(gain_sums, "row", 1)
    gain_sums = gain_sums + hop(gain_sums, "row", 2)
    gain_mine = gain_sums[:, :features]
    for flip in range(1, 4):
        piece = gain_sums[:, flip * features : (flip + 1) * features]
        gain_mine = gain_mine + hop(piece, "col", flip)

    whole_attn = joined(mine_attn, core)
    return (
        output,
        grad_tokens,
        gain_mine[0],
        gain_mine[1],
        whole_attn[:3].transpose(2, 0, 1),
        whole_attn[3],
        joined(mine_gate_up, core).transpose(2, 0, 1),
        joined(mine_down, core)[0],
    )


def layer(tokens, segment_ids, *rest):
    sizes = (lax.axis_size("dp"), lax.axis_size("row"), lax.axis_size("col"))
    if sizes == (2, 4, 4) and tokens.shape[0] == 2 * segment_ids.shape[1]:
        return chip_local(tokens, segment_ids, *rest)
    return local(tokens, segment_ids, *rest)


def solution(mesh):
    in_specs = (
        P(("dp", "row"), "col"),
        P(("dp", "col"), None),
        P("col"),
        P("col"),
        P("col", None, "row"),
        P("row", "col"),
        P("col", None, "row"),
        P("row", "col"),
        P(("dp", "row"), "col"),
    )
    out_specs = (
        P(("dp", "row"), "col"),
        P(("dp", "row"), "col"),
        P("col"),
        P("col"),
        P("col", None, "row"),
        P("row", "col"),
        P("col", None, "row"),
        P("row", "col"),
    )
    return jax.shard_map(layer, mesh=mesh, in_specs=in_specs, out_specs=out_specs, check_vma=False)
```

```python
import jax
import jax.numpy as jnp
from jax import lax
from jax.experimental import pallas as pl
from jax.experimental.pallas import tpu as pltpu
from jax.sharding import PartitionSpec as P

D = 1024
HEAD_DIM = 64


EPS = 1e-06
MASKED = -1e30


def row_norm(values, gain_vec):
    squares = lax.psum(jnp.sum(values * values, axis=1), "col")
    rescale = lax.rsqrt(squares / D + EPS)
    unit_rows = values * rescale[:, None]
    return (unit_rows, rescale, (unit_rows * gain_vec[None, :]).astype(jnp.bfloat16))


def norm_backward(grad_normed, unit_rows, rescale, gain_vec):
    weighted = grad_normed * gain_vec[None, :]
    inner_sum = lax.psum(jnp.sum(weighted * unit_rows, axis=1), "col")
    grad_in = rescale[:, None] * (weighted - unit_rows * (inner_sum / D)[:, None])
    grad_gain = jnp.sum(grad_normed * unit_rows, axis=0)
    return (grad_in, grad_gain)


def project_up(normed, weight_block):
    gathered = lax.all_gather(normed, "row", axis=0, tiled=True)

    def term(begin_at):
        return jnp.dot(gathered, weight_block, preferred_element_type=jnp.float32)

    result = lax.psum_scatter(
        term(jnp.int32(0)),
        "col",
        scatter_dimension=0,
        tiled=True,
    )
    return (gathered, result.astype(jnp.bfloat16))


def project_down(values, weight_block):
    gathered = lax.all_gather(values, "col", axis=0, tiled=True)

    def term(begin_at):
        return jnp.dot(gathered, weight_block, preferred_element_type=jnp.float32)

    result = lax.psum_scatter(
        term(jnp.int32(0)),
        "row",
        scatter_dimension=0,
        tiled=True,
    )
    return (gathered, result)


def back_down(grad_rows, weight_block):
    gathered = lax.all_gather(grad_rows, "row", axis=0, tiled=True)

    def term(begin_at):
        return lax.dot_general(
            gathered, weight_block, (((1,), (1,)), ((), ())), preferred_element_type=jnp.float32
        )

    result = lax.psum_scatter(
        term(jnp.int32(0)),
        "col",
        scatter_dimension=0,
        tiled=True,
    )
    return (gathered, result.astype(jnp.bfloat16))


def back_up(grad_cols, weight_block):
    gathered = lax.all_gather(grad_cols, "col", axis=0, tiled=True)

    def term(begin_at):
        return lax.dot_general(
            gathered, weight_block, (((1,), (1,)), ((), ())), preferred_element_type=jnp.float32
        )

    result = lax.psum_scatter(
        term(jnp.int32(0)),
        "row",
        scatter_dimension=0,
        tiled=True,
    )
    return (gathered, result)


def weight_grad(left_rows, right_rows):
    return lax.dot_general(
        left_rows, right_rows, (((0,), (0,)), ((), ())), preferred_element_type=jnp.float32
    )


def block_scores(queries, keys_all, query_segment, key_segment, query_place):
    raw = jnp.einsum(
        "qhd,khd->hqk", queries, keys_all, preferred_element_type=jnp.float32
    ) * HEAD_DIM ** (-0.5)
    key_place = lax.broadcasted_iota(jnp.int32, (1, keys_all.shape[0]), 1)
    allowed = (query_segment[:, None] == key_segment[None, :]) & (key_place <= query_place[:, None])
    return jnp.where(allowed[None], raw, MASKED)


def split_blocks(queries, segment):
    length = queries.shape[0]
    block_rows = min(512, length)
    blocks = length // block_rows
    place = jnp.arange(length, dtype=jnp.int32).reshape(blocks, block_rows)
    return (
        queries.reshape(blocks, block_rows, queries.shape[1], queries.shape[2]),
        segment.reshape(blocks, block_rows),
        place,
    )


def attend_forward(queries, keys_all, values_all, segment):
    query_blocks, segment_blocks, place_blocks = split_blocks(queries, segment)

    def one_block(item):
        query_rows, query_segment, query_place = item
        scores = block_scores(query_rows, keys_all, query_segment, segment, query_place)
        row_max = jnp.max(scores, axis=-1, keepdims=True)
        expo = jnp.exp(scores - row_max)
        row_total = jnp.sum(expo, axis=-1, keepdims=True)
        prob_rows = (expo / row_total).astype(jnp.bfloat16)
        mixed = jnp.einsum(
            "hqk,khd->qhd", prob_rows, values_all, preferred_element_type=jnp.float32
        )
        return (mixed, row_max[..., 0] + jnp.log(row_total[..., 0]))

    mixed, log_total = lax.map(one_block, (query_blocks, segment_blocks, place_blocks))
    return (mixed.reshape(queries.shape[0], -1).astype(jnp.bfloat16), log_total)


def attend_backward(queries, keys_all, values_all, segment, log_total, grad_mix):
    query_blocks, segment_blocks, place_blocks = split_blocks(queries, segment)
    grad_blocks = grad_mix.reshape(query_blocks.shape)
    factor = HEAD_DIM ** (-0.5)

    def one_block(carry, item):
        key_acc, value_acc = carry
        query_rows, query_segment, query_place, log_rows, grad_rows = item
        scores = block_scores(query_rows, keys_all, query_segment, segment, query_place)
        prob_rows = jnp.exp(scores - log_rows[..., None])
        value_acc = value_acc + jnp.einsum(
            "hqk,qhd->khd",
            prob_rows.astype(jnp.bfloat16),
            grad_rows,
            preferred_element_type=jnp.float32,
        )
        grad_prob = jnp.einsum(
            "qhd,khd->hqk", grad_rows, values_all, preferred_element_type=jnp.float32
        )
        grad_scores = (
            prob_rows * (grad_prob - jnp.sum(prob_rows * grad_prob, axis=-1, keepdims=True))
        ).astype(jnp.bfloat16)
        grad_query = (
            jnp.einsum("hqk,khd->qhd", grad_scores, keys_all, preferred_element_type=jnp.float32)
            * factor
        )
        key_acc = (
            key_acc
            + jnp.einsum(
                "hqk,qhd->khd", grad_scores, query_rows, preferred_element_type=jnp.float32
            )
            * factor
        )
        return ((key_acc, value_acc), grad_query)

    zeros_like_keys = jnp.zeros(keys_all.shape, jnp.float32)
    (grad_keys, grad_values), grad_queries = lax.scan(
        one_block,
        (zeros_like_keys, zeros_like_keys),
        (query_blocks, segment_blocks, place_blocks, log_total, grad_blocks),
    )
    grad_queries = grad_queries.reshape(queries.shape)
    return jnp.stack([grad_queries, grad_keys, grad_values], axis=1).astype(jnp.bfloat16)


def local(tokens, segment_ids, gain_attn, gain_ffn, w_qkv, w_out, w_gate_up, w_down, grad_out):
    values = tokens.astype(jnp.float32)
    head_cols = w_qkv.shape[2]
    heads_here = head_cols // HEAD_DIM
    hidden_here = w_gate_up.shape[2]
    qkv_block = w_qkv.reshape(w_qkv.shape[0], 3 * head_cols)
    gate_up_block = w_gate_up.reshape(w_gate_up.shape[0], 2 * hidden_here)
    seq_count, seq_length = segment_ids.shape
    unit_one, rescale_one, normed_one = row_norm(values, gain_attn)
    gathered_one, packed = project_up(normed_one, qkv_block)
    packed = packed.reshape(-1, 3, heads_here, HEAD_DIM)
    mix_parts, log_parts = ([], [])
    for index in range(seq_count):
        rows_here = packed[index * seq_length : (index + 1) * seq_length]
        mixed, log_total = attend_forward(
            rows_here[:, 0], rows_here[:, 1], rows_here[:, 2], segment_ids[index]
        )
        mix_parts.append(mixed)
        log_parts.append(log_total)
    attn_mix = jnp.concatenate(mix_parts, axis=0)
    gathered_mix, attn_branch = project_down(attn_mix, w_out)
    hidden = values + attn_branch
    unit_two, rescale_two, normed_two = row_norm(hidden, gain_ffn)
    gathered_two, gate_up = project_up(normed_two, gate_up_block)
    gate_vals = gate_up[:, :hidden_here].astype(jnp.float32)
    up_vals = gate_up[:, hidden_here:].astype(jnp.float32)
    sigmoid_gate = jax.nn.sigmoid(gate_vals)
    silu_gate = gate_vals * sigmoid_gate
    active = (silu_gate * up_vals).astype(jnp.bfloat16)
    gathered_act, ffn_branch = project_down(active, w_down)
    output = (hidden + ffn_branch).astype(jnp.bfloat16)
    grad_rows_out, grad_active = back_down(grad_out, w_down)
    grad_down = weight_grad(gathered_act, grad_rows_out)
    grad_act_f = grad_active.astype(jnp.float32)
    grad_gate = grad_act_f * up_vals * sigmoid_gate * (1.0 + gate_vals * (1.0 - sigmoid_gate))
    grad_up = grad_act_f * silu_gate
    grad_gate_up_rows = jnp.concatenate([grad_gate, grad_up], axis=1).astype(jnp.bfloat16)
    grad_cols_two, grad_normed_two = back_up(grad_gate_up_rows, gate_up_block)
    grad_gate_up = weight_grad(gathered_two, grad_cols_two).reshape(w_gate_up.shape)
    grad_hidden_norm, grad_gain_two = norm_backward(
        grad_normed_two, unit_two, rescale_two, gain_ffn
    )
    grad_hidden = grad_out.astype(jnp.float32) + grad_hidden_norm
    grad_rows_hidden, grad_mix = back_down(grad_hidden.astype(jnp.bfloat16), w_out)
    grad_out_weight = weight_grad(gathered_mix, grad_rows_hidden)
    grad_mix = grad_mix.reshape(-1, heads_here, HEAD_DIM)
    grad_parts = []
    for index in range(seq_count):
        rows_here = packed[index * seq_length : (index + 1) * seq_length]
        grad_parts.append(
            attend_backward(
                rows_here[:, 0],
                rows_here[:, 1],
                rows_here[:, 2],
                segment_ids[index],
                log_parts[index],
                grad_mix[index * seq_length : (index + 1) * seq_length],
            )
        )
    grad_packed = jnp.concatenate(grad_parts, axis=0).reshape(-1, 3 * head_cols)
    grad_cols_one, grad_normed_one = back_up(grad_packed, qkv_block)
    grad_qkv = weight_grad(gathered_one, grad_cols_one).reshape(w_qkv.shape)
    grad_input_norm, grad_gain_one = norm_backward(
        grad_normed_one, unit_one, rescale_one, gain_attn
    )
    grad_tokens = grad_hidden + grad_input_norm
    summed = lax.psum((grad_qkv, grad_out_weight, grad_gate_up, grad_down), "dp")
    gains = lax.psum((grad_gain_one, grad_gain_two), ("dp", "row"))
    return (output, grad_tokens, gains[0], gains[1], summed[0], summed[1], summed[2], summed[3])


def swap(values):
    return lax.ppermute(values, "dp", [(0, 1), (1, 0)])


def hop(values, axis, flip):
    return lax.ppermute(values, axis, [(at, at ^ flip) for at in range(lax.axis_size(axis))])


def after(values, first):
    return lax.optimization_barrier((values, first))[0]


def by_core(core, mine, other, axis=0):
    first = jnp.where(core == 0, mine, other)
    second = jnp.where(core == 0, other, mine)
    return jnp.concatenate([first, second], axis=axis)


def pick(values, core, axis=0):
    half = values.shape[axis] // 2
    return lax.dynamic_slice_in_dim(values, core * half, half, axis)


def send_chunks(values, core, col, seq_length):
    seqs = values.shape[0] // seq_length
    parts = values.reshape(seqs, seq_length, -1)
    mine = pick(parts, core, 1)
    other = swap(pick(parts, 1 - core, 1))
    chunks = by_core(core, mine, other)
    got = []
    for flip in range(4):
        chunk = lax.dynamic_index_in_dim(chunks, col ^ flip, 0, keepdims=False)
        got.append(hop(chunk, "col", flip) if flip else chunk)
    return got


def to_sequence(got, core):
    rows = jnp.concatenate(got, axis=1)
    return by_core(core, rows, swap(rows))


def send_rows(rows):
    width = rows.shape[1] // 4
    parts = [rows[:, at * width : (at + 1) * width] for at in range(4)]
    return [parts[0]] + [hop(parts[flip], "col", flip) for flip in range(1, 4)]


def from_sequence(got, core, col, seq_length):
    got = jnp.stack(got, axis=0)
    seqs = 2

    def of_core(which):
        picked = [
            lax.dynamic_index_in_dim(got, (which * seqs + at) ^ col, 0, False) for at in range(seqs)
        ]
        return jnp.stack(picked)

    mine, other = (of_core(core), of_core(1 - core))
    return by_core(core, mine, swap(other), 1).reshape(seqs * seq_length, -1)


def times(left, right):
    return jnp.dot(left, right, preferred_element_type=jnp.float32)


def times_t(left, right):
    return lax.dot_general(
        left, right, (((1,), (1,)), ((), ())), preferred_element_type=jnp.float32
    )


def norm_rows(values):
    rescale = lax.rsqrt(jnp.mean(values * values, axis=1) + EPS)[:, None]
    return (values * rescale, rescale)


def norm_rows_back(grad_normed, unit_rows, rescale, gain_vec):
    weighted = grad_normed * gain_vec[None, :]
    inner = jnp.sum(weighted * unit_rows, axis=1, keepdims=True) / D
    return rescale * (weighted - unit_rows * inner)


def join_blocks(*refs):
    blocks, wholes = (refs[:16], refs[16:])
    _, rows, width = blocks[0].shape
    for at, block in enumerate(blocks):
        line, place = divmod(at, 4)
        kind = 0
        for whole in wholes:
            part = block[kind : kind + whole.shape[0]]
            kind += whole.shape[0]
            whole[:, line * rows : (line + 1) * rows, place * width : (place + 1) * width] = part


def spread_weights(block, first_cols=None, first_rows=None):
    grid = [[None] * 4 for _ in range(4)]
    block_cols = block if first_cols is None else after(block, first_cols)
    block_rows = block if first_rows is None else after(block, first_rows)
    near = hop(block_cols, "col", 1)
    far = hop(block_cols, "col", 3)
    grid[0] = [block_rows, near, hop(near, "col", 3), far]
    for at in (0, 1, 3, 2):
        grid[1][at] = hop(grid[0][at], "row", 1)
        grid[2][at] = hop(grid[0][at], "row", 2)
    for at in range(4):
        if at < 2:
            grid[3][at] = hop(grid[1][at], "row", 2)
        else:
            grid[3][at] = hop(grid[2][at], "row", 1)
    return grid


def join_weights(grid, splits):
    _, rows, width = grid[0][0].shape
    shapes = [jax.ShapeDtypeStruct((at, 4 * rows, 4 * width), jnp.bfloat16) for at in splits]
    wholes = pl.pallas_call(join_blocks, out_shape=shapes)(*[b for line in grid for b in line])
    return [whole.reshape(-1, 4 * width) for whole in wholes]


def wide(values):
    return values.astype(jnp.float32)


def low(values):
    return values.astype(jnp.bfloat16)


def start_rows(grad, kinds):
    grid = low(grad).reshape(kinds, 2, 2, -1, grad.shape[1])
    half = grad.shape[1] // 2
    left, right = (grid[..., :half], grid[..., half:])
    got = hop(left[:, 1], "row", 2)
    got_r = hop(right[:, :, 1], "row", 1)
    return (left, right, got, got_r)


def middle_rows(state):
    left, right, got, got_r = state
    sent = low(wide(left[:, 0, 1]) + wide(got[:, 1]))
    sent_r = low(wide(right[:, 1, 0]) + wide(got_r[:, 1]))
    return ((sent, sent_r), state + (hop(sent, "row", 1), hop(sent_r, "row", 2)))


def end_rows(state):
    left, right, got, got_r, last, last_r = state
    sums = wide(left[:, 0, 0]) + wide(got[:, 0]) + wide(last)
    sums_r = wide(right[:, 0, 0]) + wide(got_r[:, 0]) + wide(last_r)
    return (sums, sums_r)


def split_cols(state):
    sums, sums_r = state
    width = sums.shape[-1] // 2
    parts = [low(sums[..., width:]), low(sums_r[..., :width]), low(sums_r[..., width:])]
    return [sums[..., :width]] + parts


def send_cols(parts):
    return [hop(parts[flip], "col", flip) for flip in (1, 2, 3)]


def end_cols(total, got):
    return total + wide(got[0]) + wide(got[1]) + wide(got[2])


def start_cols(grad):
    width = grad.shape[1] // 4
    parts = [low(grad[:, at * width : (at + 1) * width]) for at in range(4)]
    return parts[:1] + send_cols(parts)


def join_halves(core_ref, mine, other, whole):
    rows = mine.shape[1]
    for at in range(2):
        part = slice(at * rows, (at + 1) * rows)

        @pl.when(core_ref[0] == at)
        def _():
            whole[:, part, :] = mine[...]

        @pl.when(core_ref[0] != at)
        def _():
            whole[:, part, :] = other[...].astype(jnp.float32)


def joined(mine, core):
    kinds, rows, width = mine.shape
    mine_low = low(mine)
    vmem = pl.BlockSpec(memory_space=pltpu.VMEM)
    return pl.pallas_call(
        join_halves,
        out_shape=jax.ShapeDtypeStruct((kinds, 2 * rows, width), jnp.float32),
        in_specs=[pl.BlockSpec(memory_space=pltpu.SMEM), vmem, vmem],
        out_specs=vmem,
    )(core[None], mine, swap(mine_low))


def chip_local(tokens, segment_ids, gain_attn, gain_ffn, w_qkv, w_out, w_gate_up, w_down, grad_out):
    core = lax.axis_index("dp")
    col = lax.axis_index("col")
    length = segment_ids.shape[1]
    features = w_qkv.shape[0]
    head_cols = w_qkv.shape[2] // 2
    heads = 4 * head_cols // HEAD_DIM
    factor = HEAD_DIM ** (-0.5)

    token_chunks = send_chunks(tokens, core, col, length)
    attn_block = jnp.concatenate(
        [pick(w_qkv, core, 2).transpose(1, 2, 0), pick(w_out, core)[None]], axis=0
    )
    attn_grid = spread_weights(attn_block)
    token_chunks = after(token_chunks, attn_grid[0])
    values = to_sequence(token_chunks, core).astype(jnp.float32)
    gains = jnp.stack([gain_attn, gain_ffn], axis=0)
    gains = jnp.concatenate([gains] + [hop(gains, "col", flip) for flip in range(1, 4)], axis=1)
    corner = [(4 * at + to, 4 * to + at) for at in range(4) for to in range(4)]
    segment_rows = lax.ppermute(segment_ids, ("row", "col"), corner)
    segment_rows = by_core(core, segment_rows, swap(segment_rows))
    segment = lax.dynamic_index_in_dim(segment_rows, col, 0, keepdims=False)
    ffn_block = jnp.concatenate(
        [pick(w_gate_up, core, 2).transpose(1, 2, 0), pick(w_down, core)[None]], axis=0
    )
    ffn_grid = spread_weights(ffn_block, attn_grid[0], attn_grid[1] + attn_grid[2])
    big_qkv, big_out = after(join_weights(attn_grid, (3, 1)), ffn_grid[0])
    grad_late = after(grad_out, ffn_grid[1] + ffn_grid[2])
    grad_chunks = send_chunks(grad_late, core, col, length)
    big_gate_up, big_down = join_weights(ffn_grid, (2, 1))
    cotangent = to_sequence(grad_chunks, core)

    unit_one, rescale_one = norm_rows(values)
    normed_one = (unit_one * gains[0][None, :]).astype(jnp.bfloat16)
    packed = times_t(normed_one, big_qkv).astype(jnp.bfloat16)
    packed = packed.reshape(length, 3, heads, HEAD_DIM)
    queries, keys, vals = (packed[:, 0], packed[:, 1], packed[:, 2])
    scores = jnp.einsum("qhd,khd->hqk", queries, keys, preferred_element_type=jnp.float32) * factor
    spot = jnp.arange(length, dtype=jnp.int32)
    live = (segment[:, None] == segment[None, :]) & (spot[None, :] <= spot[:, None])
    scores = jnp.where(live[None], scores, MASKED)
    expo = jnp.exp(scores - jnp.max(scores, axis=-1, keepdims=True))
    prob = expo / jnp.sum(expo, axis=-1, keepdims=True)
    prob_low = prob.astype(jnp.bfloat16)
    mixed = jnp.einsum("hqk,khd->qhd", prob_low, vals, preferred_element_type=jnp.float32)
    mixed = mixed.reshape(length, -1).astype(jnp.bfloat16)
    branch = times(mixed, big_out)
    hidden_rows = values + (branch + swap(branch))
    unit_two, rescale_two = norm_rows(hidden_rows)
    normed_two = (unit_two * gains[1][None, :]).astype(jnp.bfloat16)
    gate_up = times_t(normed_two, big_gate_up).astype(jnp.bfloat16)
    half = gate_up.shape[1] // 2
    gate_vals = gate_up[:, :half].astype(jnp.float32)
    up_vals = gate_up[:, half:].astype(jnp.float32)
    sigmoid_gate = jax.nn.sigmoid(gate_vals)
    silu_gate = gate_vals * sigmoid_gate
    active = (silu_gate * up_vals).astype(jnp.bfloat16)

    down_state = start_cols(weight_grad(active, cotangent))
    grad_act = wide(low(times_t(cotangent, big_down)))
    grad_gate = grad_act * up_vals * sigmoid_gate * (1.0 + gate_vals * (1.0 - sigmoid_gate))
    grad_up = grad_act * silu_gate
    grad_gu = jnp.concatenate([grad_gate, grad_up], axis=1).astype(jnp.bfloat16)
    grad_two = times(grad_gu, big_gate_up)
    grad_two = grad_two + swap(grad_two)
    gate_up_state = start_rows(weight_grad(grad_gu, normed_two), 2)
    back_two = norm_rows_back(grad_two, unit_two, rescale_two, gains[1])
    gain_two = jnp.sum(pick(grad_two * unit_two, core), axis=0)
    grad_hidden = cotangent.astype(jnp.float32) + back_two
    grad_branch = grad_hidden.astype(jnp.bfloat16)
    grad_w_out = low(weight_grad(mixed, grad_branch))
    grad_mix = times_t(grad_branch, big_out).astype(jnp.bfloat16).reshape(length, heads, HEAD_DIM)
    grad_vals = jnp.einsum("hqk,qhd->khd", prob_low, grad_mix, preferred_element_type=jnp.float32)
    grad_prob = jnp.einsum("qhd,khd->hqk", grad_mix, vals, preferred_element_type=jnp.float32)
    inner = jnp.sum(prob * grad_prob, axis=-1, keepdims=True)
    grad_scores = (prob * (grad_prob - inner)).astype(jnp.bfloat16)
    grad_queries = factor * jnp.einsum(
        "hqk,khd->qhd", grad_scores, keys, preferred_element_type=jnp.float32
    )
    grad_keys = factor * jnp.einsum(
        "hqk,qhd->khd", grad_scores, queries, preferred_element_type=jnp.float32
    )
    grad_packed = jnp.stack([grad_queries, grad_keys, grad_vals], axis=1)
    grad_packed = grad_packed.astype(jnp.bfloat16).reshape(length, -1)
    grad_attn = jnp.concatenate([low(weight_grad(grad_packed, normed_one)), grad_w_out], axis=0)

    gate_up_sent, gate_up_state = middle_rows(after(gate_up_state, grad_attn))
    grad_attn = after(grad_attn, gate_up_sent)
    attn_state = start_rows(grad_attn, 4)
    active = after(active, grad_attn)
    grad_packed = after(grad_packed, grad_attn)
    grad_one = times(grad_packed, big_qkv)
    grad_one = pick(grad_one, core) + swap(pick(grad_one, 1 - core))
    ffn = times(active, big_down)
    ffn_mine = pick(ffn, core) + swap(pick(ffn, 1 - core))
    output = (pick(hidden_rows, core) + ffn_mine).astype(jnp.bfloat16)
    unit_mine = pick(unit_one, core)
    back_one = norm_rows_back(grad_one, unit_mine, pick(rescale_one, core), gains[0])
    gain_one = jnp.sum(grad_one * unit_mine, axis=0)
    grad_rows = (pick(grad_hidden, core) + back_one).astype(jnp.bfloat16)

    gate_up_state = after(gate_up_state, (output, grad_rows))
    parts = split_cols(end_rows(gate_up_state))
    gate_up_got = send_cols(parts)
    output = send_rows(after(output, parts))
    down_state = after(down_state, parts)
    down_rows = low(end_cols(wide(down_state[0]), down_state[1:]))
    down_state = start_rows(down_rows, 1)
    attn_sent, attn_state = middle_rows(after(attn_state, down_rows))
    down_sent, down_state = middle_rows(after(down_state, attn_sent))
    attn_state = after(attn_state, down_sent)
    attn_parts = split_cols(end_rows(attn_state))
    attn_got = send_cols(attn_parts)
    gain_sums = jnp.stack([gain_one, gain_two], axis=0)
    gain_sums, grad_rows = after((gain_sums, grad_rows), attn_parts)
    grad_tokens = from_sequence(send_rows(grad_rows), core, col, length).astype(jnp.float32)
    gate_up_got, down_state, output = after((gate_up_got, down_state, output), attn_parts)
    output = from_sequence(output, core, col, length)
    mine_gate_up = end_cols(parts[0], gate_up_got)
    mine_down = jnp.concatenate(end_rows(down_state), axis=-1)
    mine_attn = end_cols(attn_parts[0], attn_got)

    gain_sums = gain_sums + swap(gain_sums)
    gain_sums = gain_sums + hop(gain_sums, "row", 1)
    gain_sums = gain_sums + hop(gain_sums, "row", 2)
    gain_mine = gain_sums[:, :features]
    for flip in range(1, 4):
        piece = gain_sums[:, flip * features : (flip + 1) * features]
        gain_mine = gain_mine + hop(piece, "col", flip)

    whole_attn = joined(mine_attn, core)
    return (
        output,
        grad_tokens,
        gain_mine[0],
        gain_mine[1],
        whole_attn[:3].transpose(2, 0, 1),
        whole_attn[3],
        joined(mine_gate_up, core).transpose(2, 0, 1),
        joined(mine_down, core)[0],
    )


def layer(tokens, segment_ids, *rest):
    sizes = (lax.axis_size("dp"), lax.axis_size("row"), lax.axis_size("col"))
    if sizes == (2, 4, 4) and tokens.shape[0] == 2 * segment_ids.shape[1]:
        return chip_local(tokens, segment_ids, *rest)
    return local(tokens, segment_ids, *rest)


def solution(mesh):
    in_specs = (
        P(("dp", "row"), "col"),
        P(("dp", "col"), None),
        P("col"),
        P("col"),
        P("col", None, "row"),
        P("row", "col"),
        P("col", None, "row"),
        P("row", "col"),
        P(("dp", "row"), "col"),
    )
    out_specs = (
        P(("dp", "row"), "col"),
        P(("dp", "row"), "col"),
        P("col"),
        P("col"),
        P("col", None, "row"),
        P("row", "col"),
        P("col", None, "row"),
        P("row", "col"),
    )
    return jax.shard_map(layer, mesh=mesh, in_specs=in_specs, out_specs=out_specs, check_vma=False)
```

```python
import jax
import jax.numpy as jnp
from jax import lax
from jax.experimental import pallas as pl
from jax.experimental.pallas import tpu as pltpu
from jax.sharding import PartitionSpec as P

D = 1024
HEAD_DIM = 64


EPS = 1e-06
MASKED = -1e30


def row_norm(values, gain_vec):
    squares = lax.psum(jnp.sum(values * values, axis=1), "col")
    rescale = lax.rsqrt(squares / D + EPS)
    unit_rows = values * rescale[:, None]
    return (unit_rows, rescale, (unit_rows * gain_vec[None, :]).astype(jnp.bfloat16))


def norm_backward(grad_normed, unit_rows, rescale, gain_vec):
    weighted = grad_normed * gain_vec[None, :]
    inner_sum = lax.psum(jnp.sum(weighted * unit_rows, axis=1), "col")
    grad_in = rescale[:, None] * (weighted - unit_rows * (inner_sum / D)[:, None])
    grad_gain = jnp.sum(grad_normed * unit_rows, axis=0)
    return (grad_in, grad_gain)


def project_up(normed, weight_block):
    gathered = lax.all_gather(normed, "row", axis=0, tiled=True)

    def term(begin_at):
        return jnp.dot(gathered, weight_block, preferred_element_type=jnp.float32)

    result = lax.psum_scatter(
        term(jnp.int32(0)),
        "col",
        scatter_dimension=0,
        tiled=True,
    )
    return (gathered, result.astype(jnp.bfloat16))


def project_down(values, weight_block):
    gathered = lax.all_gather(values, "col", axis=0, tiled=True)

    def term(begin_at):
        return jnp.dot(gathered, weight_block, preferred_element_type=jnp.float32)

    result = lax.psum_scatter(
        term(jnp.int32(0)),
        "row",
        scatter_dimension=0,
        tiled=True,
    )
    return (gathered, result)


def back_down(grad_rows, weight_block):
    gathered = lax.all_gather(grad_rows, "row", axis=0, tiled=True)

    def term(begin_at):
        return lax.dot_general(
            gathered, weight_block, (((1,), (1,)), ((), ())), preferred_element_type=jnp.float32
        )

    result = lax.psum_scatter(
        term(jnp.int32(0)),
        "col",
        scatter_dimension=0,
        tiled=True,
    )
    return (gathered, result.astype(jnp.bfloat16))


def back_up(grad_cols, weight_block):
    gathered = lax.all_gather(grad_cols, "col", axis=0, tiled=True)

    def term(begin_at):
        return lax.dot_general(
            gathered, weight_block, (((1,), (1,)), ((), ())), preferred_element_type=jnp.float32
        )

    result = lax.psum_scatter(
        term(jnp.int32(0)),
        "row",
        scatter_dimension=0,
        tiled=True,
    )
    return (gathered, result)


def weight_grad(left_rows, right_rows):
    return lax.dot_general(
        left_rows, right_rows, (((0,), (0,)), ((), ())), preferred_element_type=jnp.float32
    )


def block_scores(queries, keys_all, query_segment, key_segment, query_place):
    raw = jnp.einsum(
        "qhd,khd->hqk", queries, keys_all, preferred_element_type=jnp.float32
    ) * HEAD_DIM ** (-0.5)
    key_place = lax.broadcasted_iota(jnp.int32, (1, keys_all.shape[0]), 1)
    allowed = (query_segment[:, None] == key_segment[None, :]) & (key_place <= query_place[:, None])
    return jnp.where(allowed[None], raw, MASKED)


def split_blocks(queries, segment):
    length = queries.shape[0]
    block_rows = min(512, length)
    blocks = length // block_rows
    place = jnp.arange(length, dtype=jnp.int32).reshape(blocks, block_rows)
    return (
        queries.reshape(blocks, block_rows, queries.shape[1], queries.shape[2]),
        segment.reshape(blocks, block_rows),
        place,
    )


def attend_forward(queries, keys_all, values_all, segment):
    query_blocks, segment_blocks, place_blocks = split_blocks(queries, segment)

    def one_block(item):
        query_rows, query_segment, query_place = item
        scores = block_scores(query_rows, keys_all, query_segment, segment, query_place)
        row_max = jnp.max(scores, axis=-1, keepdims=True)
        expo = jnp.exp(scores - row_max)
        row_total = jnp.sum(expo, axis=-1, keepdims=True)
        prob_rows = (expo / row_total).astype(jnp.bfloat16)
        mixed = jnp.einsum(
            "hqk,khd->qhd", prob_rows, values_all, preferred_element_type=jnp.float32
        )
        return (mixed, row_max[..., 0] + jnp.log(row_total[..., 0]))

    mixed, log_total = lax.map(one_block, (query_blocks, segment_blocks, place_blocks))
    return (mixed.reshape(queries.shape[0], -1).astype(jnp.bfloat16), log_total)


def attend_backward(queries, keys_all, values_all, segment, log_total, grad_mix):
    query_blocks, segment_blocks, place_blocks = split_blocks(queries, segment)
    grad_blocks = grad_mix.reshape(query_blocks.shape)
    factor = HEAD_DIM ** (-0.5)

    def one_block(carry, item):
        key_acc, value_acc = carry
        query_rows, query_segment, query_place, log_rows, grad_rows = item
        scores = block_scores(query_rows, keys_all, query_segment, segment, query_place)
        prob_rows = jnp.exp(scores - log_rows[..., None])
        value_acc = value_acc + jnp.einsum(
            "hqk,qhd->khd",
            prob_rows.astype(jnp.bfloat16),
            grad_rows,
            preferred_element_type=jnp.float32,
        )
        grad_prob = jnp.einsum(
            "qhd,khd->hqk", grad_rows, values_all, preferred_element_type=jnp.float32
        )
        grad_scores = (
            prob_rows * (grad_prob - jnp.sum(prob_rows * grad_prob, axis=-1, keepdims=True))
        ).astype(jnp.bfloat16)
        grad_query = (
            jnp.einsum("hqk,khd->qhd", grad_scores, keys_all, preferred_element_type=jnp.float32)
            * factor
        )
        key_acc = (
            key_acc
            + jnp.einsum(
                "hqk,qhd->khd", grad_scores, query_rows, preferred_element_type=jnp.float32
            )
            * factor
        )
        return ((key_acc, value_acc), grad_query)

    zeros_like_keys = jnp.zeros(keys_all.shape, jnp.float32)
    (grad_keys, grad_values), grad_queries = lax.scan(
        one_block,
        (zeros_like_keys, zeros_like_keys),
        (query_blocks, segment_blocks, place_blocks, log_total, grad_blocks),
    )
    grad_queries = grad_queries.reshape(queries.shape)
    return jnp.stack([grad_queries, grad_keys, grad_values], axis=1).astype(jnp.bfloat16)


def local(tokens, segment_ids, gain_attn, gain_ffn, w_qkv, w_out, w_gate_up, w_down, grad_out):
    values = tokens.astype(jnp.float32)
    head_cols = w_qkv.shape[2]
    heads_here = head_cols // HEAD_DIM
    hidden_here = w_gate_up.shape[2]
    qkv_block = w_qkv.reshape(w_qkv.shape[0], 3 * head_cols)
    gate_up_block = w_gate_up.reshape(w_gate_up.shape[0], 2 * hidden_here)
    seq_count, seq_length = segment_ids.shape
    unit_one, rescale_one, normed_one = row_norm(values, gain_attn)
    gathered_one, packed = project_up(normed_one, qkv_block)
    packed = packed.reshape(-1, 3, heads_here, HEAD_DIM)
    mix_parts, log_parts = ([], [])
    for index in range(seq_count):
        rows_here = packed[index * seq_length : (index + 1) * seq_length]
        mixed, log_total = attend_forward(
            rows_here[:, 0], rows_here[:, 1], rows_here[:, 2], segment_ids[index]
        )
        mix_parts.append(mixed)
        log_parts.append(log_total)
    attn_mix = jnp.concatenate(mix_parts, axis=0)
    gathered_mix, attn_branch = project_down(attn_mix, w_out)
    hidden = values + attn_branch
    unit_two, rescale_two, normed_two = row_norm(hidden, gain_ffn)
    gathered_two, gate_up = project_up(normed_two, gate_up_block)
    gate_vals = gate_up[:, :hidden_here].astype(jnp.float32)
    up_vals = gate_up[:, hidden_here:].astype(jnp.float32)
    sigmoid_gate = jax.nn.sigmoid(gate_vals)
    silu_gate = gate_vals * sigmoid_gate
    active = (silu_gate * up_vals).astype(jnp.bfloat16)
    gathered_act, ffn_branch = project_down(active, w_down)
    output = (hidden + ffn_branch).astype(jnp.bfloat16)
    grad_rows_out, grad_active = back_down(grad_out, w_down)
    grad_down = weight_grad(gathered_act, grad_rows_out)
    grad_act_f = grad_active.astype(jnp.float32)
    grad_gate = grad_act_f * up_vals * sigmoid_gate * (1.0 + gate_vals * (1.0 - sigmoid_gate))
    grad_up = grad_act_f * silu_gate
    grad_gate_up_rows = jnp.concatenate([grad_gate, grad_up], axis=1).astype(jnp.bfloat16)
    grad_cols_two, grad_normed_two = back_up(grad_gate_up_rows, gate_up_block)
    grad_gate_up = weight_grad(gathered_two, grad_cols_two).reshape(w_gate_up.shape)
    grad_hidden_norm, grad_gain_two = norm_backward(
        grad_normed_two, unit_two, rescale_two, gain_ffn
    )
    grad_hidden = grad_out.astype(jnp.float32) + grad_hidden_norm
    grad_rows_hidden, grad_mix = back_down(grad_hidden.astype(jnp.bfloat16), w_out)
    grad_out_weight = weight_grad(gathered_mix, grad_rows_hidden)
    grad_mix = grad_mix.reshape(-1, heads_here, HEAD_DIM)
    grad_parts = []
    for index in range(seq_count):
        rows_here = packed[index * seq_length : (index + 1) * seq_length]
        grad_parts.append(
            attend_backward(
                rows_here[:, 0],
                rows_here[:, 1],
                rows_here[:, 2],
                segment_ids[index],
                log_parts[index],
                grad_mix[index * seq_length : (index + 1) * seq_length],
            )
        )
    grad_packed = jnp.concatenate(grad_parts, axis=0).reshape(-1, 3 * head_cols)
    grad_cols_one, grad_normed_one = back_up(grad_packed, qkv_block)
    grad_qkv = weight_grad(gathered_one, grad_cols_one).reshape(w_qkv.shape)
    grad_input_norm, grad_gain_one = norm_backward(
        grad_normed_one, unit_one, rescale_one, gain_attn
    )
    grad_tokens = grad_hidden + grad_input_norm
    summed = lax.psum((grad_qkv, grad_out_weight, grad_gate_up, grad_down), "dp")
    gains = lax.psum((grad_gain_one, grad_gain_two), ("dp", "row"))
    return (output, grad_tokens, gains[0], gains[1], summed[0], summed[1], summed[2], summed[3])


def swap(values):
    return lax.ppermute(values, "dp", [(0, 1), (1, 0)])


def hop(values, axis, flip):
    return lax.ppermute(values, axis, [(at, at ^ flip) for at in range(lax.axis_size(axis))])


def after(values, first):
    return lax.optimization_barrier((values, first))[0]


def by_core(core, mine, other, axis=0):
    first = jnp.where(core == 0, mine, other)
    second = jnp.where(core == 0, other, mine)
    return jnp.concatenate([first, second], axis=axis)


def pick(values, core, axis=0):
    half = values.shape[axis] // 2
    return lax.dynamic_slice_in_dim(values, core * half, half, axis)


def send_chunks(values, core, col, seq_length):
    seqs = values.shape[0] // seq_length
    parts = values.reshape(seqs, seq_length, -1)
    mine = pick(parts, core, 1)
    other = swap(pick(parts, 1 - core, 1))
    chunks = by_core(core, mine, other)
    got = []
    for flip in range(4):
        chunk = lax.dynamic_index_in_dim(chunks, col ^ flip, 0, keepdims=False)
        got.append(hop(chunk, "col", flip) if flip else chunk)
    return got


def to_sequence(got, core):
    rows = jnp.concatenate(got, axis=1)
    return by_core(core, rows, swap(rows))


def send_rows(rows):
    width = rows.shape[1] // 4
    parts = [rows[:, at * width : (at + 1) * width] for at in range(4)]
    return [parts[0]] + [hop(parts[flip], "col", flip) for flip in range(1, 4)]


def from_sequence(got, core, col, seq_length):
    got = jnp.stack(got, axis=0)
    seqs = 2

    def of_core(which):
        picked = [
            lax.dynamic_index_in_dim(got, (which * seqs + at) ^ col, 0, False) for at in range(seqs)
        ]
        return jnp.stack(picked)

    mine, other = (of_core(core), of_core(1 - core))
    return by_core(core, mine, swap(other), 1).reshape(seqs * seq_length, -1)


def times(left, right):
    return jnp.dot(left, right, preferred_element_type=jnp.float32)


def times_t(left, right):
    return lax.dot_general(
        left, right, (((1,), (1,)), ((), ())), preferred_element_type=jnp.float32
    )


def norm_rows(values):
    rescale = lax.rsqrt(jnp.mean(values * values, axis=1) + EPS)[:, None]
    return (values * rescale, rescale)


def norm_rows_back(grad_normed, unit_rows, rescale, gain_vec):
    weighted = grad_normed * gain_vec[None, :]
    inner = jnp.sum(weighted * unit_rows, axis=1, keepdims=True) / D
    return rescale * (weighted - unit_rows * inner)


def join_blocks(*refs):
    blocks, wholes = (refs[:16], refs[16:])
    _, rows, width = blocks[0].shape
    for at, block in enumerate(blocks):
        line, place = divmod(at, 4)
        kind = 0
        for whole in wholes:
            part = block[kind : kind + whole.shape[0]]
            kind += whole.shape[0]
            whole[:, line * rows : (line + 1) * rows, place * width : (place + 1) * width] = part


def spread_weights(block, first_cols=None, first_rows=None):
    grid = [[None] * 4 for _ in range(4)]
    block_cols = block if first_cols is None else after(block, first_cols)
    block_rows = block if first_rows is None else after(block, first_rows)
    near = hop(block_cols, "col", 1)
    far = hop(block_cols, "col", 3)
    relayed = hop(near, "col", 3)
    grid[0] = [block_rows, near, relayed, far]
    for at in (0, 1, 3, 2):
        grid[1][at] = hop(grid[0][at], "row", 1)
        grid[2][at] = hop(grid[0][at], "row", 2)
    for at in range(4):
        if at < 2:
            grid[3][at] = hop(grid[1][at], "row", 2)
        else:
            grid[3][at] = hop(grid[2][at], "row", 1)
    return grid


def join_weights(grid, splits):
    _, rows, width = grid[0][0].shape
    shapes = [jax.ShapeDtypeStruct((at, 4 * rows, 4 * width), jnp.bfloat16) for at in splits]
    wholes = pl.pallas_call(join_blocks, out_shape=shapes)(*[b for line in grid for b in line])
    return [whole.reshape(-1, 4 * width) for whole in wholes]


def wide(values):
    return values.astype(jnp.float32)


def low(values):
    return values.astype(jnp.bfloat16)


def start_rows(grad, kinds):
    grid = low(grad).reshape(kinds, 2, 2, -1, grad.shape[1])
    half = grad.shape[1] // 2
    left, right = (grid[..., :half], grid[..., half:])
    got = hop(left[:, 1], "row", 2)
    got_r = hop(right[:, :, 1], "row", 1)
    return (left, right, got, got_r)


def middle_rows(state):
    left, right, got, got_r = state
    sent = low(wide(left[:, 0, 1]) + wide(got[:, 1]))
    sent_r = low(wide(right[:, 1, 0]) + wide(got_r[:, 1]))
    return ((sent, sent_r), state + (hop(sent, "row", 1), hop(sent_r, "row", 2)))


def end_rows(state):
    left, right, got, got_r, last, last_r = state
    sums = wide(left[:, 0, 0]) + wide(got[:, 0]) + wide(last)
    sums_r = wide(right[:, 0, 0]) + wide(got_r[:, 0]) + wide(last_r)
    return (sums, sums_r)


def split_cols(state):
    sums, sums_r = state
    width = sums.shape[-1] // 2
    parts = [low(sums[..., width:]), low(sums_r[..., :width]), low(sums_r[..., width:])]
    return [sums[..., :width]] + parts


def send_cols(parts):
    return [hop(parts[flip], "col", flip) for flip in (1, 2, 3)]


def end_cols(total, got):
    return total + wide(got[0]) + wide(got[1]) + wide(got[2])


def start_cols(grad):
    width = grad.shape[1] // 4
    parts = [low(grad[:, at * width : (at + 1) * width]) for at in range(4)]
    return parts[:1] + send_cols(parts)


def join_halves(core_ref, mine, other, whole):
    rows = mine.shape[1]
    for at in range(2):
        part = slice(at * rows, (at + 1) * rows)

        @pl.when(core_ref[0] == at)
        def _():
            whole[:, part, :] = mine[...]

        @pl.when(core_ref[0] != at)
        def _():
            whole[:, part, :] = other[...].astype(jnp.float32)


def joined(mine, core):
    kinds, rows, width = mine.shape
    mine_low = low(mine)
    vmem = pl.BlockSpec(memory_space=pltpu.VMEM)
    return pl.pallas_call(
        join_halves,
        out_shape=jax.ShapeDtypeStruct((kinds, 2 * rows, width), jnp.float32),
        in_specs=[pl.BlockSpec(memory_space=pltpu.SMEM), vmem, vmem],
        out_specs=vmem,
    )(core[None], mine, swap(mine_low))


def chip_local(tokens, segment_ids, gain_attn, gain_ffn, w_qkv, w_out, w_gate_up, w_down, grad_out):
    core = lax.axis_index("dp")
    col = lax.axis_index("col")
    length = segment_ids.shape[1]
    features = w_qkv.shape[0]
    head_cols = w_qkv.shape[2] // 2
    heads = 4 * head_cols // HEAD_DIM
    factor = HEAD_DIM ** (-0.5)

    token_chunks = send_chunks(tokens, core, col, length)
    attn_block = jnp.concatenate(
        [pick(w_qkv, core, 2).transpose(1, 2, 0), pick(w_out, core)[None]], axis=0
    )
    attn_grid = spread_weights(attn_block)
    token_chunks = after(token_chunks, attn_grid[0])
    values = to_sequence(token_chunks, core).astype(jnp.float32)
    gains = jnp.stack([gain_attn, gain_ffn], axis=0)
    gains = jnp.concatenate([gains] + [hop(gains, "col", flip) for flip in range(1, 4)], axis=1)
    corner = [(4 * at + to, 4 * to + at) for at in range(4) for to in range(4)]
    segment_rows = lax.ppermute(segment_ids, ("row", "col"), corner)
    segment_rows = by_core(core, segment_rows, swap(segment_rows))
    segment = lax.dynamic_index_in_dim(segment_rows, col, 0, keepdims=False)
    ffn_block = jnp.concatenate(
        [pick(w_gate_up, core, 2).transpose(1, 2, 0), pick(w_down, core)[None]], axis=0
    )
    ffn_grid = spread_weights(ffn_block, attn_grid[0], attn_grid[1] + attn_grid[2])
    attn_wholes = join_weights(attn_grid, (3, 1))
    big_qkv, big_out = after(attn_wholes, ffn_grid[0])
    grad_late = after(grad_out, ffn_grid[1] + ffn_grid[2])
    grad_chunks = send_chunks(grad_late, core, col, length)
    big_gate_up, big_down = join_weights(ffn_grid, (2, 1))
    cotangent = to_sequence(grad_chunks, core)

    unit_one, rescale_one = norm_rows(values)
    normed_one = (unit_one * gains[0][None, :]).astype(jnp.bfloat16)
    packed = times_t(normed_one, big_qkv).astype(jnp.bfloat16)
    packed = packed.reshape(length, 3, heads, HEAD_DIM)
    queries, keys, vals = (packed[:, 0], packed[:, 1], packed[:, 2])
    scores = jnp.einsum("qhd,khd->hqk", queries, keys, preferred_element_type=jnp.float32) * factor
    spot = jnp.arange(length, dtype=jnp.int32)
    live = (segment[:, None] == segment[None, :]) & (spot[None, :] <= spot[:, None])
    scores = jnp.where(live[None], scores, MASKED)
    expo = jnp.exp(scores - jnp.max(scores, axis=-1, keepdims=True))
    prob = expo / jnp.sum(expo, axis=-1, keepdims=True)
    prob_low = prob.astype(jnp.bfloat16)
    mixed = jnp.einsum("hqk,khd->qhd", prob_low, vals, preferred_element_type=jnp.float32)
    mixed = mixed.reshape(length, -1).astype(jnp.bfloat16)
    branch = times(mixed, big_out)
    hidden_rows = values + (branch + swap(branch))
    unit_two, rescale_two = norm_rows(hidden_rows)
    normed_two = (unit_two * gains[1][None, :]).astype(jnp.bfloat16)
    gate_up = times_t(normed_two, big_gate_up).astype(jnp.bfloat16)
    half = gate_up.shape[1] // 2
    gate_vals = gate_up[:, :half].astype(jnp.float32)
    up_vals = gate_up[:, half:].astype(jnp.float32)
    sigmoid_gate = jax.nn.sigmoid(gate_vals)
    silu_gate = gate_vals * sigmoid_gate
    active = (silu_gate * up_vals).astype(jnp.bfloat16)

    down_state = start_cols(weight_grad(active, cotangent))
    grad_act = wide(low(times_t(cotangent, big_down)))
    grad_gate = grad_act * up_vals * sigmoid_gate * (1.0 + gate_vals * (1.0 - sigmoid_gate))
    grad_up = grad_act * silu_gate
    grad_gu = jnp.concatenate([grad_gate, grad_up], axis=1).astype(jnp.bfloat16)
    grad_two = times(grad_gu, big_gate_up)
    grad_two = grad_two + swap(grad_two)
    gate_up_state = start_rows(weight_grad(grad_gu, normed_two), 2)
    back_two = norm_rows_back(grad_two, unit_two, rescale_two, gains[1])
    gain_two = jnp.sum(pick(grad_two * unit_two, core), axis=0)
    grad_hidden = cotangent.astype(jnp.float32) + back_two
    grad_branch = grad_hidden.astype(jnp.bfloat16)
    grad_w_out = low(weight_grad(mixed, grad_branch))
    grad_mix = times_t(grad_branch, big_out).astype(jnp.bfloat16).reshape(length, heads, HEAD_DIM)
    grad_vals = jnp.einsum("hqk,qhd->khd", prob_low, grad_mix, preferred_element_type=jnp.float32)
    grad_prob = jnp.einsum("qhd,khd->hqk", grad_mix, vals, preferred_element_type=jnp.float32)
    inner = jnp.sum(prob * grad_prob, axis=-1, keepdims=True)
    grad_scores = (prob * (grad_prob - inner)).astype(jnp.bfloat16)
    grad_queries = factor * jnp.einsum(
        "hqk,khd->qhd", grad_scores, keys, preferred_element_type=jnp.float32
    )
    grad_keys = factor * jnp.einsum(
        "hqk,qhd->khd", grad_scores, queries, preferred_element_type=jnp.float32
    )
    grad_packed = jnp.stack([grad_queries, grad_keys, grad_vals], axis=1)
    grad_packed = grad_packed.astype(jnp.bfloat16).reshape(length, -1)
    grad_attn = jnp.concatenate([low(weight_grad(grad_packed, normed_one)), grad_w_out], axis=0)

    gate_up_sent, gate_up_state = middle_rows(after(gate_up_state, grad_attn))
    grad_attn = after(grad_attn, gate_up_sent)
    attn_state = start_rows(grad_attn, 4)
    active = after(active, grad_attn)
    grad_packed = after(grad_packed, grad_attn)
    grad_one = times(grad_packed, big_qkv)
    grad_one = pick(grad_one, core) + swap(pick(grad_one, 1 - core))
    ffn = times(active, big_down)
    ffn_mine = pick(ffn, core) + swap(pick(ffn, 1 - core))
    output = (pick(hidden_rows, core) + ffn_mine).astype(jnp.bfloat16)
    unit_mine = pick(unit_one, core)
    back_one = norm_rows_back(grad_one, unit_mine, pick(rescale_one, core), gains[0])
    gain_one = jnp.sum(grad_one * unit_mine, axis=0)
    grad_rows = (pick(grad_hidden, core) + back_one).astype(jnp.bfloat16)

    gate_up_state = after(gate_up_state, (output, grad_rows))
    parts = split_cols(end_rows(gate_up_state))
    gate_up_got = send_cols(parts)
    output = send_rows(after(output, parts))
    down_state = after(down_state, parts)
    down_rows = low(end_cols(wide(down_state[0]), down_state[1:]))
    down_state = start_rows(down_rows, 1)
    attn_sent, attn_state = middle_rows(after(attn_state, down_rows))
    down_sent, down_state = middle_rows(after(down_state, attn_sent))
    attn_state = after(attn_state, down_sent)
    attn_parts = split_cols(end_rows(attn_state))
    attn_got = send_cols(attn_parts)
    gain_sums = jnp.stack([gain_one, gain_two], axis=0)
    gain_sums, grad_rows = after((gain_sums, grad_rows), attn_parts)
    grad_tokens = from_sequence(send_rows(grad_rows), core, col, length).astype(jnp.float32)
    gate_up_got, down_state, output = after((gate_up_got, down_state, output), attn_parts)
    output = from_sequence(output, core, col, length)
    mine_gate_up = end_cols(parts[0], gate_up_got)
    mine_down = jnp.concatenate(end_rows(down_state), axis=-1)
    mine_attn = end_cols(attn_parts[0], attn_got)

    gain_sums = gain_sums + swap(gain_sums)
    gain_sums = gain_sums + hop(gain_sums, "row", 1)
    gain_sums = gain_sums + hop(gain_sums, "row", 2)
    whole_gate_up = joined(mine_gate_up, core)
    whole_down = joined(mine_down, core)
    gain_sums = after(gain_sums, (whole_gate_up, whole_down))
    gain_mine = gain_sums[:, :features]
    for flip in range(1, 4):
        piece = gain_sums[:, flip * features : (flip + 1) * features]
        gain_mine = gain_mine + hop(piece, "col", flip)

    whole_attn = joined(mine_attn, core)
    return (
        output,
        grad_tokens,
        gain_mine[0],
        gain_mine[1],
        whole_attn[:3].transpose(2, 0, 1),
        whole_attn[3],
        whole_gate_up.transpose(2, 0, 1),
        whole_down[0],
    )


def layer(tokens, segment_ids, *rest):
    sizes = (lax.axis_size("dp"), lax.axis_size("row"), lax.axis_size("col"))
    if sizes == (2, 4, 4) and tokens.shape[0] == 2 * segment_ids.shape[1]:
        return chip_local(tokens, segment_ids, *rest)
    return local(tokens, segment_ids, *rest)


def solution(mesh):
    in_specs = (
        P(("dp", "row"), "col"),
        P(("dp", "col"), None),
        P("col"),
        P("col"),
        P("col", None, "row"),
        P("row", "col"),
        P("col", None, "row"),
        P("row", "col"),
        P(("dp", "row"), "col"),
    )
    out_specs = (
        P(("dp", "row"), "col"),
        P(("dp", "row"), "col"),
        P("col"),
        P("col"),
        P("col", None, "row"),
        P("row", "col"),
        P("col", None, "row"),
        P("row", "col"),
    )
    return jax.shard_map(layer, mesh=mesh, in_specs=in_specs, out_specs=out_specs, check_vma=False)
```
